128 devices in a mesh: tile: 64 (over z, y, x), slide: 2 (over core).
Axes of the slice: x: 4, y: 4, z: 4, core: 2. Of those that a mesh axis runs over, the one named last changes fastest.
Arguments:
- features: bfloat16 [256, 32, 32, 256], P(('slide', 'tile')), parts along dimension 0, may hold values from -8 to 8
- neighbours: int32 [256, 8], P(('slide', 'tile')), parts along dimension 0, may hold values from 0 to 128, as said below
- conv_weight: bfloat16 [3, 3, 256, 256], replicated, may hold values from -0.125 to 0.125
- patch_weight: bfloat16 [4096, 768], replicated, may hold values from -1 to 1
- query_weight: bfloat16 [768, 768], replicated, may hold values from -2 to 2
- key_weight: bfloat16 [768, 768], replicated, may hold values from -2 to 2
- value_weight: bfloat16 [768, 768], replicated, may hold values from -0.21875 to 0.21875
- output_weight: bfloat16 [768, 768], replicated, may hold values from -0.21875 to 0.21875
- cotangent: bfloat16 [16384, 768], P(('slide', 'tile')), parts along dimension 0, may hold values from -6 to 6
Outputs:
- mixed: bfloat16 [16384, 768], P(('slide', 'tile')), parts along dimension 0
- output_grad: float32 [1536, 768], P('slide'), parts along dimension 0
The draws below stay inside these ranges and needn't reach their ends.
There are 2 independent parts, one for each index of `slide`. The reference program is written for one: setup_inputs(seed, part) draws one part's arguments, and reference() takes and returns one part's arrays. A program takes and returns all parts, laid end to end along the dimension named above; an argument that names none is the same for every part. Nothing has to cross between parts.
Inputs may be any that keep to these rules, and one draw needn't show every extreme that they name: Tiles are tissue cells of a grid 16 cells wide; the tile numbers are given to the tissue cells in a drawn order, so neighbours may have any numbers; each entry is the index of the tissue tile at that grid offset, or 128.
All inputs are finite; a program needn't handle non-finite values.
Results may differ from the reference program's by a relative error of at most 0.02.
Values may be sent and summed in bfloat16 or wider, within the bound.
No kernel may reach another device: no remote copies, remote signals or barrier semaphores. Data moves between devices by JAX's collectives and lax.ppermute only.
A program may use at most 192 MiB of HBM per device.

```python
import math
import jax
import jax.numpy as jnp
from jax import lax

CELLS = 32
CH = 256
PATCH = 4
HEADS = 12
HD = 64
DM = 768
TOK_DEV = 128
TILES = 128
TOKENS = 8192
N_TILE = 64


def draw_neighbours(key, part):
    cells = 2 * TILES
    order = jax.random.permutation(key, cells)
    chosen = jnp.sort(order[:TILES])
    numbering = jax.random.permutation(jax.random.fold_in(key, 5), TILES)
    cell_of = chosen[numbering]
    rows = cell_of // 16
    cols = cell_of % 16
    height = cells // 16
    grid_map = jnp.full((cells,), TILES, jnp.int32).at[cell_of].set(jnp.arange(TILES, dtype=jnp.int32))
    offsets = [(-1, -1), (-1, 0), (-1, 1), (0, -1), (0, 1), (1, -1), (1, 0), (1, 1)]
    result = []
    for row_off, col_off in offsets:
        near_row = rows + row_off
        near_col = cols + col_off
        inside = (near_row >= 0) & (near_row < height) & (near_col >= 0) & (near_col < 16)
        place = jnp.clip(near_row * 16 + near_col, 0, cells - 1)
        result.append(jnp.where(inside, grid_map[place], TILES))
    return jnp.stack(result, axis=1).astype(jnp.int32)


def bounded_normal(key, shape):
    return jnp.clip(jax.random.normal(key, shape, jnp.float32), -5.0, 5.0)


def shared_pattern(key):
    base = jax.random.fold_in(key, 9001)
    token_signs = (2 * jax.random.randint(jax.random.fold_in(base, 1), (DM,), 0, 2) - 1).astype(jnp.float32)
    chosen_head = jax.random.randint(jax.random.fold_in(base, 2), (), 0, HEADS)
    head_signs = (2 * jax.random.randint(jax.random.fold_in(base, 3), (DM,), 0, 2) - 1).astype(jnp.float32)
    inside = jnp.arange(DM) // HD == chosen_head
    head_dir = jnp.where(inside, head_signs, 0.0) / math.sqrt(HD)
    return (token_signs, head_dir)


def drawn_projection(key, salt):
    token_signs, head_dir = shared_pattern(key)
    drawn = bounded_normal(jax.random.fold_in(key, salt), (DM, DM)) / math.sqrt(DM)
    strength = math.sqrt(300.0 * math.sqrt(HD)) / (0.714 * math.sqrt(DM))
    planted = strength * (token_signs / math.sqrt(DM))[:, None] * head_dir[None, :]
    return (drawn + planted).astype(jnp.bfloat16)


def draw_features(key, part):
    shuffled = jax.random.permutation(jax.random.fold_in(key, 21), TILES)
    tile_scale = 0.5 * 4.0 ** (shuffled.astype(jnp.float32) / (TILES - 1))
    shape = (TILES, CELLS, CELLS, CH)
    base = jnp.clip(jax.random.normal(jax.random.fold_in(key, 22), shape, jnp.float32), -4.0, 4.0)
    return (base * tile_scale[:, None, None, None]).astype(jnp.bfloat16)


def draw_patch_weight(key, part):
    token_signs, head_dir = shared_pattern(key)
    fan = PATCH * PATCH * CH
    drawn = bounded_normal(jax.random.fold_in(key, 31), (fan, DM)) / math.sqrt(fan)
    return (drawn + token_signs[None, :] / fan).astype(jnp.bfloat16)


def draw_query_weight(key, part):
    return drawn_projection(key, 41)


def draw_key_weight(key, part):
    return drawn_projection(key, 51)


def levels(own_key, extent, shards, least, largest):
    loudness, own = 1.0, jax.random.fold_in(own_key, 6)
    for position, blocks in shards:
        steps = jnp.exp(jax.random.uniform(jax.random.fold_in(own, position), (blocks,), jnp.float32, least / len(shards), largest / len(shards)))
        loudness = loudness * jnp.repeat(steps, extent[position] // blocks).reshape([-1 if axis == position else 1 for axis in range(len(extent))])
    return loudness


def gaussian(own_key, dims, spread, bound, cuts=(), held_as=jnp.bfloat16):
    entries = jax.random.normal(own_key, dims, jnp.float32) * spread
    if len(cuts) > 0:
        entries = levels(own_key, dims, cuts, -0.22, 0.18) * entries
    return jnp.clip(entries, min=-bound, max=bound).astype(held_as)


def setup_inputs(seed: int = 0, part: int = 0) -> dict:
    splits = jax.random.split(jax.random.key(seed), 10)
    part_keys = jax.random.split(jax.random.fold_in(splits[9], part), 10)
    features = draw_features(jax.random.fold_in(jax.random.fold_in(splits[9], part), 71), part)
    neighbours = draw_neighbours(jax.random.fold_in(jax.random.fold_in(splits[9], part), 71), part)
    conv_weight = gaussian(splits[2], (3, 3, CH, CH), (9 * CH) ** -0.5, 0.125)
    patch_weight = draw_patch_weight(jax.random.fold_in(splits[9], 71), part)
    query_weight = draw_query_weight(jax.random.fold_in(splits[9], 71), part)
    key_weight = draw_key_weight(jax.random.fold_in(splits[9], 71), part)
    value_weight = gaussian(splits[6], (DM, DM), DM ** -0.5, 0.21875)
    output_weight = gaussian(splits[7], (DM, DM), DM ** -0.5, 0.21875)
    cotangent = gaussian(part_keys[8], (TOKENS, DM), 1.0, 6.0, ((0, 64),))
    return {"features": features, "neighbours": neighbours, "conv_weight": conv_weight, "patch_weight": patch_weight, "query_weight": query_weight, "key_weight": key_weight, "value_weight": value_weight, "output_weight": output_weight, "cotangent": cotangent}


def tile_faces(maps):
    return jnp.stack([maps[:, 0], maps[:, -1], maps[:, :, 0], maps[:, :, -1]], axis=1)


def pad_tiles(maps, all_faces, links):
    upper = all_faces[links[:, 1], 1]
    lower = all_faces[links[:, 6], 0]
    left_col = all_faces[links[:, 3], 3]
    right_col = all_faces[links[:, 4], 2]
    corner_ul = all_faces[links[:, 0], 1, -1]
    corner_ur = all_faces[links[:, 2], 1, 0]
    corner_dl = all_faces[links[:, 5], 0, -1]
    corner_dr = all_faces[links[:, 7], 0, 0]
    top_row = jnp.concatenate([corner_ul[:, None], upper, corner_ur[:, None]], axis=1)
    bottom_row = jnp.concatenate([corner_dl[:, None], lower, corner_dr[:, None]], axis=1)
    middle = jnp.concatenate([left_col[:, :, None], maps, right_col[:, :, None]], axis=2)
    return jnp.concatenate([top_row[:, None], middle, bottom_row[:, None]], axis=1)


def conv_tiles(padded, kernel):
    count = padded.shape[0]
    side = padded.shape[1] - 2
    chans = padded.shape[3]
    total = jnp.zeros((count * side * side, kernel.shape[3]), jnp.float32)
    for row_off in range(3):
        for col_off in range(3):
            window = padded[:, row_off:row_off + side, col_off:col_off + side, :].reshape(-1, chans)
            total = total + jnp.dot(window, kernel[row_off, col_off], preferred_element_type=jnp.float32)
    return jax.nn.gelu(total).astype(jnp.bfloat16).reshape(count, side, side, -1)


def patchify(hidden, patch):
    count, side, _, chans = hidden.shape
    blocks = side // patch
    grid = hidden.reshape(count, blocks, patch, blocks, patch, chans).transpose(0, 1, 3, 2, 4, 5)
    return grid.reshape(count * blocks * blocks, patch * patch * chans)


def reference(features, neighbours, conv_weight, patch_weight, query_weight, key_weight, value_weight, output_weight, cotangent):
    all_faces = jnp.concatenate([tile_faces(features), jnp.zeros((1, 4, CELLS, CH), jnp.bfloat16)], axis=0)
    padded = pad_tiles(features, all_faces, neighbours)
    hidden = conv_tiles(padded, conv_weight)
    tokens = jnp.dot(patchify(hidden, PATCH), patch_weight, preferred_element_type=jnp.float32).astype(jnp.bfloat16)
    query = jnp.dot(tokens, query_weight, preferred_element_type=jnp.float32).astype(jnp.bfloat16)
    keys = jnp.dot(tokens, key_weight, preferred_element_type=jnp.float32).astype(jnp.bfloat16)
    values = jnp.dot(tokens, value_weight, preferred_element_type=jnp.float32).astype(jnp.bfloat16)
    keys_f = keys.astype(jnp.float32).reshape(TOKENS, HEADS, HD)
    values_f = values.astype(jnp.float32).reshape(TOKENS, HEADS, HD)
    scale = HD ** -0.5

    def attend_block(query_block):
        scores = jnp.einsum("qhd,khd->hqk", query_block.astype(jnp.float32), keys_f) * scale
        weights = jax.nn.softmax(scores, axis=-1).astype(jnp.bfloat16).astype(jnp.float32)
        return jnp.einsum("hqk,khd->qhd", weights, values_f)

    blocks = query.reshape(N_TILE, TOK_DEV, HEADS, HD)
    attended = lax.map(attend_block, blocks).reshape(TOKENS, DM).astype(jnp.bfloat16)
    mixed = (tokens.astype(jnp.float32) + jnp.dot(attended, output_weight, preferred_element_type=jnp.float32)).astype(jnp.bfloat16)
    output_grad = jnp.dot(attended.T, cotangent, preferred_element_type=jnp.float32)
    return mixed, output_grad
```

```python
import jax
import jax.numpy as jnp
from jax import lax
from jax.experimental import pallas as pl
from jax.experimental.pallas import tpu as pltpu
from jax.sharding import PartitionSpec as P

PATCH = 4
HEADS = 12
HD = 64
DM = 768
SPLIT = 4
HG = HEADS // SPLIT
GW = HG * HD
BLK = 32
QKVW = 640
OW = 256
HALO = 144
BF = jnp.bfloat16
F32 = jnp.float32


def hi_bit(coord):
    return coord >> 1


def lo_bit(coord):
    return (coord ^ (coord >> 1)) & 1


def split_device(dev):
    z, y, x = dev >> 4, (dev >> 2) & 3, dev & 3
    outer = hi_bit(z) * 4 + hi_bit(y) * 2 + hi_bit(x)
    inner = lo_bit(z) * 4 + lo_bit(y) * 2 + lo_bit(x)
    return outer, inner


def device_groups():
    place = {}
    for dev in range(64):
        place[split_device(dev)] = dev
    inner_groups = [[place[(a, b)] for b in range(8)] for a in range(8)]
    outer_groups = [[place[(a, b)] for a in range(8)] for b in range(8)]
    return inner_groups, outer_groups


INNER, OUTER = device_groups()


def swap(x, groups=None):
    return lax.all_to_all(
        x, "tile", split_axis=0, concat_axis=0, tiled=True, axis_index_groups=groups
    )


EDGES = ((1, 0, 32), (6, 32, 0), (3, 64, 96), (4, 96, 64))
CORNERS = ((0, 0, 3), (2, 31, 2), (5, 32, 1), (7, 63, 0))


def route_kernel(links_ref, mine_ref, faces_ref, out_ref):
    out_ref[...] = jnp.zeros(out_ref.shape, BF)
    mine = mine_ref[0]
    row_ids = lax.broadcasted_iota(jnp.int32, (16, 256), 0)

    def per_tile(src, carry):
        def target(direction):
            tile = links_ref[src * 8 + direction]
            outer, inner = split_device(tile >> 1)
            return (tile < 128) & (inner == mine), outer & 7, tile & 1

        for direction, first, dest in EDGES:
            hit, outer, slot = target(direction)

            @pl.when(hit)
            def _():
                out_ref[outer * 2 + slot, dest : dest + 32, :] = faces_ref[src, first : first + 32, :]

        for direction, row, dest in CORNERS:
            hit, outer, slot = target(direction)

            @pl.when(hit)
            def _():
                base = row // 16 * 16
                cell = faces_ref[src, base : base + 16, :].astype(F32)[row - base : row - base + 1, :]
                old = out_ref[outer * 2 + slot, 128:144, :].astype(F32)
                new = jnp.where(row_ids == dest, jnp.broadcast_to(cell, (16, 256)), old)
                out_ref[outer * 2 + slot, 128:144, :] = new.astype(BF)

        return carry

    lax.fori_loop(0, 16, per_tile, 0)


def route(links, mine, faces):
    return pl.pallas_call(
        route_kernel,
        grid=(1,),
        in_specs=[
            pl.BlockSpec(memory_space=pltpu.SMEM),
            pl.BlockSpec(memory_space=pltpu.SMEM),
            pl.BlockSpec((16, HALO, 256), lambda i: (0, 0, 0)),
        ],
        out_specs=pl.BlockSpec((16, HALO, 256), lambda i: (0, 0, 0)),
        out_shape=jax.ShapeDtypeStruct((16, HALO, 256), BF),
        name="route",
    )(links, mine, faces)


def attend_kernel(q_ref, kv_ref, out_ref, key_ref, val_ref):
    @pl.when(pl.program_id(0) == 0)
    def _():
        lanes = lax.broadcasted_iota(jnp.int32, (2048, 64), 1)
        ones = jnp.where(lanes == 0, 1.0, 0.0).astype(BF)
        for g in range(HG):
            key_ref[g] = kv_ref[:, GW + g * HD : GW + (g + 1) * HD]
            val_ref[g, :, :HD] = kv_ref[:, 2 * GW + g * HD : 2 * GW + (g + 1) * HD]
            val_ref[g, :, HD:] = ones

    rows = q_ref.shape[0]
    lanes = lax.broadcasted_iota(jnp.int32, (rows, OW - GW), 1)
    tail = jnp.zeros((rows, OW - GW), F32)
    for g in range(HG):
        query = q_ref[:, g * HD : (g + 1) * HD] * BF(HD ** -0.5)
        scores = lax.dot_general(
            query, key_ref[g], (((1,), (1,)), ((), ())), preferred_element_type=F32
        )
        top = jnp.max(scores, axis=1, keepdims=True)
        weights = jnp.exp(scores - top).astype(BF)
        res = jnp.dot(weights, val_ref[g], preferred_element_type=F32)
        total = res[:, HD : HD + 1]
        out_ref[:, g * HD : (g + 1) * HD] = (res[:, :HD] / total).astype(BF)
        lse = top + jnp.log(total)
        first = lse.astype(BF).astype(F32)
        second = (lse - first).astype(BF).astype(F32)
        third = lse - first - second
        for n, part in enumerate((first, second, third)):
            tail = jnp.where(lanes == 3 * g + n, part, tail)
    out_ref[:, GW:] = tail.astype(BF)


def attend(packed):
    rows = 256
    return pl.pallas_call(
        attend_kernel,
        grid=(2048 // rows,),
        in_specs=[
            pl.BlockSpec((rows, QKVW), lambda i: (i, 0)),
            pl.BlockSpec((2048, QKVW), lambda i: (0, 0)),
        ],
        out_specs=pl.BlockSpec((rows, OW), lambda i: (i, 0)),
        out_shape=jax.ShapeDtypeStruct((2048, OW), BF),
        scratch_shapes=[pltpu.VMEM((HG, 2048, HD), BF), pltpu.VMEM((HG, 2048, 2 * HD), BF)],
        compiler_params=pltpu.CompilerParams(vmem_limit_bytes=48 << 20),
        name="attend",
    )(packed, packed)


def finish_kernel(parts_ref, tokens_ref, weight_ref, cot_ref, mixed_ref, grad_ref, att_ref):
    for h in range(SPLIT):
        for a in range(SPLIT):
            pieces = [parts_ref[(h * SPLIT + a) * SPLIT + b].astype(F32) for b in range(SPLIT)]
            for g in range(HG):
                col = GW + 3 * g
                lses = [
                    p[:, col : col + 1] + p[:, col + 1 : col + 2] + p[:, col + 2 : col + 3] for p in pieces
                ]
                top = jnp.maximum(jnp.maximum(lses[0], lses[1]), jnp.maximum(lses[2], lses[3]))
                ws = [jnp.exp(v - top) for v in lses]
                total = ws[0] + ws[1] + ws[2] + ws[3]
                acc = sum(w * p[:, g * HD : (g + 1) * HD] for w, p in zip(ws, pieces)) / total
                att_ref[a * BLK : (a + 1) * BLK, h * GW + g * HD : h * GW + (g + 1) * HD] = acc.astype(BF)
    att = att_ref[...]
    grad_ref[...] = lax.dot_general(
        att, cot_ref[...], (((0,), (0,)), ((), ())), preferred_element_type=F32
    ).astype(BF)
    mixed_ref[...] = (
        tokens_ref[...].astype(F32) + jnp.dot(att, weight_ref[...], preferred_element_type=F32)
    ).astype(BF)


def finish(parts, tokens, weight, cot):
    return pl.pallas_call(
        finish_kernel,
        out_shape=(
            jax.ShapeDtypeStruct((128, DM), BF),
            jax.ShapeDtypeStruct((DM, DM), BF),
        ),
        scratch_shapes=[pltpu.VMEM((128, DM), BF)],
        name="finish",
    )(parts, tokens, weight, cot)


def pad_tiles(maps, halo):
    top_row = jnp.concatenate([halo[:, 128:129], halo[:, 0:32], halo[:, 129:130]], axis=1)
    bottom_row = jnp.concatenate([halo[:, 130:131], halo[:, 32:64], halo[:, 131:132]], axis=1)
    middle = jnp.concatenate([halo[:, 64:96, None], maps, halo[:, 96:128, None]], axis=2)
    return jnp.concatenate([top_row[:, None], middle, bottom_row[:, None]], axis=1)


def conv_tiles(padded, kernel):
    count = padded.shape[0]
    side = padded.shape[1] - 2
    chans = padded.shape[3]
    total = jnp.zeros((count * side * side, kernel.shape[3]), F32)
    for row_off in range(3):
        for col_off in range(3):
            window = padded[:, row_off : row_off + side, col_off : col_off + side, :].reshape(-1, chans)
            total = total + jnp.dot(window, kernel[row_off, col_off], preferred_element_type=F32)
    return jax.nn.gelu(total).astype(BF).reshape(count, side, side, -1)


def patchify(hidden, patch):
    count, side, _, chans = hidden.shape
    blocks = side // patch
    grid = hidden.reshape(count, blocks, patch, blocks, patch, chans).transpose(0, 1, 3, 2, 4, 5)
    return grid.reshape(count * blocks * blocks, patch * patch * chans)


def local(
    features,
    neighbours,
    conv_weight,
    patch_weight,
    query_weight,
    key_weight,
    value_weight,
    output_weight,
    cotangent,
):
    outer, inner = split_device(lax.axis_index("tile"))
    link_rows = jnp.pad(neighbours.astype(BF)[:, None, :], ((0, 0), (0, 15), (0, 248)))
    faces = jnp.concatenate(
        [features[:, 0], features[:, -1], features[:, :, 0], features[:, :, -1], link_rows], axis=1
    )
    faces = swap(jnp.broadcast_to(faces[None], (8,) + faces.shape), INNER).reshape(16, HALO, 256)
    links = faces[:, 128, :8].astype(jnp.int32).reshape(128)
    halo = swap(route(links, inner.reshape(1), faces), OUTER).reshape(8, 2, HALO, 256)
    halo = jnp.sum(halo.astype(F32), axis=0).astype(BF)
    hidden = conv_tiles(pad_tiles(features, halo), conv_weight)
    tokens = jnp.dot(patchify(hidden, PATCH), patch_weight, preferred_element_type=F32).astype(BF)
    query = jnp.dot(tokens, query_weight, preferred_element_type=F32).astype(BF)
    keys = jnp.dot(tokens, key_weight, preferred_element_type=F32).astype(BF)
    values = jnp.dot(tokens, value_weight, preferred_element_type=F32).astype(BF)

    def by_block(x):
        return x.reshape(SPLIT, BLK, SPLIT, GW).transpose(2, 0, 1, 3)

    full = (SPLIT, SPLIT, SPLIT, BLK, GW)
    packed = jnp.concatenate(
        [
            jnp.broadcast_to(by_block(query)[:, :, None], full),
            jnp.broadcast_to(by_block(keys)[:, None], full),
            jnp.broadcast_to(by_block(values)[:, None], full),
            jnp.zeros((SPLIT, SPLIT, SPLIT, BLK, QKVW - 3 * GW), BF),
        ],
        axis=-1,
    ).reshape(64, BLK, QKVW)
    packed = swap(packed).reshape(64 * BLK, QKVW)
    parts = swap(attend(packed).reshape(64, BLK, OW))
    mixed, grad = finish(parts, tokens, output_weight, cotangent)

    def total(x):
        return jnp.sum(x.reshape(8, DM // 8, DM).astype(F32), axis=0).astype(BF)

    grad = total(swap(grad.reshape(8, DM // 8, DM), INNER))
    grad = total(swap(jnp.broadcast_to(grad[None], (8,) + grad.shape), OUTER))
    grad = swap(jnp.broadcast_to(grad[None], (8,) + grad.shape), INNER)
    return mixed, grad.reshape(DM, DM).astype(F32)


def solution(mesh):
    in_specs = (
        P(("slide", "tile"), None, None, None),
        P(("slide", "tile"), None),
        P(),
        P(),
        P(),
        P(),
        P(),
        P(),
        P(("slide", "tile"), None),
    )
    out_specs = (P(("slide", "tile"), None), P("slide", None))
    return jax.shard_map(local, mesh=mesh, in_specs=in_specs, out_specs=out_specs, check_vma=False)
```

```python
import jax
import jax.numpy as jnp
from jax import lax
from jax.experimental import pallas as pl
from jax.experimental.pallas import tpu as pltpu
from jax.sharding import PartitionSpec as P

PATCH = 4
HEADS = 12
HD = 64
DM = 768
SPLIT = 4
HG = HEADS // SPLIT
GW = HG * HD
BLK = 32
QKVW = 640
OW = 256
HALO = 136
BF = jnp.bfloat16
F32 = jnp.float32


def hi_bit(coord):
    return coord >> 1


def lo_bit(coord):
    return (coord ^ (coord >> 1)) & 1


def split_device(dev):
    z, y, x = dev >> 4, (dev >> 2) & 3, dev & 3
    outer = hi_bit(z) * 4 + hi_bit(y) * 2 + hi_bit(x)
    inner = lo_bit(z) * 4 + lo_bit(y) * 2 + lo_bit(x)
    return outer, inner


def device_groups():
    place = {}
    for dev in range(64):
        place[split_device(dev)] = dev
    inner_groups = [[place[(a, b)] for b in range(8)] for a in range(8)]
    outer_groups = [[place[(a, b)] for a in range(8)] for b in range(8)]
    return inner_groups, outer_groups


INNER, OUTER = device_groups()


def swap(x, groups=None):
    return lax.all_to_all(
        x, "tile", split_axis=0, concat_axis=0, tiled=True, axis_index_groups=groups
    )


EDGES = ((1, 0, 32), (6, 32, 0), (3, 64, 96), (4, 96, 64))
CORNERS = ((0, 0, 3), (2, 31, 2), (5, 32, 1), (7, 63, 0))


def route_kernel(links_ref, mine_ref, faces_ref, out_ref):
    out_ref[...] = jnp.zeros(out_ref.shape, BF)
    mine = mine_ref[0]
    row_ids = lax.broadcasted_iota(jnp.int32, (8, 256), 0)

    def per_tile(src, carry):
        def target(direction):
            tile = links_ref[src * 8 + direction]
            outer, inner = split_device(tile >> 1)
            return (tile < 128) & (inner == mine), outer & 7, tile & 1

        for direction, first, dest in EDGES:
            hit, outer, slot = target(direction)

            @pl.when(hit)
            def _():
                out_ref[outer * 2 + slot, dest : dest + 32, :] = faces_ref[src, first : first + 32, :]

        for direction, row, dest in CORNERS:
            hit, outer, slot = target(direction)

            @pl.when(hit)
            def _():
                base = row // 8 * 8
                cell = faces_ref[src, base : base + 8, :].astype(F32)[row - base : row - base + 1, :]
                old = out_ref[outer * 2 + slot, 128:HALO, :].astype(F32)
                new = jnp.where(row_ids == dest, jnp.broadcast_to(cell, (8, 256)), old)
                out_ref[outer * 2 + slot, 128:HALO, :] = new.astype(BF)

        return carry

    lax.fori_loop(0, 16, per_tile, 0)


def route(links, mine, faces):
    return pl.pallas_call(
        route_kernel,
        grid=(1,),
        in_specs=[
            pl.BlockSpec(memory_space=pltpu.SMEM),
            pl.BlockSpec(memory_space=pltpu.SMEM),
            pl.BlockSpec((16, HALO, 256), lambda i: (0, 0, 0)),
        ],
        out_specs=pl.BlockSpec((16, HALO, 256), lambda i: (0, 0, 0)),
        out_shape=jax.ShapeDtypeStruct((16, HALO, 256), BF),
        name="route",
    )(links, mine, faces)


def attend_kernel(q_ref, kv_ref, out_ref, key_ref, val_ref):
    @pl.when(pl.program_id(0) == 0)
    def _():
        lanes = lax.broadcasted_iota(jnp.int32, (2048, 64), 1)
        ones = jnp.where(lanes == 0, 1.0, 0.0).astype(BF)
        for g in range(HG):
            key_ref[g] = kv_ref[:, GW + g * HD : GW + (g + 1) * HD]
            val_ref[g, :, :HD] = kv_ref[:, 2 * GW + g * HD : 2 * GW + (g + 1) * HD]
            val_ref[g, :, HD:] = ones

    rows = q_ref.shape[0]
    lanes = lax.broadcasted_iota(jnp.int32, (rows, OW - GW), 1)
    tail = jnp.zeros((rows, OW - GW), F32)
    for g in range(HG):
        query = q_ref[:, g * HD : (g + 1) * HD] * BF(HD ** -0.5)
        scores = lax.dot_general(
            query, key_ref[g], (((1,), (1,)), ((), ())), preferred_element_type=F32
        )
        top = jnp.max(scores, axis=1, keepdims=True)
        weights = jnp.exp(scores - top).astype(BF)
        res = jnp.dot(weights, val_ref[g], preferred_element_type=F32)
        total = res[:, HD : HD + 1]
        out_ref[:, g * HD : (g + 1) * HD] = (res[:, :HD] / total).astype(BF)
        lse = top + jnp.log(total)
        first = lse.astype(BF).astype(F32)
        second = (lse - first).astype(BF).astype(F32)
        third = lse - first - second
        for n, part in enumerate((first, second, third)):
            tail = jnp.where(lanes == 3 * g + n, part, tail)
    out_ref[:, GW:] = tail.astype(BF)


def attend(packed):
    rows = 256
    return pl.pallas_call(
        attend_kernel,
        grid=(2048 // rows,),
        in_specs=[
            pl.BlockSpec((rows, QKVW), lambda i: (i, 0)),
            pl.BlockSpec((2048, QKVW), lambda i: (0, 0)),
        ],
        out_specs=pl.BlockSpec((rows, OW), lambda i: (i, 0)),
        out_shape=jax.ShapeDtypeStruct((2048, OW), BF),
        scratch_shapes=[pltpu.VMEM((HG, 2048, HD), BF), pltpu.VMEM((HG, 2048, 2 * HD), BF)],
        compiler_params=pltpu.CompilerParams(vmem_limit_bytes=48 << 20),
        name="attend",
    )(packed, packed)


def finish_kernel(parts_ref, tokens_ref, weight_ref, cot_ref, mixed_ref, grad_ref, att_ref):
    for h in range(SPLIT):
        for a in range(SPLIT):
            pieces = [parts_ref[(h * SPLIT + a) * SPLIT + b].astype(F32) for b in range(SPLIT)]
            for g in range(HG):
                col = GW + 3 * g
                lses = [
                    p[:, col : col + 1] + p[:, col + 1 : col + 2] + p[:, col + 2 : col + 3] for p in pieces
                ]
                top = jnp.maximum(jnp.maximum(lses[0], lses[1]), jnp.maximum(lses[2], lses[3]))
                ws = [jnp.exp(v - top) for v in lses]
                total = ws[0] + ws[1] + ws[2] + ws[3]
                acc = sum(w * p[:, g * HD : (g + 1) * HD] for w, p in zip(ws, pieces)) / total
                att_ref[a * BLK : (a + 1) * BLK, h * GW + g * HD : h * GW + (g + 1) * HD] = acc.astype(BF)
    att = att_ref[...]
    grad = lax.dot_general(att, cot_ref[...], (((0,), (0,)), ((), ())), preferred_element_type=F32)
    for c in range(DM // 128):
        grad_ref[c] = grad[:, c * 128 : (c + 1) * 128].astype(BF)
    mixed_ref[...] = (
        tokens_ref[...].astype(F32) + jnp.dot(att, weight_ref[...], preferred_element_type=F32)
    ).astype(BF)


def finish(parts, tokens, weight, cot):
    return pl.pallas_call(
        finish_kernel,
        out_shape=(
            jax.ShapeDtypeStruct((128, DM), BF),
            jax.ShapeDtypeStruct((DM // 128, DM, 128), BF),
        ),
        scratch_shapes=[pltpu.VMEM((128, DM), BF)],
        name="finish",
    )(parts, tokens, weight, cot)


def pad_tiles(maps, halo):
    top_row = jnp.concatenate([halo[:, 128:129], halo[:, 0:32], halo[:, 129:130]], axis=1)
    bottom_row = jnp.concatenate([halo[:, 130:131], halo[:, 32:64], halo[:, 131:132]], axis=1)
    middle = jnp.concatenate([halo[:, 64:96, None], maps, halo[:, 96:128, None]], axis=2)
    return jnp.concatenate([top_row[:, None], middle, bottom_row[:, None]], axis=1)


def conv_tiles(padded, kernel):
    count = padded.shape[0]
    side = padded.shape[1] - 2
    chans = padded.shape[3]
    total = jnp.zeros((count * side * side, kernel.shape[3]), F32)
    for row_off in range(3):
        for col_off in range(3):
            window = padded[:, row_off : row_off + side, col_off : col_off + side, :].reshape(-1, chans)
            total = total + jnp.dot(window, kernel[row_off, col_off], preferred_element_type=F32)
    return jax.nn.gelu(total).astype(BF).reshape(count, side, side, -1)


def patchify(hidden, patch):
    count, side, _, chans = hidden.shape
    blocks = side // patch
    grid = hidden.reshape(count, blocks, patch, blocks, patch, chans).transpose(0, 1, 3, 2, 4, 5)
    return grid.reshape(count * blocks * blocks, patch * patch * chans)


def local(
    features,
    neighbours,
    conv_weight,
    patch_weight,
    query_weight,
    key_weight,
    value_weight,
    output_weight,
    cotangent,
):
    outer, inner = split_device(lax.axis_index("tile"))
    link_rows = jnp.pad(neighbours.astype(BF)[:, None, :], ((0, 0), (0, 7), (0, 248)))
    faces = jnp.concatenate(
        [features[:, 0], features[:, -1], features[:, :, 0], features[:, :, -1], link_rows], axis=1
    )
    faces = swap(jnp.broadcast_to(faces[None], (8,) + faces.shape), INNER).reshape(16, HALO, 256)
    links = faces[:, 128, :8].astype(jnp.int32).reshape(128)
    halo = swap(route(links, inner.reshape(1), faces), OUTER).reshape(8, 2, HALO, 256)
    halo = jnp.sum(halo.astype(F32), axis=0).astype(BF)
    hidden = conv_tiles(pad_tiles(features, halo), conv_weight)
    tokens = jnp.dot(patchify(hidden, PATCH), patch_weight, preferred_element_type=F32).astype(BF)
    query = jnp.dot(tokens, query_weight, preferred_element_type=F32).astype(BF)
    keys = jnp.dot(tokens, key_weight, preferred_element_type=F32).astype(BF)
    values = jnp.dot(tokens, value_weight, preferred_element_type=F32).astype(BF)

    def by_block(x):
        return x.reshape(SPLIT, BLK, SPLIT, GW).transpose(2, 0, 1, 3)

    full = (SPLIT, SPLIT, SPLIT, BLK, GW)
    packed = jnp.concatenate(
        [
            jnp.broadcast_to(by_block(query)[:, :, None], full),
            jnp.broadcast_to(by_block(keys)[:, None], full),
            jnp.broadcast_to(by_block(values)[:, None], full),
            jnp.zeros((SPLIT, SPLIT, SPLIT, BLK, QKVW - 3 * GW), BF),
        ],
        axis=-1,
    ).reshape(64, BLK, QKVW)
    packed = swap(packed).reshape(64 * BLK, QKVW)
    parts = swap(attend(packed).reshape(64, BLK, OW))
    mixed, grad = finish(parts, tokens, output_weight, cotangent)

    grad = swap(grad.reshape(64, 72, 128))
    grad = jnp.sum(grad.astype(F32), axis=0).astype(BF)
    grad = swap(jnp.broadcast_to(grad[None], (64, 72, 128)))
    grad = grad.reshape(DM // 128, DM, 128).transpose(1, 0, 2).reshape(DM, DM)
    return mixed, grad.astype(F32)


def solution(mesh):
    in_specs = (
        P(("slide", "tile"), None, None, None),
        P(("slide", "tile"), None),
        P(),
        P(),
        P(),
        P(),
        P(),
        P(),
        P(("slide", "tile"), None),
    )
    out_specs = (P(("slide", "tile"), None), P("slide", None))
    return jax.shard_map(local, mesh=mesh, in_specs=in_specs, out_specs=out_specs, check_vma=False)
```

```python
import jax
import jax.numpy as jnp
from jax import lax
from jax.experimental import pallas as pl
from jax.experimental.pallas import tpu as pltpu
from jax.sharding import PartitionSpec as P

PATCH = 4
HEADS = 12
HD = 64
DM = 768
SPLIT = 4
HG = HEADS // SPLIT
GW = HG * HD
BLK = 32
CHUNK = 144
OW = 256
HALO = 136
BF = jnp.bfloat16
F32 = jnp.float32


def hi_bit(coord):
    return coord >> 1


def lo_bit(coord):
    return (coord ^ (coord >> 1)) & 1


def split_device(dev):
    z, y, x = dev >> 4, (dev >> 2) & 3, dev & 3
    outer = hi_bit(z) * 4 + hi_bit(y) * 2 + hi_bit(x)
    inner = lo_bit(z) * 4 + lo_bit(y) * 2 + lo_bit(x)
    return outer, inner


def device_groups():
    place = {}
    for dev in range(64):
        place[split_device(dev)] = dev
    inner_groups = [[place[(a, b)] for b in range(8)] for a in range(8)]
    outer_groups = [[place[(a, b)] for a in range(8)] for b in range(8)]
    return inner_groups, outer_groups


INNER, OUTER = device_groups()


def swap(x, groups=None):
    return lax.all_to_all(
        x, "tile", split_axis=0, concat_axis=0, tiled=True, axis_index_groups=groups
    )


EDGES = ((1, 0, 32), (6, 32, 0), (3, 64, 96), (4, 96, 64))
CORNERS = ((0, 0, 3), (2, 31, 2), (5, 32, 1), (7, 63, 0))


def route_kernel(links_ref, mine_ref, faces_ref, out_ref):
    out_ref[...] = jnp.zeros(out_ref.shape, BF)
    mine = mine_ref[0]
    row_ids = lax.broadcasted_iota(jnp.int32, (8, 256), 0)

    def per_tile(src, carry):
        def target(direction):
            tile = links_ref[src * 8 + direction]
            outer, inner = split_device(tile >> 1)
            return (tile < 128) & (inner == mine), outer & 7, tile & 1

        for direction, first, dest in EDGES:
            hit, outer, slot = target(direction)

            @pl.when(hit)
            def _():
                out_ref[outer * 2 + slot, dest : dest + 32, :] = faces_ref[src, first : first + 32, :]

        for direction, row, dest in CORNERS:
            hit, outer, slot = target(direction)

            @pl.when(hit)
            def _():
                base = row // 8 * 8
                cell = faces_ref[src, base : base + 8, :].astype(F32)[row - base : row - base + 1, :]
                old = out_ref[outer * 2 + slot, 128:HALO, :].astype(F32)
                new = jnp.where(row_ids == dest, jnp.broadcast_to(cell, (8, 256)), old)
                out_ref[outer * 2 + slot, 128:HALO, :] = new.astype(BF)

        return carry

    lax.fori_loop(0, 16, per_tile, 0)


def route(links, mine, faces):
    return pl.pallas_call(
        route_kernel,
        grid=(1,),
        in_specs=[
            pl.BlockSpec(memory_space=pltpu.SMEM),
            pl.BlockSpec(memory_space=pltpu.SMEM),
            pl.BlockSpec((16, HALO, 256), lambda i: (0, 0, 0)),
        ],
        out_specs=pl.BlockSpec((16, HALO, 256), lambda i: (0, 0, 0)),
        out_shape=jax.ShapeDtypeStruct((16, HALO, 256), BF),
        name="route",
    )(links, mine, faces)


def attend_kernel(in_ref, all_ref, out_ref, key_ref, val_ref):
    @pl.when(pl.program_id(0) == 0)
    def _():
        lanes = lax.broadcasted_iota(jnp.int32, (2048, HD), 1)
        ones = jnp.where(lanes == 0, 1.0, 0.0).astype(BF)
        for g in range(HG):
            val_ref[g, :, HD:] = ones
        for g in range(2):
            key_ref[g] = all_ref[:, 32:64, g * HD : (g + 1) * HD].reshape(2048, HD)
            val_ref[g, :, :HD] = all_ref[:, 64:96, g * HD : (g + 1) * HD].reshape(2048, HD)
            key_ref[2, g * 1024 : (g + 1) * 1024, :] = all_ref[
                :, 96 + g * 16 : 112 + g * 16, HD:
            ].reshape(1024, HD)
            val_ref[2, g * 1024 : (g + 1) * 1024, :HD] = all_ref[
                :, 128:144, g * HD : (g + 1) * HD
            ].reshape(1024, HD)

    rows = in_ref.shape[0] * BLK
    lanes = lax.broadcasted_iota(jnp.int32, (rows, HD), 1)
    tail = jnp.zeros((rows, HD), F32)
    for g in range(HG):
        first, lane = ((0, 0), (0, HD), (96, 0))[g]
        query = in_ref[:, first : first + BLK, lane : lane + HD].reshape(rows, HD) * BF(HD ** -0.5)
        scores = lax.dot_general(
            query, key_ref[g], (((1,), (1,)), ((), ())), preferred_element_type=F32
        )
        top = jnp.max(scores, axis=1, keepdims=True)
        weights = jnp.exp(scores - top).astype(BF)
        res = jnp.dot(weights, val_ref[g], preferred_element_type=F32)
        total = res[:, HD : HD + 1]
        out_ref[:, g * HD : (g + 1) * HD] = (res[:, :HD] / total).astype(BF)
        lse = top + jnp.log(total)
        one = lse.astype(BF).astype(F32)
        two = (lse - one).astype(BF).astype(F32)
        three = lse - one - two
        for n, part in enumerate((one, two, three)):
            tail = jnp.where(lanes == 3 * g + n, part, tail)
    out_ref[:, GW:] = tail.astype(BF)


def attend(packed):
    srcs = 8
    return pl.pallas_call(
        attend_kernel,
        grid=(64 // srcs,),
        in_specs=[
            pl.BlockSpec((srcs, CHUNK, 128), lambda i: (i, 0, 0)),
            pl.BlockSpec((64, CHUNK, 128), lambda i: (0, 0, 0)),
        ],
        out_specs=pl.BlockSpec((srcs * BLK, OW), lambda i: (i, 0)),
        out_shape=jax.ShapeDtypeStruct((2048, OW), BF),
        scratch_shapes=[pltpu.VMEM((HG, 2048, HD), BF), pltpu.VMEM((HG, 2048, 2 * HD), BF)],
        compiler_params=pltpu.CompilerParams(vmem_limit_bytes=48 << 20),
        name="attend",
    )(packed, packed)


def finish_kernel(parts_ref, tokens_ref, weight_ref, cot_ref, mixed_ref, grad_ref, att_ref):
    for h in range(SPLIT):
        for a in range(SPLIT):
            pieces = [parts_ref[(h * SPLIT + a) * SPLIT + b].astype(F32) for b in range(SPLIT)]
            for g in range(HG):
                col = GW + 3 * g
                lses = [
                    p[:, col : col + 1] + p[:, col + 1 : col + 2] + p[:, col + 2 : col + 3] for p in pieces
                ]
                top = jnp.maximum(jnp.maximum(lses[0], lses[1]), jnp.maximum(lses[2], lses[3]))
                ws = [jnp.exp(v - top) for v in lses]
                total = ws[0] + ws[1] + ws[2] + ws[3]
                acc = sum(w * p[:, g * HD : (g + 1) * HD] for w, p in zip(ws, pieces)) / total
                head = 2 * h + g if g < 2 else 8 + h
                att_ref[a * BLK : (a + 1) * BLK, head * HD : (head + 1) * HD] = acc.astype(BF)
    att = att_ref[...]
    grad = lax.dot_general(att, cot_ref[...], (((0,), (0,)), ((), ())), preferred_element_type=F32)
    for c in range(DM // 128):
        grad_ref[c] = grad[:, c * 128 : (c + 1) * 128].astype(BF)
    mixed_ref[...] = (
        tokens_ref[...].astype(F32) + jnp.dot(att, weight_ref[...], preferred_element_type=F32)
    ).astype(BF)


def finish(parts, tokens, weight, cot):
    return pl.pallas_call(
        finish_kernel,
        out_shape=(
            jax.ShapeDtypeStruct((128, DM), BF),
            jax.ShapeDtypeStruct((DM // 128, DM, 128), BF),
        ),
        scratch_shapes=[pltpu.VMEM((128, DM), BF)],
        name="finish",
    )(parts, tokens, weight, cot)


def spread_kernel(in_ref, out_ref):
    out_ref[...] = in_ref[0].astype(F32)


def spread(grad):
    return pl.pallas_call(
        spread_kernel,
        grid=(DM // 128,),
        in_specs=[pl.BlockSpec((1, DM, 128), lambda i: (i, 0, 0))],
        out_specs=pl.BlockSpec((DM, 128), lambda i: (0, i)),
        out_shape=jax.ShapeDtypeStruct((DM, DM), F32),
        name="spread",
    )(grad)


ZW = 48
Z0 = 8


def stem_kernel(
    halo_ref,
    conv_ref,
    features_hbm,
    patch_hbm,
    query_hbm,
    key_hbm,
    value_hbm,
    tokens_ref,
    packed_ref,
    maps_ref,
    side_ref,
    left_ref,
    mid_ref,
    right_ref,
    hid_ref,
    patch_ref,
    wq_ref,
    wk_ref,
    wv_ref,
    sems,
):
    loads = [pltpu.make_async_copy(features_hbm.at[t], maps_ref.at[t, 1:33], sems.at[t]) for t in range(2)]
    pairs = ((patch_hbm, patch_ref), (query_hbm, wq_ref), (key_hbm, wk_ref), (value_hbm, wv_ref))
    loads += [pltpu.make_async_copy(src, dst, sems.at[2 + n]) for n, (src, dst) in enumerate(pairs)]
    for load in loads:
        load.start()
    zrefs = (left_ref, mid_ref, right_ref)

    def halo_rows(t, first, count):
        total = halo_ref[0, t, first : first + count, :].astype(F32)
        for n in range(1, 8):
            total = total + halo_ref[n, t, first : first + count, :].astype(F32)
        return total

    for t in range(2):
        maps_ref[t, 0] = halo_rows(t, 0, 32).astype(BF)
        maps_ref[t, 33] = halo_rows(t, 32, 32).astype(BF)
        corner = halo_rows(t, 128, 8)
        for side in range(2):
            side_ref[side, t, Z0 : Z0 + 32, :] = halo_rows(t, 64 + 32 * side, 32)
            side_ref[side, t, Z0 - 1 : Z0, :] = corner[side : side + 1]
            side_ref[side, t, Z0 + 32 : Z0 + 33, :] = corner[2 + side : 3 + side]
    for t in range(2):
        for side in range(2):
            edge = jnp.zeros((32, 256), F32)
            for dy in range(3):
                part = side_ref[side, t, Z0 - 1 + dy : Z0 + 31 + dy, :].astype(BF)
                edge = edge + jnp.dot(part, conv_ref[dy * 3 + side * 2], preferred_element_type=F32)
            dest, first = ((left_ref, Z0 - 1), (right_ref, Z0 + 32))[side]
            for lt in range(2):
                dest[lt, pl.ds(t * 32 * ZW + first, 32, stride=ZW), :] = edge[:, lt * 128 : lt * 128 + 128]
    for t in range(2):
        loads[t].wait()
        for y in range(0, 32, 8):
            for dx in range(3):
                acc = jnp.zeros((256, 256), F32)
                for dy in range(3):
                    rows = maps_ref[t, y + dy : y + dy + 8].reshape(256, 256)
                    acc = acc + jnp.dot(rows, conv_ref[dy * 3 + dx], preferred_element_type=F32)
                for n in range(8):
                    first = (t * 32 + y + n) * ZW + Z0
                    for lt in range(2):
                        zrefs[dx][lt, first : first + 32, :] = acc[n * 32 : n * 32 + 32, lt * 128 : lt * 128 + 128]

    for r in range(4):
        for c in range(4):
            for t in range(2):
                for pr in range(8):
                    first = (t * 32 + pr * 4 + r) * ZW + Z0 + c
                    row = (t * 8 + pr) * 8
                    for lt in range(2):
                        total = (
                            mid_ref[lt, pl.ds(first, 8, stride=4), :]
                            + left_ref[lt, pl.ds(first - 1, 8, stride=4), :]
                            + right_ref[lt, pl.ds(first + 1, 8, stride=4), :]
                        )
                        col = (r * 4 + c) * 256 + lt * 128
                        hid_ref[row : row + 8, col : col + 128] = jax.nn.gelu(total).astype(BF)
    loads[2].wait()
    tokens = jnp.dot(hid_ref[...], patch_ref[...], preferred_element_type=F32).astype(BF)
    tokens_ref[...] = tokens
    for load in loads[3:]:
        load.wait()
    query = jnp.dot(tokens, wq_ref[...], preferred_element_type=F32)
    keys = jnp.dot(tokens, wk_ref[...], preferred_element_type=F32)
    values = jnp.dot(tokens, wv_ref[...], preferred_element_type=F32)
    low = lax.broadcasted_iota(jnp.int32, (128, 128), 1) < HD

    def pair_of(x, h):
        return x[:, h * 128 : (h + 1) * 128]

    for h in range(SPLIT):
        one = 4 + h // 2
        q1, k1, v1 = pair_of(query, one), pair_of(keys, one), pair_of(values, one)
        if h % 2 == 0:
            k1 = pltpu.roll(k1, HD, 1)
            v2 = pltpu.roll(v1, HD, 1)
        else:
            q1 = pltpu.roll(q1, HD, 1)
            v2 = v1
            v1 = pltpu.roll(v1, HD, 1)
        qk = jnp.where(low, q1, k1).astype(BF)
        pieces = (pair_of(query, h).astype(BF), pair_of(keys, h).astype(BF), pair_of(values, h).astype(BF))
        for a in range(SPLIT):
            for b in range(SPLIT):
                at = (h * SPLIT + a) * SPLIT + b
                qa, kb = slice(a * BLK, (a + 1) * BLK), slice(b * BLK, (b + 1) * BLK)
                packed_ref[at, 0:32, :] = pieces[0][qa]
                packed_ref[at, 32:64, :] = pieces[1][kb]
                packed_ref[at, 64:96, :] = pieces[2][kb]
                if a == b:
                    packed_ref[at, 96:128, :] = qk[qa]
                else:
                    packed_ref[at, 96:128, :] = jnp.where(low[:BLK], q1[qa], k1[kb]).astype(BF)
                half = b * BLK + BLK // 2
                packed_ref[at, 128:144, :] = jnp.where(
                    low[: BLK // 2], v1[b * BLK : half], v2[half : (b + 1) * BLK]
                ).astype(BF)


def stem(halo, conv_weight, features, patch_weight, query_weight, key_weight, value_weight):
    hbm = pl.BlockSpec(memory_space=pl.ANY)
    vmem = pl.BlockSpec(memory_space=pltpu.VMEM)
    return pl.pallas_call(
        stem_kernel,
        in_specs=[vmem, vmem] + [hbm] * 5,
        out_specs=(vmem, vmem),
        out_shape=(
            jax.ShapeDtypeStruct((128, DM), BF),
            jax.ShapeDtypeStruct((64, CHUNK, 128), BF),
        ),
        scratch_shapes=[
            pltpu.VMEM((2, 34, 32, 256), BF),
            pltpu.VMEM((2, 2, ZW, 256), F32),
            pltpu.VMEM((2, 64 * ZW, 128), F32),
            pltpu.VMEM((2, 64 * ZW, 128), F32),
            pltpu.VMEM((2, 64 * ZW, 128), F32),
            pltpu.VMEM((128, 4096), BF),
            pltpu.VMEM((4096, DM), BF),
            pltpu.VMEM((DM, DM), BF),
            pltpu.VMEM((DM, DM), BF),
            pltpu.VMEM((DM, DM), BF),
            pltpu.SemaphoreType.DMA((6,)),
        ],
        compiler_params=pltpu.CompilerParams(vmem_limit_bytes=48 << 20),
        name="stem",
    )(halo, conv_weight, features, patch_weight, query_weight, key_weight, value_weight)


def local(
    features,
    neighbours,
    conv_weight,
    patch_weight,
    query_weight,
    key_weight,
    value_weight,
    output_weight,
    cotangent,
):
    outer, inner = split_device(lax.axis_index("tile"))
    link_rows = jnp.pad(neighbours.astype(BF)[:, None, :], ((0, 0), (0, 7), (0, 248)))
    faces = jnp.concatenate(
        [features[:, 0], features[:, -1], features[:, :, 0], features[:, :, -1], link_rows], axis=1
    )
    faces = swap(jnp.broadcast_to(faces[None], (8,) + faces.shape), INNER).reshape(16, HALO, 256)
    links = faces[:, 128, :8].astype(jnp.int32).reshape(128)
    halo = swap(route(links, inner.reshape(1), faces), OUTER).reshape(8, 2, HALO, 256)
    halo, conv_weight = lax.optimization_barrier((halo, conv_weight))
    taps = conv_weight.reshape(9, 256, 256)
    tokens, packed = stem(halo, taps, features, patch_weight, query_weight, key_weight, value_weight)
    packed = swap(packed)
    parts = swap(attend(packed).reshape(64, BLK, OW))
    mixed, grad = finish(parts, tokens, output_weight, cotangent)

    grad = swap(grad.reshape(64, 72, 128))
    grad = jnp.sum(grad.astype(F32), axis=0).astype(BF)
    grad = swap(jnp.broadcast_to(grad[None], (64, 72, 128)))
    return mixed, spread(grad.reshape(DM // 128, DM, 128))


def solution(mesh):
    in_specs = (
        P(("slide", "tile"), None, None, None),
        P(("slide", "tile"), None),
        P(),
        P(),
        P(),
        P(),
        P(),
        P(),
        P(("slide", "tile"), None),
    )
    out_specs = (P(("slide", "tile"), None), P("slide", None))
    return jax.shard_map(local, mesh=mesh, in_specs=in_specs, out_specs=out_specs, check_vma=False)
```

```python
import jax
import jax.numpy as jnp
from jax import lax
from jax.experimental import pallas as pl
from jax.experimental.pallas import tpu as pltpu
from jax.sharding import PartitionSpec as P

PATCH = 4
HEADS = 12
HD = 64
DM = 768
SPLIT = 4
HG = HEADS // SPLIT
GW = HG * HD
BLK = 32
CHUNK = 144
OW = 256
HALO = 136
BF = jnp.bfloat16
F32 = jnp.float32


def hi_bit(coord):
    return coord >> 1


def lo_bit(coord):
    return (coord ^ (coord >> 1)) & 1


def split_device(dev):
    z, y, x = dev >> 4, (dev >> 2) & 3, dev & 3
    outer = hi_bit(z) * 4 + hi_bit(y) * 2 + hi_bit(x)
    inner = lo_bit(z) * 4 + lo_bit(y) * 2 + lo_bit(x)
    return outer, inner


def device_groups():
    place = {}
    for dev in range(64):
        place[split_device(dev)] = dev
    inner_groups = [[place[(a, b)] for b in range(8)] for a in range(8)]
    outer_groups = [[place[(a, b)] for a in range(8)] for b in range(8)]
    return inner_groups, outer_groups


INNER, OUTER = device_groups()


def place(h, a, b):
    def coord(hi, lo):
        return hi * 2 + (hi ^ lo)

    return coord(a >> 1, b >> 1) * 16 + coord(a & 1, b & 1) * 4 + h


KEY_GROUPS = [[place(h, a, b) for b in range(SPLIT)] for h in range(SPLIT) for a in range(SPLIT)]
HEAD_GROUPS = [[place(h, a, b) for a in range(SPLIT) for b in range(SPLIT)] for h in range(SPLIT)]


def swap(x, groups=None):
    return lax.all_to_all(
        x, "tile", split_axis=0, concat_axis=0, tiled=True, axis_index_groups=groups
    )


EDGES = ((1, 0, 32), (6, 32, 0), (3, 64, 96), (4, 96, 64))
CORNERS = ((0, 0, 3), (2, 31, 2), (5, 32, 1), (7, 63, 0))


def route_kernel(links_ref, mine_ref, faces_ref, out_ref):
    out_ref[...] = jnp.zeros(out_ref.shape, BF)
    mine = mine_ref[0]
    row_ids = lax.broadcasted_iota(jnp.int32, (8, 256), 0)

    def per_tile(src, carry):
        def target(direction):
            tile = links_ref[src * 8 + direction]
            outer, inner = split_device(tile >> 1)
            return (tile < 128) & (inner == mine), outer & 7, tile & 1

        for direction, first, dest in EDGES:
            hit, outer, slot = target(direction)

            @pl.when(hit)
            def _():
                out_ref[outer * 2 + slot, dest : dest + 32, :] = faces_ref[src, first : first + 32, :]

        for direction, row, dest in CORNERS:
            hit, outer, slot = target(direction)

            @pl.when(hit)
            def _():
                base = row // 8 * 8
                cell = faces_ref[src, base : base + 8, :].astype(F32)[row - base : row - base + 1, :]
                old = out_ref[outer * 2 + slot, 128:HALO, :].astype(F32)
                new = jnp.where(row_ids == dest, jnp.broadcast_to(cell, (8, 256)), old)
                out_ref[outer * 2 + slot, 128:HALO, :] = new.astype(BF)

        return carry

    lax.fori_loop(0, 16, per_tile, 0)


def route(links, mine, faces):
    return pl.pallas_call(
        route_kernel,
        grid=(1,),
        in_specs=[
            pl.BlockSpec(memory_space=pltpu.SMEM),
            pl.BlockSpec(memory_space=pltpu.SMEM),
            pl.BlockSpec((16, HALO, 256), lambda i: (0, 0, 0)),
        ],
        out_specs=pl.BlockSpec((16, HALO, 256), lambda i: (0, 0, 0)),
        out_shape=jax.ShapeDtypeStruct((16, HALO, 256), BF),
        name="route",
    )(links, mine, faces)


def attend_kernel(in_ref, all_ref, out_ref, key_ref, val_ref, row_ref):
    @pl.when(pl.program_id(0) == 0)
    def _():
        lanes = lax.broadcasted_iota(jnp.int32, (2048, HD), 1)
        ones = jnp.where(lanes == 0, 1.0, 0.0).astype(BF)
        for g in range(HG):
            val_ref[g, :, HD:] = ones
        for g in range(2):
            key_ref[g] = all_ref[:, 32:64, g * HD : (g + 1) * HD].reshape(2048, HD)
            val_ref[g, :, :HD] = all_ref[:, 64:96, g * HD : (g + 1) * HD].reshape(2048, HD)
            key_ref[2, g * 1024 : (g + 1) * 1024, :] = all_ref[
                :, 96 + g * 16 : 112 + g * 16, HD:
            ].reshape(1024, HD)
            val_ref[2, g * 1024 : (g + 1) * 1024, :HD] = all_ref[
                :, 128:144, g * HD : (g + 1) * HD
            ].reshape(1024, HD)

    rows = in_ref.shape[0] * BLK
    lanes = lax.broadcasted_iota(jnp.int32, (rows, HD), 1)
    tail = jnp.zeros((rows, HD), F32)
    scores = []
    for g in range(HG):
        first, lane = ((0, 0), (0, HD), (96, 0))[g]
        query = in_ref[:, first : first + BLK, lane : lane + HD].reshape(rows, HD) * BF(HD ** -0.5)
        scores.append(
            lax.dot_general(query, key_ref[g], (((1,), (1,)), ((), ())), preferred_element_type=F32)
        )
    for g in range(HG):
        top = jnp.max(scores[g], axis=1, keepdims=True)
        weights = jnp.exp(scores[g] - top).astype(BF)
        res = jnp.dot(weights, val_ref[g], preferred_element_type=F32)
        total = res[:, HD : HD + 1]
        row_ref[:, g * HD : (g + 1) * HD] = res[:, :HD] / total
        lse = top + jnp.log(total)
        one = lse.astype(BF).astype(F32)
        two = (lse - one).astype(BF).astype(F32)
        three = lse - one - two
        for n, part in enumerate((one, two, three)):
            tail = jnp.where(lanes == 3 * g + n, part, tail)
    row_ref[:, GW:] = tail
    for n in range(rows // BLK):
        for b in range(SPLIT):
            first = n * BLK + b * 8
            out_ref[b, n * 8 : n * 8 + 8, :] = row_ref[first : first + 8, :].astype(BF)


def attend(packed):
    srcs = 8
    return pl.pallas_call(
        attend_kernel,
        grid=(64 // srcs,),
        in_specs=[
            pl.BlockSpec((srcs, CHUNK, 128), lambda i: (i, 0, 0)),
            pl.BlockSpec((64, CHUNK, 128), lambda i: (0, 0, 0)),
        ],
        out_specs=pl.BlockSpec((SPLIT, srcs * 8, OW), lambda i: (0, i, 0)),
        out_shape=jax.ShapeDtypeStruct((SPLIT, 512, OW), BF),
        scratch_shapes=[
            pltpu.VMEM((HG, 2048, HD), BF),
            pltpu.VMEM((HG, 2048, 2 * HD), BF),
            pltpu.VMEM((srcs * BLK, OW), F32),
        ],
        compiler_params=pltpu.CompilerParams(vmem_limit_bytes=48 << 20),
        name="attend",
    )(packed, packed)


SHARE = 72
ROWS = SHARE + 16


def merge_kernel(parts_ref, cot_ref, att_ref, grad_ref, pair_ref, single_ref):
    tails = []
    for b in range(SPLIT):
        tail = parts_ref[b, :, 128:].astype(F32)
        tails.append(tail + pltpu.roll(tail, 127, 1) + pltpu.roll(tail, 126, 1))
    top = jnp.maximum(jnp.maximum(tails[0], tails[1]), jnp.maximum(tails[2], tails[3]))
    ws = [jnp.exp(tail - top) for tail in tails]
    total = ws[0] + ws[1] + ws[2] + ws[3]
    low = lax.broadcasted_iota(jnp.int32, (512, 128), 1) < HD
    pair = jnp.zeros((512, 128), F32)
    single = jnp.zeros((512, 128), F32)
    for b in range(SPLIT):
        share = ws[b] / total
        w0, w1, w2 = (share[:, HD + 3 * g : HD + 3 * g + 1] for g in range(HG))
        pair = pair + jnp.where(low, w0, w1) * parts_ref[b, :, :128].astype(F32)
        single = single + w2 * parts_ref[b, :, 128:].astype(F32)
    single = jnp.where(low, single, 0.0)
    pair_ref[...] = pair.astype(BF)
    single_ref[...] = single.astype(BF)
    for n in range(64):
        att_ref[n, :8, :] = pair[n * 8 : n * 8 + 8].astype(BF)
        att_ref[n, 8:, :] = single[n * 8 : n * 8 + 8].astype(BF)
    for first, ref, count in ((0, pair_ref, 128), (128, single_ref, 64)):
        grad = lax.dot_general(
            ref[...], cot_ref[...], (((0,), (0,)), ((), ())), preferred_element_type=F32
        )
        for c in range(DM // 128):
            grad_ref[c, first : first + count, :] = grad[:count, c * 128 : (c + 1) * 128].astype(BF)


def merge(parts, cot):
    return pl.pallas_call(
        merge_kernel,
        out_shape=(
            jax.ShapeDtypeStruct((64, 16, 128), BF),
            jax.ShapeDtypeStruct((DM // 128, GW, 128), BF),
        ),
        scratch_shapes=[pltpu.VMEM((512, 128), BF), pltpu.VMEM((512, 128), BF)],
        name="merge",
    )(parts, cot)


def share_kernel(terms_ref, att_ref, out_ref):
    total = terms_ref[0].astype(F32)
    for n in range(1, 16):
        total = total + terms_ref[n].astype(F32)
    total = total.astype(BF)
    for n in range(64):
        out_ref[n, :SHARE, :] = total
        out_ref[n, SHARE:, :] = att_ref[n]


def share_out(terms, att):
    return pl.pallas_call(
        share_kernel, out_shape=jax.ShapeDtypeStruct((64, ROWS, 128), BF), name="share"
    )(terms, att)


def finish_kernel(all_ref, tokens_ref, weight_ref, mixed_ref, grad_ref, att_ref):
    lanes = lax.broadcasted_iota(jnp.int32, (8, 128), 1) < HD
    for a in range(SPLIT):
        for b in range(SPLIT):
            row = a * BLK + b * 8
            for h in range(SPLIT):
                att_ref[row : row + 8, h * 128 : (h + 1) * 128] = all_ref[place(h, a, b), SHARE : SHARE + 8, :]
            for h in range(0, SPLIT, 2):
                even = all_ref[place(h, a, b), SHARE + 8 :, :].astype(F32)
                odd = pltpu.roll(all_ref[place(h + 1, a, b), SHARE + 8 :, :].astype(F32), HD, 1)
                first = 512 + h * HD
                att_ref[row : row + 8, first : first + 128] = jnp.where(lanes, even, odd).astype(BF)
    for h in range(SPLIT):
        for m in range(16):
            at = place(h, m // SPLIT, m % SPLIT)
            done = 0
            while done < SHARE:
                block, row = divmod(m * SHARE + done, GW)
                count = min(SHARE - done, (128 if row < 128 else GW) - row)
                dest = h * 128 + row if row < 128 else 512 + h * HD + row - 128
                grad_ref[dest : dest + count, block * 128 : (block + 1) * 128] = all_ref[
                    at, done : done + count, :
                ].astype(F32)
                done += count
    mixed_ref[...] = (
        tokens_ref[...].astype(F32) + jnp.dot(att_ref[...], weight_ref[...], preferred_element_type=F32)
    ).astype(BF)


def finish(received, tokens, weight):
    return pl.pallas_call(
        finish_kernel,
        out_shape=(
            jax.ShapeDtypeStruct((128, DM), BF),
            jax.ShapeDtypeStruct((DM, DM), F32),
        ),
        scratch_shapes=[pltpu.VMEM((128, DM), BF)],
        name="finish",
    )(received, tokens, weight)


ZW = 48
Z0 = 8


def stem_kernel(
    halo_ref,
    conv_ref,
    cot_ref,
    features_hbm,
    patch_hbm,
    query_hbm,
    key_hbm,
    value_hbm,
    tokens_ref,
    packed_ref,
    cots_ref,
    maps_ref,
    side_ref,
    left_ref,
    mid_ref,
    right_ref,
    hid_ref,
    patch_ref,
    wq_ref,
    wk_ref,
    wv_ref,
    sems,
):
    loads = [pltpu.make_async_copy(features_hbm.at[t], maps_ref.at[t, 1:33], sems.at[t]) for t in range(2)]
    pairs = ((patch_hbm, patch_ref), (query_hbm, wq_ref), (key_hbm, wk_ref), (value_hbm, wv_ref))
    loads += [pltpu.make_async_copy(src, dst, sems.at[2 + n]) for n, (src, dst) in enumerate(pairs)]
    for load in loads:
        load.start()
    zrefs = (left_ref, mid_ref, right_ref)

    def halo_rows(t, first, count):
        total = halo_ref[0, t, first : first + count, :].astype(F32)
        for n in range(1, 8):
            total = total + halo_ref[n, t, first : first + count, :].astype(F32)
        return total

    for t in range(2):
        maps_ref[t, 0] = halo_rows(t, 0, 32).astype(BF)
        maps_ref[t, 33] = halo_rows(t, 32, 32).astype(BF)
        corner = halo_rows(t, 128, 8)
        for side in range(2):
            side_ref[side, t, Z0 : Z0 + 32, :] = halo_rows(t, 64 + 32 * side, 32)
            side_ref[side, t, Z0 - 1 : Z0, :] = corner[side : side + 1]
            side_ref[side, t, Z0 + 32 : Z0 + 33, :] = corner[2 + side : 3 + side]
    for t in range(2):
        for side in range(2):
            edge = jnp.zeros((32, 256), F32)
            for dy in range(3):
                part = side_ref[side, t, Z0 - 1 + dy : Z0 + 31 + dy, :].astype(BF)
                edge = edge + jnp.dot(part, conv_ref[dy * 3 + side * 2], preferred_element_type=F32)
            dest, first = ((left_ref, Z0 - 1), (right_ref, Z0 + 32))[side]
            for lt in range(2):
                dest[lt, pl.ds(t * 32 * ZW + first, 32, stride=ZW), :] = edge[:, lt * 128 : lt * 128 + 128]
    for t in range(2):
        loads[t].wait()
        for y in range(0, 32, 8):
            for dx in range(3):
                acc = jnp.zeros((256, 256), F32)
                for dy in range(3):
                    rows = maps_ref[t, y + dy : y + dy + 8].reshape(256, 256)
                    acc = acc + jnp.dot(rows, conv_ref[dy * 3 + dx], preferred_element_type=F32)
                for n in range(8):
                    first = (t * 32 + y + n) * ZW + Z0
                    for lt in range(2):
                        zrefs[dx][lt, first : first + 32, :] = acc[n * 32 : n * 32 + 32, lt * 128 : lt * 128 + 128]

    for r in range(4):
        for c in range(4):
            for t in range(2):
                for pr in range(8):
                    first = (t * 32 + pr * 4 + r) * ZW + Z0 + c
                    row = (t * 8 + pr) * 8
                    for lt in range(2):
                        total = (
                            mid_ref[lt, pl.ds(first, 8, stride=4), :]
                            + left_ref[lt, pl.ds(first - 1, 8, stride=4), :]
                            + right_ref[lt, pl.ds(first + 1, 8, stride=4), :]
                        )
                        col = (r * 4 + c) * 256 + lt * 128
                        hid_ref[row : row + 8, col : col + 128] = jax.nn.gelu(total).astype(BF)
    loads[2].wait()
    tokens = jnp.dot(hid_ref[...], patch_ref[...], preferred_element_type=F32).astype(BF)
    tokens_ref[...] = tokens
    for load in loads[3:]:
        load.wait()
    query = jnp.dot(tokens, wq_ref[...], preferred_element_type=F32)
    keys = jnp.dot(tokens, wk_ref[...], preferred_element_type=F32)
    values = jnp.dot(tokens, wv_ref[...], preferred_element_type=F32)
    low = lax.broadcasted_iota(jnp.int32, (128, 128), 1) < HD

    def pair_of(x, h):
        return x[:, h * 128 : (h + 1) * 128]

    for h in range(SPLIT):
        one = 4 + h // 2
        q1, k1, v1 = pair_of(query, one), pair_of(keys, one), pair_of(values, one)
        if h % 2 == 0:
            k1 = pltpu.roll(k1, HD, 1)
            v2 = pltpu.roll(v1, HD, 1)
        else:
            q1 = pltpu.roll(q1, HD, 1)
            v2 = v1
            v1 = pltpu.roll(v1, HD, 1)
        qk = jnp.where(low, q1, k1).astype(BF)
        pieces = (pair_of(query, h).astype(BF), pair_of(keys, h).astype(BF), pair_of(values, h).astype(BF))
        for a in range(SPLIT):
            for b in range(SPLIT):
                at = place(h, a, b)
                cots_ref[at] = cot_ref[a * BLK + b * 8 : a * BLK + b * 8 + 8, :]
                qa, kb = slice(a * BLK, (a + 1) * BLK), slice(b * BLK, (b + 1) * BLK)
                packed_ref[at, 0:32, :] = pieces[0][qa]
                packed_ref[at, 32:64, :] = pieces[1][kb]
                packed_ref[at, 64:96, :] = pieces[2][kb]
                if a == b:
                    packed_ref[at, 96:128, :] = qk[qa]
                else:
                    packed_ref[at, 96:128, :] = jnp.where(low[:BLK], q1[qa], k1[kb]).astype(BF)
                half = b * BLK + BLK // 2
                packed_ref[at, 128:144, :] = jnp.where(
                    low[: BLK // 2], v1[b * BLK : half], v2[half : (b + 1) * BLK]
                ).astype(BF)


def stem(halo, conv_weight, cotangent, features, patch_weight, query_weight, key_weight, value_weight):
    hbm = pl.BlockSpec(memory_space=pl.ANY)
    vmem = pl.BlockSpec(memory_space=pltpu.VMEM)
    return pl.pallas_call(
        stem_kernel,
        in_specs=[vmem, vmem, vmem] + [hbm] * 5,
        out_specs=(vmem, vmem, vmem),
        out_shape=(
            jax.ShapeDtypeStruct((128, DM), BF),
            jax.ShapeDtypeStruct((64, CHUNK, 128), BF),
            jax.ShapeDtypeStruct((64, 8, DM), BF),
        ),
        scratch_shapes=[
            pltpu.VMEM((2, 34, 32, 256), BF),
            pltpu.VMEM((2, 2, ZW, 256), F32),
            pltpu.VMEM((2, 64 * ZW, 128), F32),
            pltpu.VMEM((2, 64 * ZW, 128), F32),
            pltpu.VMEM((2, 64 * ZW, 128), F32),
            pltpu.VMEM((128, 4096), BF),
            pltpu.VMEM((4096, DM), BF),
            pltpu.VMEM((DM, DM), BF),
            pltpu.VMEM((DM, DM), BF),
            pltpu.VMEM((DM, DM), BF),
            pltpu.SemaphoreType.DMA((6,)),
        ],
        compiler_params=pltpu.CompilerParams(vmem_limit_bytes=48 << 20),
        name="stem",
    )(halo, conv_weight, cotangent, features, patch_weight, query_weight, key_weight, value_weight)


def local(
    features,
    neighbours,
    conv_weight,
    patch_weight,
    query_weight,
    key_weight,
    value_weight,
    output_weight,
    cotangent,
):
    outer, inner = split_device(lax.axis_index("tile"))
    link_rows = jnp.pad(neighbours.astype(BF)[:, None, :], ((0, 0), (0, 7), (0, 248)))
    faces = jnp.concatenate(
        [features[:, 0], features[:, -1], features[:, :, 0], features[:, :, -1], link_rows], axis=1
    )
    faces = swap(jnp.broadcast_to(faces[None], (8,) + faces.shape), INNER).reshape(16, HALO, 256)
    links = faces[:, 128, :8].astype(jnp.int32).reshape(128)
    halo = swap(route(links, inner.reshape(1), faces), OUTER).reshape(8, 2, HALO, 256)
    halo, conv_weight = lax.optimization_barrier((halo, conv_weight))
    taps = conv_weight.reshape(9, 256, 256)
    tokens, packed, cots = stem(
        halo, taps, cotangent, features, patch_weight, query_weight, key_weight, value_weight
    )
    packed = swap(packed)
    packed, cots = lax.optimization_barrier((packed, cots))
    cots = swap(cots).reshape(512, DM)
    parts = swap(attend(packed), KEY_GROUPS)
    att, grad = merge(parts, cots)
    terms = swap(grad.reshape(16, SHARE, 128), HEAD_GROUPS)
    received = swap(share_out(terms, att))
    return finish(received, tokens, output_weight)


def solution(mesh):
    in_specs = (
        P(("slide", "tile"), None, None, None),
        P(("slide", "tile"), None),
        P(),
        P(),
        P(),
        P(),
        P(),
        P(),
        P(("slide", "tile"), None),
    )
    out_specs = (P(("slide", "tile"), None), P("slide", None))
    return jax.shard_map(local, mesh=mesh, in_specs=in_specs, out_specs=out_specs, check_vma=False)
```

```python
import jax
import jax.numpy as jnp
from jax import lax
from jax.experimental import pallas as pl
from jax.experimental.pallas import tpu as pltpu
from jax.sharding import PartitionSpec as P

PATCH = 4
HEADS = 12
HD = 64
DM = 768
SPLIT = 4
HG = HEADS // SPLIT
GW = HG * HD
BLK = 32
CHUNK = 96
OW = 256
HALO = 136
BF = jnp.bfloat16
F32 = jnp.float32


def hi_bit(coord):
    return coord >> 1


def lo_bit(coord):
    return (coord ^ (coord >> 1)) & 1


def split_device(dev):
    z, y, x = dev >> 4, (dev >> 2) & 3, dev & 3
    outer = hi_bit(z) * 4 + hi_bit(y) * 2 + hi_bit(x)
    inner = lo_bit(z) * 4 + lo_bit(y) * 2 + lo_bit(x)
    return outer, inner


def device_groups():
    place = {}
    for dev in range(64):
        place[split_device(dev)] = dev
    inner_groups = [[place[(a, b)] for b in range(8)] for a in range(8)]
    outer_groups = [[place[(a, b)] for a in range(8)] for b in range(8)]
    return inner_groups, outer_groups


INNER, OUTER = device_groups()


def place(h, a, b):
    def coord(hi, lo):
        return hi * 2 + (hi ^ lo)

    return coord(a >> 1, b >> 1) * 16 + coord(a & 1, b & 1) * 4 + h


KEY_GROUPS = [[place(h, a, b) for b in range(SPLIT)] for h in range(SPLIT) for a in range(SPLIT)]
HEAD_GROUPS = [[place(h, a, b) for a in range(SPLIT) for b in range(SPLIT)] for h in range(SPLIT)]


def swap(x, groups=None):
    return lax.all_to_all(
        x, "tile", split_axis=0, concat_axis=0, tiled=True, axis_index_groups=groups
    )


def faces_kernel(links_ref, features_hbm, out_hbm, sides_ref, cols_ref, faces_ref, sems):
    loads = []
    for t in range(2):
        for n, y in enumerate((0, 31)):
            loads.append((features_hbm.at[t, y], faces_ref.at[t, n * 32 : n * 32 + 32]))
        for n, x in enumerate((0, 24)):
            loads.append((features_hbm.at[t, :, x : x + 8], sides_ref.at[t, n]))
    loads = [pltpu.make_async_copy(src, dst, sems.at[n]) for n, (src, dst) in enumerate(loads)]
    for load in loads:
        load.start()
    lanes = lax.broadcasted_iota(jnp.int32, (8, 128), 1)
    for t in range(2):
        row = jnp.zeros((8, 128), F32)
        for d in range(8):
            row = jnp.where(lanes == d, links_ref[t, d].astype(F32), row)
        faces_ref[t, 128:HALO, :128] = row.astype(BF)
        faces_ref[t, 128:HALO, 128:] = jnp.zeros((8, 128), BF)
    for load in loads:
        load.wait()
    for t in range(2):
        for n, x in enumerate((0, 7)):
            for lt in range(2):
                cols_ref[...] = sides_ref[t, n, :, :, lt * 128 : lt * 128 + 128].astype(F32).reshape(256, 128)
                faces_ref[t, 64 + n * 32 : 96 + n * 32, lt * 128 : lt * 128 + 128] = cols_ref[
                    pl.ds(x, 32, stride=8), :
                ].astype(BF)
    stores = [pltpu.make_async_copy(faces_ref, out_hbm.at[n], sems.at[n]) for n in range(8)]
    for store in stores:
        store.start()
    for store in stores:
        store.wait()


def gather_faces(links, features):
    hbm = pl.BlockSpec(memory_space=pl.ANY)
    return pl.pallas_call(
        faces_kernel,
        in_specs=[pl.BlockSpec(memory_space=pltpu.SMEM), hbm],
        out_specs=hbm,
        out_shape=jax.ShapeDtypeStruct((8, 2, HALO, 256), BF),
        scratch_shapes=[
            pltpu.VMEM((2, 2, 32, 8, 256), BF),
            pltpu.VMEM((256, 128), F32),
            pltpu.VMEM((2, HALO, 256), BF),
            pltpu.SemaphoreType.DMA((8,)),
        ],
        name="faces",
    )(links, features)


EDGES = {1: (0, 32), 6: (32, 0), 3: (64, 96), 4: (96, 64)}
CORNERS = {0: (0, 3), 2: (31, 2), 5: (32, 1), 7: (63, 0)}


def route_kernel(targets_ref, faces_ref, out_ref):
    out_ref[...] = jnp.zeros(out_ref.shape, BF)
    row_ids = lax.broadcasted_iota(jnp.int32, (8, 256), 0)

    def per_tile(src, carry):
        for direction in range(8):
            target = targets_ref[src, direction]

            @pl.when(target >= 0)
            def _():
                if direction in EDGES:
                    first, dest = EDGES[direction]
                    out_ref[target, dest : dest + 32, :] = faces_ref[src, first : first + 32, :]
                else:
                    row, dest = CORNERS[direction]
                    base = row // 8 * 8
                    cell = faces_ref[src, base : base + 8, :].astype(F32)[row - base : row - base + 1, :]
                    old = out_ref[target, 128:HALO, :].astype(F32)
                    new = jnp.where(row_ids == dest, jnp.broadcast_to(cell, (8, 256)), old)
                    out_ref[target, 128:HALO, :] = new.astype(BF)

        return carry

    lax.fori_loop(0, 16, per_tile, 0)


def route(targets, faces):
    vmem = pl.BlockSpec(memory_space=pltpu.VMEM)
    return pl.pallas_call(
        route_kernel,
        in_specs=[pl.BlockSpec(memory_space=pltpu.SMEM), vmem],
        out_specs=vmem,
        out_shape=jax.ShapeDtypeStruct((16, HALO, 256), BF),
        name="route",
    )(targets, faces)


def attend_heads(units):
    scores = [
        lax.dot_general(q * BF(HD ** -0.5), k, (((1,), (1,)), ((), ())), preferred_element_type=F32)
        for q, k, _ in units
    ]
    results = []
    for score, (_, _, value) in zip(scores, units):
        top = jnp.max(score, axis=1, keepdims=True)
        weights = jnp.exp(score - top).astype(BF)
        res = jnp.dot(weights, value, preferred_element_type=F32)
        total = res[:, HD : HD + 1]
        lse = top + jnp.log(total)
        one = lse.astype(BF).astype(F32)
        two = (lse - one).astype(BF).astype(F32)
        results.append((res[:, :HD] / total, (one, two, lse - one - two)))
    return results


def put_rows(row_ref, out_ref, lanes):
    for n in range(row_ref.shape[0] // BLK):
        for b in range(SPLIT):
            first = n * BLK + b * 8
            out_ref[b, n * 8 : n * 8 + 8, :] = row_ref[first : first + 8, lanes].astype(BF)


def pair_kernel(in_ref, all_ref, out_ref, key_ref, val_ref, row_ref):
    @pl.when(pl.program_id(0) == 0)
    def _():
        ones = jnp.where(lax.broadcasted_iota(jnp.int32, (2048, HD), 1) == 0, 1.0, 0.0).astype(BF)
        for g in range(2):
            key_ref[g] = all_ref[:, 32:64, g * HD : (g + 1) * HD].reshape(2048, HD)
            val_ref[g, :, :HD] = all_ref[:, 64:96, g * HD : (g + 1) * HD].reshape(2048, HD)
            val_ref[g, :, HD:] = ones

    half = 8
    units = []
    for first in range(0, in_ref.shape[0], half):
        for g in range(2):
            query = in_ref[first : first + half, :BLK, g * HD : (g + 1) * HD].reshape(half * BLK, HD)
            units.append((query, key_ref[g], val_ref[g]))
    results = attend_heads(units)
    lanes = lax.broadcasted_iota(jnp.int32, (half * BLK, 128), 1)
    for n in range(len(units) // 2):
        rows = slice(n * half * BLK, (n + 1) * half * BLK)
        tail = jnp.zeros((half * BLK, 128), F32)
        for g in range(2):
            out, parts = results[2 * n + g]
            row_ref[rows, g * HD : (g + 1) * HD] = out
            for i, part in enumerate(parts):
                tail = jnp.where(lanes == HD + 3 * g + i, part, tail)
        row_ref[rows, 128:] = tail
    put_rows(row_ref, out_ref, slice(0, OW))


def single_kernel(in_ref, all_ref, part_ref, out_ref, key_ref, val_ref, row_ref):
    @pl.when(pl.program_id(0) == 0)
    def _():
        ones = jnp.where(lax.broadcasted_iota(jnp.int32, (2048, HD), 1) == 0, 1.0, 0.0).astype(BF)
        val_ref[:, HD:] = ones
        for g in range(2):
            rows = slice(g * 1024, (g + 1) * 1024)
            key_ref[rows, :] = all_ref[:, g * 16 : g * 16 + 16, HD:].reshape(1024, HD)
            val_ref[rows, :HD] = all_ref[:, 32:48, g * HD : (g + 1) * HD].reshape(1024, HD)

    half = 8
    units = []
    for first in range(0, in_ref.shape[0], half):
        query = in_ref[first : first + half, :BLK, :HD].reshape(half * BLK, HD)
        units.append((query, key_ref[...], val_ref[...]))
    results = attend_heads(units)
    lanes = lax.broadcasted_iota(jnp.int32, (half * BLK, 128), 1)
    for n, (out, parts) in enumerate(results):
        rows = slice(n * half * BLK, (n + 1) * half * BLK)
        tail = jnp.zeros((half * BLK, 128), F32)
        for i, part in enumerate(parts):
            tail = jnp.where(lanes == HD + 6 + i, part, tail)
        row_ref[rows, :] = tail
        row_ref[rows, :HD] = out
    for n in range(row_ref.shape[0] // BLK):
        for b in range(SPLIT):
            first = n * BLK + b * 8
            old = part_ref[b, n * 8 : n * 8 + 8, 128:].astype(F32)
            out_ref[b, n * 8 : n * 8 + 8, :128] = part_ref[b, n * 8 : n * 8 + 8, :128]
            out_ref[b, n * 8 : n * 8 + 8, 128:] = (old + row_ref[first : first + 8, :]).astype(BF)


def attend_pair(packed):
    srcs = 16
    return pl.pallas_call(
        pair_kernel,
        grid=(64 // srcs,),
        in_specs=[
            pl.BlockSpec((srcs, CHUNK, 128), lambda i: (i, 0, 0)),
            pl.BlockSpec((64, CHUNK, 128), lambda i: (0, 0, 0)),
        ],
        out_specs=pl.BlockSpec((SPLIT, srcs * 8, OW), lambda i: (0, i, 0)),
        out_shape=jax.ShapeDtypeStruct((SPLIT, 512, OW), BF),
        scratch_shapes=[
            pltpu.VMEM((2, 2048, HD), BF),
            pltpu.VMEM((2, 2048, 2 * HD), BF),
            pltpu.VMEM((srcs * BLK, OW), F32),
        ],
        compiler_params=pltpu.CompilerParams(vmem_limit_bytes=48 << 20),
        name="attend_pair",
    )(packed, packed)


def attend_single(rest, parts):
    srcs = 16
    block = pl.BlockSpec((SPLIT, srcs * 8, OW), lambda i: (0, i, 0))
    return pl.pallas_call(
        single_kernel,
        grid=(64 // srcs,),
        in_specs=[
            pl.BlockSpec((srcs, CHUNK, 128), lambda i: (i, 0, 0)),
            pl.BlockSpec((64, CHUNK, 128), lambda i: (0, 0, 0)),
            block,
        ],
        out_specs=block,
        out_shape=jax.ShapeDtypeStruct((SPLIT, 512, OW), BF),
        scratch_shapes=[
            pltpu.VMEM((2048, HD), BF),
            pltpu.VMEM((2048, 2 * HD), BF),
            pltpu.VMEM((srcs * BLK, 128), F32),
        ],
        compiler_params=pltpu.CompilerParams(vmem_limit_bytes=48 << 20),
        name="attend_single",
    )(rest, rest, parts)


SHARE = 72
ROWS = SHARE + 16


def merge_kernel(parts_ref, rest_ref, att_ref, grad_ref, pair_ref, single_ref, cot_ref):
    for c in range(DM // 128):
        cot_ref[:, c * 128 : (c + 1) * 128] = rest_ref[:, 48 + 8 * c : 56 + 8 * c, :].reshape(512, 128)
    tails = []
    for b in range(SPLIT):
        tail = parts_ref[b, :, 128:].astype(F32)
        tails.append(tail + pltpu.roll(tail, 127, 1) + pltpu.roll(tail, 126, 1))
    top = jnp.maximum(jnp.maximum(tails[0], tails[1]), jnp.maximum(tails[2], tails[3]))
    ws = [jnp.exp(tail - top) for tail in tails]
    total = ws[0] + ws[1] + ws[2] + ws[3]
    low = lax.broadcasted_iota(jnp.int32, (512, 128), 1) < HD
    pair = jnp.zeros((512, 128), F32)
    single = jnp.zeros((512, 128), F32)
    for b in range(SPLIT):
        share = ws[b] / total
        w0, w1, w2 = (share[:, HD + 3 * g : HD + 3 * g + 1] for g in range(HG))
        pair = pair + jnp.where(low, w0, w1) * parts_ref[b, :, :128].astype(F32)
        single = single + w2 * parts_ref[b, :, 128:].astype(F32)
    single = jnp.where(low, single, 0.0)
    pair_ref[...] = pair.astype(BF)
    single_ref[...] = single.astype(BF)
    for n in range(64):
        att_ref[n, :8, :] = pair[n * 8 : n * 8 + 8].astype(BF)
        att_ref[n, 8:, :] = single[n * 8 : n * 8 + 8].astype(BF)
    for first, ref, count in ((0, pair_ref, 128), (128, single_ref, 64)):
        grad = lax.dot_general(
            ref[...], cot_ref[...], (((0,), (0,)), ((), ())), preferred_element_type=F32
        )
        for c in range(DM // 128):
            grad_ref[c, first : first + count, :] = grad[:count, c * 128 : (c + 1) * 128].astype(BF)


def merge(parts, rest):
    return pl.pallas_call(
        merge_kernel,
        out_shape=(
            jax.ShapeDtypeStruct((64, 16, 128), BF),
            jax.ShapeDtypeStruct((DM // 128, GW, 128), BF),
        ),
        scratch_shapes=[pltpu.VMEM((512, 128), BF), pltpu.VMEM((512, 128), BF), pltpu.VMEM((512, DM), BF)],
        name="merge",
    )(parts, rest)


def share_kernel(terms_ref, att_ref, out_ref):
    total = terms_ref[0].astype(F32)
    for n in range(1, 16):
        total = total + terms_ref[n].astype(F32)
    total = total.astype(BF)
    for n in range(64):
        out_ref[n, :SHARE, :] = total
        out_ref[n, SHARE:, :] = att_ref[n]


def share_out(terms, att):
    return pl.pallas_call(
        share_kernel, out_shape=jax.ShapeDtypeStruct((64, ROWS, 128), BF), name="share"
    )(terms, att)


def finish_kernel(all_ref, tokens_ref, weight_ref, mixed_ref, grad_ref, att_ref):
    lanes = lax.broadcasted_iota(jnp.int32, (8, 128), 1) < HD
    for a in range(SPLIT):
        for b in range(SPLIT):
            row = a * BLK + b * 8
            for h in range(SPLIT):
                att_ref[row : row + 8, h * 128 : (h + 1) * 128] = all_ref[place(h, a, b), SHARE : SHARE + 8, :]
            for h in range(0, SPLIT, 2):
                even = all_ref[place(h, a, b), SHARE + 8 :, :].astype(F32)
                odd = pltpu.roll(all_ref[place(h + 1, a, b), SHARE + 8 :, :].astype(F32), HD, 1)
                first = 512 + h * HD
                att_ref[row : row + 8, first : first + 128] = jnp.where(lanes, even, odd).astype(BF)
    for h in range(SPLIT):
        for m in range(16):
            at = place(h, m // SPLIT, m % SPLIT)
            done = 0
            while done < SHARE:
                block, row = divmod(m * SHARE + done, GW)
                count = min(SHARE - done, (128 if row < 128 else GW) - row)
                dest = h * 128 + row if row < 128 else 512 + h * HD + row - 128
                grad_ref[dest : dest + count, block * 128 : (block + 1) * 128] = all_ref[
                    at, done : done + count, :
                ].astype(F32)
                done += count
    mixed_ref[...] = (
        tokens_ref[...].astype(F32) + jnp.dot(att_ref[...], weight_ref[...], preferred_element_type=F32)
    ).astype(BF)


def finish(received, tokens, weight):
    return pl.pallas_call(
        finish_kernel,
        out_shape=(
            jax.ShapeDtypeStruct((128, DM), BF),
            jax.ShapeDtypeStruct((DM, DM), F32),
        ),
        scratch_shapes=[pltpu.VMEM((128, DM), BF)],
        name="finish",
    )(received, tokens, weight)


ZW = 48
Z0 = 8


def stem_kernel(
    halo_ref,
    conv_ref,
    cot_ref,
    features_hbm,
    patch_hbm,
    query_hbm,
    key_hbm,
    value_hbm,
    tokens_ref,
    packed_ref,
    rest_ref,
    maps_ref,
    side_ref,
    left_ref,
    mid_ref,
    right_ref,
    hid_ref,
    patch_ref,
    wq_ref,
    wk_ref,
    wv_ref,
    sems,
):
    loads = [pltpu.make_async_copy(features_hbm.at[t], maps_ref.at[t, 1:33], sems.at[t]) for t in range(2)]
    pairs = ((patch_hbm, patch_ref), (query_hbm, wq_ref), (key_hbm, wk_ref), (value_hbm, wv_ref))
    loads += [pltpu.make_async_copy(src, dst, sems.at[2 + n]) for n, (src, dst) in enumerate(pairs)]
    for load in loads:
        load.start()
    zrefs = (left_ref, mid_ref, right_ref)

    def halo_rows(t, first, count):
        total = halo_ref[0, t, first : first + count, :].astype(F32)
        for n in range(1, 8):
            total = total + halo_ref[n, t, first : first + count, :].astype(F32)
        return total

    for t in range(2):
        maps_ref[t, 0] = halo_rows(t, 0, 32).astype(BF)
        maps_ref[t, 33] = halo_rows(t, 32, 32).astype(BF)
        corner = halo_rows(t, 128, 8)
        for side in range(2):
            side_ref[side, t, Z0 : Z0 + 32, :] = halo_rows(t, 64 + 32 * side, 32)
            side_ref[side, t, Z0 - 1 : Z0, :] = corner[side : side + 1]
            side_ref[side, t, Z0 + 32 : Z0 + 33, :] = corner[2 + side : 3 + side]
    for t in range(2):
        for side in range(2):
            edge = jnp.zeros((32, 256), F32)
            for dy in range(3):
                part = side_ref[side, t, Z0 - 1 + dy : Z0 + 31 + dy, :].astype(BF)
                edge = edge + jnp.dot(part, conv_ref[dy * 3 + side * 2], preferred_element_type=F32)
            dest, first = ((left_ref, Z0 - 1), (right_ref, Z0 + 32))[side]
            for lt in range(2):
                dest[lt, pl.ds(t * 32 * ZW + first, 32, stride=ZW), :] = edge[:, lt * 128 : lt * 128 + 128]
    for t in range(2):
        loads[t].wait()
        for y in range(0, 32, 8):
            for dx in range(3):
                acc = jnp.zeros((256, 256), F32)
                for dy in range(3):
                    rows = maps_ref[t, y + dy : y + dy + 8].reshape(256, 256)
                    acc = acc + jnp.dot(rows, conv_ref[dy * 3 + dx], preferred_element_type=F32)
                for n in range(8):
                    first = (t * 32 + y + n) * ZW + Z0
                    for lt in range(2):
                        zrefs[dx][lt, first : first + 32, :] = acc[n * 32 : n * 32 + 32, lt * 128 : lt * 128 + 128]

    for r in range(4):
        for c in range(4):
            for t in range(2):
                for pr in range(8):
                    first = (t * 32 + pr * 4 + r) * ZW + Z0 + c
                    row = (t * 8 + pr) * 8
                    for lt in range(2):
                        total = (
                            mid_ref[lt, pl.ds(first, 8, stride=4), :]
                            + left_ref[lt, pl.ds(first - 1, 8, stride=4), :]
                            + right_ref[lt, pl.ds(first + 1, 8, stride=4), :]
                        )
                        col = (r * 4 + c) * 256 + lt * 128
                        hid_ref[row : row + 8, col : col + 128] = jax.nn.gelu(total).astype(BF)
    loads[2].wait()
    tokens = jnp.dot(hid_ref[...], patch_ref[...], preferred_element_type=F32).astype(BF)
    tokens_ref[...] = tokens
    for load in loads[3:]:
        load.wait()
    query = jnp.dot(tokens, wq_ref[...], preferred_element_type=F32)
    keys = jnp.dot(tokens, wk_ref[...], preferred_element_type=F32)
    values = jnp.dot(tokens, wv_ref[...], preferred_element_type=F32)
    low = lax.broadcasted_iota(jnp.int32, (128, 128), 1) < HD

    def pair_of(x, h):
        return x[:, h * 128 : (h + 1) * 128]

    for h in range(SPLIT):
        one = 4 + h // 2
        q1, k1, v1 = pair_of(query, one), pair_of(keys, one), pair_of(values, one)
        if h % 2 == 0:
            k1 = pltpu.roll(k1, HD, 1)
            v2 = pltpu.roll(v1, HD, 1)
        else:
            q1 = pltpu.roll(q1, HD, 1)
            v2 = v1
            v1 = pltpu.roll(v1, HD, 1)
        pieces = (pair_of(query, h).astype(BF), pair_of(keys, h).astype(BF), pair_of(values, h).astype(BF))
        for a in range(SPLIT):
            for b in range(SPLIT):
                at = place(h, a, b)
                qa, kb = slice(a * BLK, (a + 1) * BLK), slice(b * BLK, (b + 1) * BLK)
                packed_ref[at, 0:32, :] = pieces[0][qa]
                packed_ref[at, 32:64, :] = pieces[1][kb]
                packed_ref[at, 64:96, :] = pieces[2][kb]
                rest_ref[at, 0:32, :] = jnp.where(low[:BLK], q1[qa], k1[kb]).astype(BF)
                half = b * BLK + BLK // 2
                rest_ref[at, 32:48, :] = jnp.where(
                    low[: BLK // 2], v1[b * BLK : half], v2[half : (b + 1) * BLK]
                ).astype(BF)
                row = a * BLK + b * 8
                for c in range(DM // 128):
                    rest_ref[at, 48 + 8 * c : 56 + 8 * c, :] = cot_ref[row : row + 8, c * 128 : (c + 1) * 128]


def stem(halo, conv_weight, cotangent, features, patch_weight, query_weight, key_weight, value_weight):
    hbm = pl.BlockSpec(memory_space=pl.ANY)
    vmem = pl.BlockSpec(memory_space=pltpu.VMEM)
    return pl.pallas_call(
        stem_kernel,
        in_specs=[vmem, vmem, vmem] + [hbm] * 5,
        out_specs=(vmem, vmem, vmem),
        out_shape=(
            jax.ShapeDtypeStruct((128, DM), BF),
            jax.ShapeDtypeStruct((64, CHUNK, 128), BF),
            jax.ShapeDtypeStruct((64, CHUNK, 128), BF),
        ),
        scratch_shapes=[
            pltpu.VMEM((2, 34, 32, 256), BF),
            pltpu.VMEM((2, 2, ZW, 256), F32),
            pltpu.VMEM((2, 64 * ZW, 128), F32),
            pltpu.VMEM((2, 64 * ZW, 128), F32),
            pltpu.VMEM((2, 64 * ZW, 128), F32),
            pltpu.VMEM((128, 4096), BF),
            pltpu.VMEM((4096, DM), BF),
            pltpu.VMEM((DM, DM), BF),
            pltpu.VMEM((DM, DM), BF),
            pltpu.VMEM((DM, DM), BF),
            pltpu.SemaphoreType.DMA((6,)),
        ],
        compiler_params=pltpu.CompilerParams(vmem_limit_bytes=48 << 20),
        name="stem",
    )(halo, conv_weight, cotangent, features, patch_weight, query_weight, key_weight, value_weight)


def local(
    features,
    neighbours,
    conv_weight,
    patch_weight,
    query_weight,
    key_weight,
    value_weight,
    output_weight,
    cotangent,
):
    _, inner = split_device(lax.axis_index("tile"))
    faces = swap(gather_faces(neighbours, features), INNER).reshape(16, HALO, 256)
    tiles = faces[:, 128, :8].astype(jnp.int32)
    outer, goal = split_device(tiles >> 1)
    targets = jnp.where((tiles < 128) & (goal == inner), (outer & 7) * 2 + (tiles & 1), -1)
    halo = swap(route(targets, faces), OUTER).reshape(8, 2, HALO, 256)
    halo, conv_weight = lax.optimization_barrier((halo, conv_weight))
    taps = conv_weight.reshape(9, 256, 256)
    tokens, packed, rest = stem(
        halo, taps, cotangent, features, patch_weight, query_weight, key_weight, value_weight
    )
    packed = swap(packed)
    packed, rest = lax.optimization_barrier((packed, rest))
    rest = swap(rest)
    parts = swap(attend_single(rest, attend_pair(packed)), KEY_GROUPS)
    att, grad = merge(parts, rest)
    terms = swap(grad.reshape(16, SHARE, 128), HEAD_GROUPS)
    received = swap(share_out(terms, att))
    return finish(received, tokens, output_weight)


def solution(mesh):
    in_specs = (
        P(("slide", "tile"), None, None, None),
        P(("slide", "tile"), None),
        P(),
        P(),
        P(),
        P(),
        P(),
        P(),
        P(("slide", "tile"), None),
    )
    out_specs = (P(("slide", "tile"), None), P("slide", None))
    return jax.shard_map(local, mesh=mesh, in_specs=in_specs, out_specs=out_specs, check_vma=False)
```

```python
import jax
import jax.numpy as jnp
from jax import lax
from jax.experimental import pallas as pl
from jax.experimental.pallas import tpu as pltpu
from jax.sharding import PartitionSpec as P

PATCH = 4
HEADS = 12
HD = 64
DM = 768
SPLIT = 4
HG = HEADS // SPLIT
GW = HG * HD
BLK = 32
CHUNK = 96
OW = 256
HALO = 136
BF = jnp.bfloat16
F32 = jnp.float32


def hi_bit(coord):
    return coord >> 1


def lo_bit(coord):
    return (coord ^ (coord >> 1)) & 1


def split_device(dev):
    z, y, x = dev >> 4, (dev >> 2) & 3, dev & 3
    outer = hi_bit(z) * 4 + hi_bit(y) * 2 + hi_bit(x)
    inner = lo_bit(z) * 4 + lo_bit(y) * 2 + lo_bit(x)
    return outer, inner


def device_groups():
    place = {}
    for dev in range(64):
        place[split_device(dev)] = dev
    inner_groups = [[place[(a, b)] for b in range(8)] for a in range(8)]
    outer_groups = [[place[(a, b)] for a in range(8)] for b in range(8)]
    return inner_groups, outer_groups


INNER, OUTER = device_groups()


def place(h, a, b):
    def coord(hi, lo):
        return hi * 2 + (hi ^ lo)

    return coord(a >> 1, b >> 1) * 16 + coord(a & 1, b & 1) * 4 + h


KEY_GROUPS = [[place(h, a, b) for b in range(SPLIT)] for h in range(SPLIT) for a in range(SPLIT)]
HEAD_GROUPS = [[place(h, a, b) for a in range(SPLIT) for b in range(SPLIT)] for h in range(SPLIT)]


def swap(x, groups=None):
    return lax.all_to_all(
        x, "tile", split_axis=0, concat_axis=0, tiled=True, axis_index_groups=groups
    )


def faces_kernel(links_ref, features_hbm, out_hbm, sides_ref, cols_ref, faces_ref, sems):
    loads = []
    for t in range(2):
        for n, y in enumerate((0, 31)):
            loads.append((features_hbm.at[t, y], faces_ref.at[t, n * 32 : n * 32 + 32]))
        for n, x in enumerate((0, 24)):
            loads.append((features_hbm.at[t, :, x : x + 8], sides_ref.at[t, n]))
    loads = [pltpu.make_async_copy(src, dst, sems.at[n]) for n, (src, dst) in enumerate(loads)]
    for load in loads:
        load.start()
    lanes = lax.broadcasted_iota(jnp.int32, (8, 128), 1)
    for t in range(2):
        row = jnp.zeros((8, 128), F32)
        for d in range(8):
            row = jnp.where(lanes == d, links_ref[t, d].astype(F32), row)
        faces_ref[t, 128:HALO, :128] = row.astype(BF)
        faces_ref[t, 128:HALO, 128:] = jnp.zeros((8, 128), BF)
    for load in loads:
        load.wait()
    for t in range(2):
        for n, x in enumerate((0, 7)):
            for lt in range(2):
                cols_ref[...] = sides_ref[t, n, :, :, lt * 128 : lt * 128 + 128].astype(F32).reshape(256, 128)
                faces_ref[t, 64 + n * 32 : 96 + n * 32, lt * 128 : lt * 128 + 128] = cols_ref[
                    pl.ds(x, 32, stride=8), :
                ].astype(BF)
    stores = [pltpu.make_async_copy(faces_ref, out_hbm.at[n], sems.at[n]) for n in range(8)]
    for store in stores:
        store.start()
    for store in stores:
        store.wait()


def gather_faces(links, features):
    hbm = pl.BlockSpec(memory_space=pltpu.HBM)
    return pl.pallas_call(
        faces_kernel,
        in_specs=[pl.BlockSpec(memory_space=pltpu.SMEM), hbm],
        out_specs=hbm,
        out_shape=jax.ShapeDtypeStruct((8, 2, HALO, 256), BF),
        scratch_shapes=[
            pltpu.VMEM((2, 2, 32, 8, 256), BF),
            pltpu.VMEM((256, 128), F32),
            pltpu.VMEM((2, HALO, 256), BF),
            pltpu.SemaphoreType.DMA((8,)),
        ],
        compiler_params=pltpu.CompilerParams(vmem_limit_bytes=6 << 20),
        name="faces",
    )(links, features)


EDGES = {1: (0, 32), 6: (32, 0), 3: (64, 96), 4: (96, 64)}
CORNERS = {0: (0, 3), 2: (31, 2), 5: (32, 1), 7: (63, 0)}


def route_kernel(targets_ref, faces_ref, out_ref):
    out_ref[...] = jnp.zeros(out_ref.shape, BF)
    row_ids = lax.broadcasted_iota(jnp.int32, (8, 256), 0)

    def per_tile(src, carry):
        for direction in range(8):
            target = targets_ref[src, direction]

            @pl.when(target >= 0)
            def _():
                if direction in EDGES:
                    first, dest = EDGES[direction]
                    out_ref[target, dest : dest + 32, :] = faces_ref[src, first : first + 32, :]
                else:
                    row, dest = CORNERS[direction]
                    base = row // 8 * 8
                    cell = faces_ref[src, base : base + 8, :].astype(F32)[row - base : row - base + 1, :]
                    old = out_ref[target, 128:HALO, :].astype(F32)
                    new = jnp.where(row_ids == dest, jnp.broadcast_to(cell, (8, 256)), old)
                    out_ref[target, 128:HALO, :] = new.astype(BF)

        return carry

    lax.fori_loop(0, 16, per_tile, 0)


def route(targets, faces):
    vmem = pl.BlockSpec(memory_space=pltpu.VMEM)
    return pl.pallas_call(
        route_kernel,
        in_specs=[pl.BlockSpec(memory_space=pltpu.SMEM), vmem],
        out_specs=vmem,
        out_shape=jax.ShapeDtypeStruct((16, HALO, 256), BF),
        compiler_params=pltpu.CompilerParams(vmem_limit_bytes=8 << 20),
        name="route",
    )(targets, faces)


def attend_heads(units):
    scores = [
        lax.dot_general(q * BF(HD ** -0.5), k, (((1,), (1,)), ((), ())), preferred_element_type=F32)
        for q, k, _ in units
    ]
    results = []
    for score, (_, _, value) in zip(scores, units):
        top = jnp.max(score, axis=1, keepdims=True)
        weights = jnp.exp(score - top).astype(BF)
        res = jnp.dot(weights, value, preferred_element_type=F32)
        total = res[:, HD : HD + 1]
        lse = top + jnp.log(total)
        one = lse.astype(BF).astype(F32)
        two = (lse - one).astype(BF).astype(F32)
        results.append((res[:, :HD] / total, (one, two, lse - one - two)))
    return results


def put_rows(row_ref, out_ref, lanes):
    for n in range(row_ref.shape[0] // BLK):
        for b in range(SPLIT):
            first = n * BLK + b * 8
            out_ref[b, n * 8 : n * 8 + 8, :] = row_ref[first : first + 8, lanes].astype(BF)


def pair_kernel(in_ref, all_ref, out_ref, key_ref, val_ref, row_ref):
    @pl.when(pl.program_id(0) == 0)
    def _():
        ones = jnp.where(lax.broadcasted_iota(jnp.int32, (2048, HD), 1) == 0, 1.0, 0.0).astype(BF)
        for g in range(2):
            key_ref[g] = all_ref[:, 32:64, g * HD : (g + 1) * HD].reshape(2048, HD)
            val_ref[g, :, :HD] = all_ref[:, 64:96, g * HD : (g + 1) * HD].reshape(2048, HD)
            val_ref[g, :, HD:] = ones

    half = 8
    units = []
    for first in range(0, in_ref.shape[0], half):
        for g in range(2):
            query = in_ref[first : first + half, :BLK, g * HD : (g + 1) * HD].reshape(half * BLK, HD)
            units.append((query, key_ref[g], val_ref[g]))
    results = attend_heads(units)
    lanes = lax.broadcasted_iota(jnp.int32, (half * BLK, 128), 1)
    for n in range(len(units) // 2):
        rows = slice(n * half * BLK, (n + 1) * half * BLK)
        tail = jnp.zeros((half * BLK, 128), F32)
        for g in range(2):
            out, parts = results[2 * n + g]
            row_ref[rows, g * HD : (g + 1) * HD] = out
            for i, part in enumerate(parts):
                tail = jnp.where(lanes == HD + 3 * g + i, part, tail)
        row_ref[rows, 128:] = tail
    put_rows(row_ref, out_ref, slice(0, OW))


def single_kernel(in_ref, all_ref, part_ref, out_ref, key_ref, val_ref, row_ref):
    @pl.when(pl.program_id(0) == 0)
    def _():
        ones = jnp.where(lax.broadcasted_iota(jnp.int32, (2048, HD), 1) == 0, 1.0, 0.0).astype(BF)
        val_ref[:, HD:] = ones
        for g in range(2):
            rows = slice(g * 1024, (g + 1) * 1024)
            key_ref[rows, :] = all_ref[:, g * 16 : g * 16 + 16, HD:].reshape(1024, HD)
            val_ref[rows, :HD] = all_ref[:, 32:48, g * HD : (g + 1) * HD].reshape(1024, HD)

    half = 8
    units = []
    for first in range(0, in_ref.shape[0], half):
        query = in_ref[first : first + half, :BLK, :HD].reshape(half * BLK, HD)
        units.append((query, key_ref[...], val_ref[...]))
    results = attend_heads(units)
    lanes = lax.broadcasted_iota(jnp.int32, (half * BLK, 128), 1)
    for n, (out, parts) in enumerate(results):
        rows = slice(n * half * BLK, (n + 1) * half * BLK)
        tail = jnp.zeros((half * BLK, 128), F32)
        for i, part in enumerate(parts):
            tail = jnp.where(lanes == HD + 6 + i, part, tail)
        row_ref[rows, :] = tail
        row_ref[rows, :HD] = out
    for n in range(row_ref.shape[0] // BLK):
        for b in range(SPLIT):
            first = n * BLK + b * 8
            old = part_ref[b, n * 8 : n * 8 + 8, 128:].astype(F32)
            out_ref[b, n * 8 : n * 8 + 8, :128] = part_ref[b, n * 8 : n * 8 + 8, :128]
            out_ref[b, n * 8 : n * 8 + 8, 128:] = (old + row_ref[first : first + 8, :]).astype(BF)


def attend_pair(packed):
    srcs = 16
    return pl.pallas_call(
        pair_kernel,
        grid=(64 // srcs,),
        in_specs=[
            pl.BlockSpec((srcs, CHUNK, 128), lambda i: (i, 0, 0)),
            pl.BlockSpec((64, CHUNK, 128), lambda i: (0, 0, 0)),
        ],
        out_specs=pl.BlockSpec((SPLIT, srcs * 8, OW), lambda i: (0, i, 0)),
        out_shape=pltpu.HBM((SPLIT, 512, OW), BF),
        scratch_shapes=[
            pltpu.VMEM((2, 2048, HD), BF),
            pltpu.VMEM((2, 2048, 2 * HD), BF),
            pltpu.VMEM((srcs * BLK, OW), F32),
        ],
        compiler_params=pltpu.CompilerParams(vmem_limit_bytes=28 << 20),
        name="attend_pair",
    )(packed, packed)


def attend_single(rest, parts):
    srcs = 16
    block = pl.BlockSpec((SPLIT, srcs * 8, OW), lambda i: (0, i, 0))
    return pl.pallas_call(
        single_kernel,
        grid=(64 // srcs,),
        in_specs=[
            pl.BlockSpec((srcs, CHUNK, 128), lambda i: (i, 0, 0)),
            pl.BlockSpec((64, CHUNK, 128), lambda i: (0, 0, 0)),
            block,
        ],
        out_specs=block,
        out_shape=jax.ShapeDtypeStruct((SPLIT, 512, OW), BF),
        scratch_shapes=[
            pltpu.VMEM((2048, HD), BF),
            pltpu.VMEM((2048, 2 * HD), BF),
            pltpu.VMEM((srcs * BLK, 128), F32),
        ],
        compiler_params=pltpu.CompilerParams(vmem_limit_bytes=20 << 20),
        name="attend_single",
    )(rest, rest, parts)


SHARE = 72
ROWS = SHARE + 16


def merge_kernel(parts_ref, rest_ref, att_ref, grad_ref, pair_ref, single_ref, cot_ref):
    for c in range(DM // 128):
        cot_ref[:, c * 128 : (c + 1) * 128] = rest_ref[:, 48 + 8 * c : 56 + 8 * c, :].reshape(512, 128)
    tails = []
    for b in range(SPLIT):
        tail = parts_ref[b, :, 128:].astype(F32)
        tails.append(tail + pltpu.roll(tail, 127, 1) + pltpu.roll(tail, 126, 1))
    top = jnp.maximum(jnp.maximum(tails[0], tails[1]), jnp.maximum(tails[2], tails[3]))
    ws = [jnp.exp(tail - top) for tail in tails]
    total = ws[0] + ws[1] + ws[2] + ws[3]
    low = lax.broadcasted_iota(jnp.int32, (512, 128), 1) < HD
    pair = jnp.zeros((512, 128), F32)
    single = jnp.zeros((512, 128), F32)
    inverse = 1.0 / total
    for b in range(SPLIT):
        share = ws[b] * inverse
        w0, w1, w2 = (share[:, HD + 3 * g : HD + 3 * g + 1] for g in range(HG))
        pair = pair + jnp.where(low, w0, w1) * parts_ref[b, :, :128].astype(F32)
        single = single + w2 * parts_ref[b, :, 128:].astype(F32)
    single = jnp.where(low, single, 0.0)
    pair_ref[...] = pair.astype(BF)
    single_ref[...] = single.astype(BF)
    for n in range(64):
        att_ref[n, :8, :] = pair[n * 8 : n * 8 + 8].astype(BF)
        att_ref[n, 8:, :] = single[n * 8 : n * 8 + 8].astype(BF)
    for first, ref, count in ((0, pair_ref, 128), (128, single_ref, 64)):
        grad = lax.dot_general(
            ref[...], cot_ref[...], (((0,), (0,)), ((), ())), preferred_element_type=F32
        )
        for c in range(DM // 128):
            grad_ref[c, first : first + count, :] = grad[:count, c * 128 : (c + 1) * 128].astype(BF)


def merge(parts, rest):
    return pl.pallas_call(
        merge_kernel,
        out_shape=(
            jax.ShapeDtypeStruct((64, 16, 128), BF),
            jax.ShapeDtypeStruct((DM // 128, GW, 128), BF),
        ),
        scratch_shapes=[pltpu.VMEM((512, 128), BF), pltpu.VMEM((512, 128), BF), pltpu.VMEM((512, DM), BF)],
        compiler_params=pltpu.CompilerParams(vmem_limit_bytes=16 << 20),
        name="merge",
    )(parts, rest)


def share_kernel(terms_ref, att_ref, out_ref, total_ref):
    @pl.when(pl.program_id(0) == 0)
    def _():
        total = terms_ref[0].astype(F32)
        for n in range(1, 16):
            total = total + terms_ref[n].astype(F32)
        total_ref[...] = total.astype(BF)

    for n in range(out_ref.shape[0]):
        out_ref[n, :SHARE, :] = total_ref[...]
        out_ref[n, SHARE:, :] = att_ref[n]


def share_out(terms, att):
    step = 16
    return pl.pallas_call(
        share_kernel,
        grid=(64 // step,),
        in_specs=[
            pl.BlockSpec((16, SHARE, 128), lambda i: (0, 0, 0)),
            pl.BlockSpec((step, 16, 128), lambda i: (i, 0, 0)),
        ],
        out_specs=pl.BlockSpec((step, ROWS, 128), lambda i: (i, 0, 0)),
        out_shape=jax.ShapeDtypeStruct((64, ROWS, 128), BF),
        scratch_shapes=[pltpu.VMEM((SHARE, 128), BF)],
        compiler_params=pltpu.CompilerParams(vmem_limit_bytes=8 << 20),
        name="share",
    )(terms, att)


def finish_kernel(all_ref, tokens_ref, weight_ref, mixed_ref, grad_hbm, att_ref, grad_ref, sems):
    for h in range(SPLIT):
        for m in range(16):
            at = place(h, m // SPLIT, m % SPLIT)
            done = 0
            while done < SHARE:
                block, row = divmod(m * SHARE + done, GW)
                count = min(SHARE - done, (128 if row < 128 else GW) - row)
                dest = h * 128 + row if row < 128 else 512 + h * HD + row - 128
                grad_ref[dest : dest + count, block * 128 : (block + 1) * 128] = all_ref[
                    at, done : done + count, :
                ].astype(F32)
                done += count
    copies = [
        pltpu.make_async_copy(grad_ref.at[n * 384 : (n + 1) * 384], grad_hbm.at[n * 384 : (n + 1) * 384], sems.at[n])
        for n in range(2)
    ]
    for copy in copies:
        copy.start()
    lanes = lax.broadcasted_iota(jnp.int32, (8, 128), 1) < HD
    for a in range(SPLIT):
        for b in range(SPLIT):
            row = a * BLK + b * 8
            for h in range(SPLIT):
                att_ref[row : row + 8, h * 128 : (h + 1) * 128] = all_ref[place(h, a, b), SHARE : SHARE + 8, :]
            for h in range(0, SPLIT, 2):
                even = all_ref[place(h, a, b), SHARE + 8 :, :].astype(F32)
                odd = pltpu.roll(all_ref[place(h + 1, a, b), SHARE + 8 :, :].astype(F32), HD, 1)
                first = 512 + h * HD
                att_ref[row : row + 8, first : first + 128] = jnp.where(lanes, even, odd).astype(BF)
    mixed_ref[...] = (
        tokens_ref[...].astype(F32) + jnp.dot(att_ref[...], weight_ref[...], preferred_element_type=F32)
    ).astype(BF)
    for copy in copies:
        copy.wait()


def finish(received, tokens, weight):
    vmem = pl.BlockSpec(memory_space=pltpu.VMEM)
    return pl.pallas_call(
        finish_kernel,
        in_specs=[vmem] * 3,
        out_specs=(vmem, pl.BlockSpec(memory_space=pl.ANY)),
        out_shape=(
            jax.ShapeDtypeStruct((128, DM), BF),
            jax.ShapeDtypeStruct((DM, DM), F32),
        ),
        scratch_shapes=[
            pltpu.VMEM((128, DM), BF),
            pltpu.VMEM((DM, DM), F32),
            pltpu.SemaphoreType.DMA((2,)),
        ],
        compiler_params=pltpu.CompilerParams(vmem_limit_bytes=12 << 20),
        name="finish",
    )(received, tokens, weight)


ZW = 48
Z0 = 8


def stem_kernel(
    halo_ref,
    conv_ref,
    cot_ref,
    features_hbm,
    patch_hbm,
    query_hbm,
    key_hbm,
    value_hbm,
    tokens_ref,
    packed_ref,
    rest_ref,
    maps_ref,
    side_ref,
    left_ref,
    mid_ref,
    right_ref,
    hid_ref,
    patch_ref,
    wq_ref,
    wk_ref,
    wv_ref,
    sems,
):
    loads = [pltpu.make_async_copy(features_hbm.at[t], maps_ref.at[t, 1:33], sems.at[t]) for t in range(2)]
    pairs = ((patch_hbm, patch_ref), (query_hbm, wq_ref), (key_hbm, wk_ref), (value_hbm, wv_ref))
    loads += [pltpu.make_async_copy(src, dst, sems.at[2 + n]) for n, (src, dst) in enumerate(pairs)]
    for load in loads:
        load.start()
    zrefs = (left_ref, mid_ref, right_ref)

    def halo_rows(t, first, count):
        total = halo_ref[0, t, first : first + count, :].astype(F32)
        for n in range(1, 8):
            total = total + halo_ref[n, t, first : first + count, :].astype(F32)
        return total

    for t in range(2):
        maps_ref[t, 0] = halo_rows(t, 0, 32).astype(BF)
        maps_ref[t, 33] = halo_rows(t, 32, 32).astype(BF)
        corner = halo_rows(t, 128, 8)
        for side in range(2):
            side_ref[side, t, Z0 : Z0 + 32, :] = halo_rows(t, 64 + 32 * side, 32)
            side_ref[side, t, Z0 - 1 : Z0, :] = corner[side : side + 1]
            side_ref[side, t, Z0 + 32 : Z0 + 33, :] = corner[2 + side : 3 + side]
    for t in range(2):
        for side in range(2):
            edge = jnp.zeros((32, 256), F32)
            for dy in range(3):
                part = side_ref[side, t, Z0 - 1 + dy : Z0 + 31 + dy, :].astype(BF)
                edge = edge + jnp.dot(part, conv_ref[dy * 3 + side * 2], preferred_element_type=F32)
            dest, first = ((left_ref, Z0 - 1), (right_ref, Z0 + 32))[side]
            for lt in range(2):
                dest[lt, pl.ds(t * 32 * ZW + first, 32, stride=ZW), :] = edge[:, lt * 128 : lt * 128 + 128]
    for t in range(2):
        loads[t].wait()
        for y in range(0, 32, 8):
            for dx in range(3):
                acc = jnp.zeros((256, 256), F32)
                for dy in range(3):
                    rows = maps_ref[t, y + dy : y + dy + 8].reshape(256, 256)
                    acc = acc + jnp.dot(rows, conv_ref[dy * 3 + dx], preferred_element_type=F32)
                for n in range(8):
                    first = (t * 32 + y + n) * ZW + Z0
                    for lt in range(2):
                        zrefs[dx][lt, first : first + 32, :] = acc[n * 32 : n * 32 + 32, lt * 128 : lt * 128 + 128]

    for r in range(4):
        for c in range(4):
            for t in range(2):
                for pr in range(8):
                    first = (t * 32 + pr * 4 + r) * ZW + Z0 + c
                    row = (t * 8 + pr) * 8
                    for lt in range(2):
                        total = (
                            mid_ref[lt, pl.ds(first, 8, stride=4), :]
                            + left_ref[lt, pl.ds(first - 1, 8, stride=4), :]
                            + right_ref[lt, pl.ds(first + 1, 8, stride=4), :]
                        )
                        col = (r * 4 + c) * 256 + lt * 128
                        hid_ref[row : row + 8, col : col + 128] = jax.nn.gelu(total).astype(BF)
    loads[2].wait()
    tokens = jnp.dot(hid_ref[...], patch_ref[...], preferred_element_type=F32).astype(BF)
    tokens_ref[...] = tokens
    for load in loads[3:]:
        load.wait()
    query = jnp.dot(tokens, wq_ref[...], preferred_element_type=F32)
    keys = jnp.dot(tokens, wk_ref[...], preferred_element_type=F32)
    values = jnp.dot(tokens, wv_ref[...], preferred_element_type=F32)
    low = lax.broadcasted_iota(jnp.int32, (128, 128), 1) < HD

    def pair_of(x, h):
        return x[:, h * 128 : (h + 1) * 128]

    for h in range(SPLIT):
        one = 4 + h // 2
        q1, k1, v1 = pair_of(query, one), pair_of(keys, one), pair_of(values, one)
        if h % 2 == 0:
            k1 = pltpu.roll(k1, HD, 1)
            v2 = pltpu.roll(v1, HD, 1)
        else:
            q1 = pltpu.roll(q1, HD, 1)
            v2 = v1
            v1 = pltpu.roll(v1, HD, 1)
        pieces = (pair_of(query, h).astype(BF), pair_of(keys, h).astype(BF), pair_of(values, h).astype(BF))
        for a in range(SPLIT):
            for b in range(SPLIT):
                at = place(h, a, b)
                qa, kb = slice(a * BLK, (a + 1) * BLK), slice(b * BLK, (b + 1) * BLK)
                packed_ref[at, 0:32, :] = pieces[0][qa]
                packed_ref[at, 32:64, :] = pieces[1][kb]
                packed_ref[at, 64:96, :] = pieces[2][kb]
                rest_ref[at, 0:32, :] = jnp.where(low[:BLK], q1[qa], k1[kb]).astype(BF)
                half = b * BLK + BLK // 2
                rest_ref[at, 32:48, :] = jnp.where(
                    low[: BLK // 2], v1[b * BLK : half], v2[half : (b + 1) * BLK]
                ).astype(BF)
                row = a * BLK + b * 8
                for c in range(DM // 128):
                    rest_ref[at, 48 + 8 * c : 56 + 8 * c, :] = cot_ref[row : row + 8, c * 128 : (c + 1) * 128]


def stem(halo, conv_weight, cotangent, features, patch_weight, query_weight, key_weight, value_weight):
    hbm = pl.BlockSpec(memory_space=pl.ANY)
    vmem = pl.BlockSpec(memory_space=pltpu.VMEM)
    return pl.pallas_call(
        stem_kernel,
        in_specs=[vmem, vmem, vmem, hbm, pl.BlockSpec(memory_space=pltpu.HBM)] + [hbm] * 3,
        out_specs=(vmem, vmem, vmem),
        out_shape=(
            jax.ShapeDtypeStruct((128, DM), BF),
            jax.ShapeDtypeStruct((64, CHUNK, 128), BF),
            jax.ShapeDtypeStruct((64, CHUNK, 128), BF),
        ),
        scratch_shapes=[
            pltpu.VMEM((2, 34, 32, 256), BF),
            pltpu.VMEM((2, 2, ZW, 256), F32),
            pltpu.VMEM((2, 64 * ZW, 128), F32),
            pltpu.VMEM((2, 64 * ZW, 128), F32),
            pltpu.VMEM((2, 64 * ZW, 128), F32),
            pltpu.VMEM((128, 4096), BF),
            pltpu.VMEM((4096, DM), BF),
            pltpu.VMEM((DM, DM), BF),
            pltpu.VMEM((DM, DM), BF),
            pltpu.VMEM((DM, DM), BF),
            pltpu.SemaphoreType.DMA((6,)),
        ],
        compiler_params=pltpu.CompilerParams(vmem_limit_bytes=36 << 20),
        name="stem",
    )(halo, conv_weight, cotangent, features, patch_weight, query_weight, key_weight, value_weight)


def in_hbm(x):
    return pltpu.with_memory_space_constraint(x, pltpu.HBM)


def local(
    features,
    neighbours,
    conv_weight,
    patch_weight,
    query_weight,
    key_weight,
    value_weight,
    output_weight,
    cotangent,
):
    _, inner = split_device(lax.axis_index("tile"))
    faces = swap(gather_faces(neighbours, in_hbm(features)), INNER).reshape(16, HALO, 256)
    tiles = faces[:, 128, :8].astype(jnp.int32)
    outer, goal = split_device(tiles >> 1)
    targets = jnp.where((tiles < 128) & (goal == inner), (outer & 7) * 2 + (tiles & 1), -1)
    halo = swap(route(targets, faces), OUTER).reshape(8, 2, HALO, 256)
    halo, conv_weight = lax.optimization_barrier((halo, conv_weight))
    taps = conv_weight.reshape(9, 256, 256)
    tokens, packed, rest = stem(
        halo, taps, cotangent, features, in_hbm(patch_weight), query_weight, key_weight, value_weight
    )
    packed = swap(packed)
    packed, rest = lax.optimization_barrier((packed, rest))
    rest = swap(rest)
    parts = swap(attend_single(rest, in_hbm(attend_pair(packed))), KEY_GROUPS)
    att, grad = merge(parts, rest)
    terms = swap(grad.reshape(16, SHARE, 128), HEAD_GROUPS)
    received = swap(share_out(terms, att))
    return finish(received, tokens, output_weight)


def solution(mesh):
    in_specs = (
        P(("slide", "tile"), None, None, None),
        P(("slide", "tile"), None),
        P(),
        P(),
        P(),
        P(),
        P(),
        P(),
        P(("slide", "tile"), None),
    )
    out_specs = (P(("slide", "tile"), None), P("slide", None))
    return jax.shard_map(local, mesh=mesh, in_specs=in_specs, out_specs=out_specs, check_vma=False)
```

```python
import jax
import jax.numpy as jnp
from jax import lax
from jax.experimental import pallas as pl
from jax.experimental.pallas import tpu as pltpu
from jax.sharding import PartitionSpec as P

PATCH = 4
HEADS = 12
HD = 64
DM = 768
SPLIT = 4
HG = HEADS // SPLIT
GW = HG * HD
BLK = 32
CHUNK = 96
OW = 256
HALO = 136
BF = jnp.bfloat16
F32 = jnp.float32


def hi_bit(coord):
    return coord >> 1


def lo_bit(coord):
    return (coord ^ (coord >> 1)) & 1


def split_device(dev):
    z, y, x = dev >> 4, (dev >> 2) & 3, dev & 3
    outer = hi_bit(z) * 4 + hi_bit(y) * 2 + hi_bit(x)
    inner = lo_bit(z) * 4 + lo_bit(y) * 2 + lo_bit(x)
    return outer, inner


def device_groups():
    place = {}
    for dev in range(64):
        place[split_device(dev)] = dev
    inner_groups = [[place[(a, b)] for b in range(8)] for a in range(8)]
    outer_groups = [[place[(a, b)] for a in range(8)] for b in range(8)]
    return inner_groups, outer_groups


INNER, OUTER = device_groups()


def place(h, a, b):
    def coord(hi, lo):
        return hi * 2 + (hi ^ lo)

    return coord(a >> 1, b >> 1) * 16 + coord(a & 1, b & 1) * 4 + h


KEY_GROUPS = [[place(h, a, b) for b in range(SPLIT)] for h in range(SPLIT) for a in range(SPLIT)]
HEAD_GROUPS = [[place(h, a, b) for a in range(SPLIT) for b in range(SPLIT)] for h in range(SPLIT)]


def swap(x, groups=None):
    return lax.all_to_all(
        x, "tile", split_axis=0, concat_axis=0, tiled=True, axis_index_groups=groups
    )


def faces_kernel(links_ref, features_hbm, out_ref, sides_ref, cols_ref, faces_ref, sems):
    loads = []
    for t in range(2):
        for n, y in enumerate((0, 31)):
            loads.append((features_hbm.at[t, y], faces_ref.at[t, n * 32 : n * 32 + 32]))
        for n, x in enumerate((0, 24)):
            loads.append((features_hbm.at[t, :, x : x + 8], sides_ref.at[t, n]))
    loads = [pltpu.make_async_copy(src, dst, sems.at[n]) for n, (src, dst) in enumerate(loads)]
    for load in loads:
        load.start()
    lanes = lax.broadcasted_iota(jnp.int32, (8, 128), 1)
    for t in range(2):
        row = jnp.zeros((8, 128), F32)
        for d in range(8):
            row = jnp.where(lanes == d, links_ref[t, d].astype(F32), row)
        faces_ref[t, 128:HALO, :128] = row.astype(BF)
        faces_ref[t, 128:HALO, 128:] = jnp.zeros((8, 128), BF)
    for load in loads:
        load.wait()
    for t in range(2):
        for n, x in enumerate((0, 7)):
            for lt in range(2):
                cols_ref[...] = sides_ref[t, n, :, :, lt * 128 : lt * 128 + 128].astype(F32).reshape(256, 128)
                faces_ref[t, 64 + n * 32 : 96 + n * 32, lt * 128 : lt * 128 + 128] = cols_ref[
                    pl.ds(x, 32, stride=8), :
                ].astype(BF)
    for n in range(8):
        out_ref[n] = faces_ref[...]


def gather_faces(links, features):
    hbm = pl.BlockSpec(memory_space=pltpu.HBM)
    return pl.pallas_call(
        faces_kernel,
        in_specs=[pl.BlockSpec(memory_space=pltpu.SMEM), hbm],
        out_specs=pl.BlockSpec(memory_space=pltpu.VMEM),
        out_shape=jax.ShapeDtypeStruct((8, 2, HALO, 256), BF),
        scratch_shapes=[
            pltpu.VMEM((2, 2, 32, 8, 256), BF),
            pltpu.VMEM((256, 128), F32),
            pltpu.VMEM((2, HALO, 256), BF),
            pltpu.SemaphoreType.DMA((8,)),
        ],
        compiler_params=pltpu.CompilerParams(vmem_limit_bytes=6 << 20),
        name="faces",
    )(links, features)


EDGES = {1: (0, 32), 6: (32, 0), 3: (64, 96), 4: (96, 64)}
CORNERS = {0: (0, 3), 2: (31, 2), 5: (32, 1), 7: (63, 0)}


def route_kernel(targets_ref, faces_ref, out_ref):
    out_ref[...] = jnp.zeros(out_ref.shape, BF)
    row_ids = lax.broadcasted_iota(jnp.int32, (8, 256), 0)

    def per_tile(src, carry):
        for direction in range(8):
            target = targets_ref[src, direction]

            @pl.when(target >= 0)
            def _():
                if direction in EDGES:
                    first, dest = EDGES[direction]
                    out_ref[target, dest : dest + 32, :] = faces_ref[src, first : first + 32, :]
                else:
                    row, dest = CORNERS[direction]
                    base = row // 8 * 8
                    cell = faces_ref[src, base : base + 8, :].astype(F32)[row - base : row - base + 1, :]
                    old = out_ref[target, 128:HALO, :].astype(F32)
                    new = jnp.where(row_ids == dest, jnp.broadcast_to(cell, (8, 256)), old)
                    out_ref[target, 128:HALO, :] = new.astype(BF)

        return carry

    lax.fori_loop(0, 16, per_tile, 0)


def route(targets, faces):
    vmem = pl.BlockSpec(memory_space=pltpu.VMEM)
    return pl.pallas_call(
        route_kernel,
        in_specs=[pl.BlockSpec(memory_space=pltpu.SMEM), vmem],
        out_specs=vmem,
        out_shape=jax.ShapeDtypeStruct((16, HALO, 256), BF),
        compiler_params=pltpu.CompilerParams(vmem_limit_bytes=8 << 20),
        name="route",
    )(targets, faces)


def attend_heads(units):
    scores = [
        lax.dot_general(q * BF(HD ** -0.5), k, (((1,), (1,)), ((), ())), preferred_element_type=F32)
        for q, k, _ in units
    ]
    results = []
    for score, (_, _, value) in zip(scores, units):
        top = jnp.max(score, axis=1, keepdims=True)
        weights = jnp.exp(score - top).astype(BF)
        res = jnp.dot(weights, value, preferred_element_type=F32)
        total = res[:, HD : HD + 1]
        lse = top + jnp.log(total)
        one = lse.astype(BF).astype(F32)
        two = (lse - one).astype(BF).astype(F32)
        results.append((res[:, :HD] / total, (one, two, lse - one - two)))
    return results


def put_rows(row_ref, out_ref, lanes):
    for n in range(row_ref.shape[0] // BLK):
        for b in range(SPLIT):
            first = n * BLK + b * 8
            out_ref[b, n * 8 : n * 8 + 8, :] = row_ref[first : first + 8, lanes].astype(BF)


def pair_kernel(in_ref, all_ref, out_ref, key_ref, val_ref, row_ref):
    @pl.when(pl.program_id(0) == 0)
    def _():
        ones = jnp.where(lax.broadcasted_iota(jnp.int32, (2048, HD), 1) == 0, 1.0, 0.0).astype(BF)
        for g in range(2):
            key_ref[g] = all_ref[:, 32:64, g * HD : (g + 1) * HD].reshape(2048, HD)
            val_ref[g, :, :HD] = all_ref[:, 64:96, g * HD : (g + 1) * HD].reshape(2048, HD)
            val_ref[g, :, HD:] = ones

    half = 8
    units = []
    for first in range(0, in_ref.shape[0], half):
        for g in range(2):
            query = in_ref[first : first + half, :BLK, g * HD : (g + 1) * HD].reshape(half * BLK, HD)
            units.append((query, key_ref[g], val_ref[g]))
    results = attend_heads(units)
    lanes = lax.broadcasted_iota(jnp.int32, (half * BLK, 128), 1)
    for n in range(len(units) // 2):
        rows = slice(n * half * BLK, (n + 1) * half * BLK)
        tail = jnp.zeros((half * BLK, 128), F32)
        for g in range(2):
            out, parts = results[2 * n + g]
            row_ref[rows, g * HD : (g + 1) * HD] = out
            for i, part in enumerate(parts):
                tail = jnp.where(lanes == HD + 3 * g + i, part, tail)
        row_ref[rows, 128:] = tail
    put_rows(row_ref, out_ref, slice(0, OW))


def single_kernel(in_ref, all_ref, part_ref, out_ref, key_ref, val_ref, row_ref):
    @pl.when(pl.program_id(0) == 0)
    def _():
        ones = jnp.where(lax.broadcasted_iota(jnp.int32, (2048, HD), 1) == 0, 1.0, 0.0).astype(BF)
        val_ref[:, HD:] = ones
        for g in range(2):
            rows = slice(g * 1024, (g + 1) * 1024)
            key_ref[rows, :] = all_ref[:, g * 16 : g * 16 + 16, HD:].reshape(1024, HD)
            val_ref[rows, :HD] = all_ref[:, 32:48, g * HD : (g + 1) * HD].reshape(1024, HD)

    half = 8
    units = []
    for first in range(0, in_ref.shape[0], half):
        query = in_ref[first : first + half, :BLK, :HD].reshape(half * BLK, HD)
        units.append((query, key_ref[...], val_ref[...]))
    results = attend_heads(units)
    lanes = lax.broadcasted_iota(jnp.int32, (half * BLK, 128), 1)
    for n, (out, parts) in enumerate(results):
        rows = slice(n * half * BLK, (n + 1) * half * BLK)
        tail = jnp.zeros((half * BLK, 128), F32)
        for i, part in enumerate(parts):
            tail = jnp.where(lanes == HD + 6 + i, part, tail)
        row_ref[rows, :] = tail
        row_ref[rows, :HD] = out
    for n in range(row_ref.shape[0] // BLK):
        for b in range(SPLIT):
            first = n * BLK + b * 8
            old = part_ref[b, n * 8 : n * 8 + 8, 128:].astype(F32)
            out_ref[b, n * 8 : n * 8 + 8, :128] = part_ref[b, n * 8 : n * 8 + 8, :128]
            out_ref[b, n * 8 : n * 8 + 8, 128:] = (old + row_ref[first : first + 8, :]).astype(BF)


def attend_pair(packed):
    srcs = 32
    return pl.pallas_call(
        pair_kernel,
        grid=(64 // srcs,),
        in_specs=[
            pl.BlockSpec((srcs, CHUNK, 128), lambda i: (i, 0, 0)),
            pl.BlockSpec((64, CHUNK, 128), lambda i: (0, 0, 0)),
        ],
        out_specs=pl.BlockSpec((SPLIT, srcs * 8, OW), lambda i: (0, i, 0)),
        out_shape=pltpu.HBM((SPLIT, 512, OW), BF),
        scratch_shapes=[
            pltpu.VMEM((2, 2048, HD), BF),
            pltpu.VMEM((2, 2048, 2 * HD), BF),
            pltpu.VMEM((srcs * BLK, OW), F32),
        ],
        compiler_params=pltpu.CompilerParams(vmem_limit_bytes=38 << 20),
        name="attend_pair",
    )(packed, packed)


def attend_single(rest, parts):
    srcs = 64
    block = pl.BlockSpec((SPLIT, srcs * 8, OW), lambda i: (0, i, 0))
    return pl.pallas_call(
        single_kernel,
        grid=(64 // srcs,),
        in_specs=[
            pl.BlockSpec((srcs, CHUNK, 128), lambda i: (i, 0, 0)),
            pl.BlockSpec((64, CHUNK, 128), lambda i: (0, 0, 0)),
            block,
        ],
        out_specs=block,
        out_shape=jax.ShapeDtypeStruct((SPLIT, 512, OW), BF),
        scratch_shapes=[
            pltpu.VMEM((2048, HD), BF),
            pltpu.VMEM((2048, 2 * HD), BF),
            pltpu.VMEM((srcs * BLK, 128), F32),
        ],
        compiler_params=pltpu.CompilerParams(vmem_limit_bytes=38 << 20),
        name="attend_single",
    )(rest, rest, parts)


SHARE = 72
ROWS = SHARE + 16


def merge_kernel(parts_ref, rest_ref, att_ref, grad_ref, pair_ref, single_ref, cot_ref):
    for c in range(DM // 128):
        cot_ref[:, c * 128 : (c + 1) * 128] = rest_ref[:, 48 + 8 * c : 56 + 8 * c, :].reshape(512, 128)
    tails = []
    for b in range(SPLIT):
        tail = parts_ref[b, :, 128:].astype(F32)
        tails.append(tail + pltpu.roll(tail, 127, 1) + pltpu.roll(tail, 126, 1))
    top = jnp.maximum(jnp.maximum(tails[0], tails[1]), jnp.maximum(tails[2], tails[3]))
    ws = [jnp.exp(tail - top) for tail in tails]
    total = ws[0] + ws[1] + ws[2] + ws[3]
    low = lax.broadcasted_iota(jnp.int32, (512, 128), 1) < HD
    pair = jnp.zeros((512, 128), F32)
    single = jnp.zeros((512, 128), F32)
    inverse = 1.0 / total
    for b in range(SPLIT):
        share = ws[b] * inverse
        w0, w1, w2 = (share[:, HD + 3 * g : HD + 3 * g + 1] for g in range(HG))
        pair = pair + jnp.where(low, w0, w1) * parts_ref[b, :, :128].astype(F32)
        single = single + w2 * parts_ref[b, :, 128:].astype(F32)
    single = jnp.where(low, single, 0.0)
    pair_ref[...] = pair.astype(BF)
    single_ref[...] = single.astype(BF)
    for n in range(64):
        att_ref[n, :8, :] = pair[n * 8 : n * 8 + 8].astype(BF)
        att_ref[n, 8:, :] = single[n * 8 : n * 8 + 8].astype(BF)
    for first, ref, count in ((0, pair_ref, 128), (128, single_ref, 64)):
        grad = lax.dot_general(
            ref[...], cot_ref[...], (((0,), (0,)), ((), ())), preferred_element_type=F32
        )
        for c in range(DM // 128):
            grad_ref[c, first : first + count, :] = grad[:count, c * 128 : (c + 1) * 128].astype(BF)


def merge(parts, rest):
    return pl.pallas_call(
        merge_kernel,
        out_shape=(
            jax.ShapeDtypeStruct((64, 16, 128), BF),
            jax.ShapeDtypeStruct((DM // 128, GW, 128), BF),
        ),
        scratch_shapes=[pltpu.VMEM((512, 128), BF), pltpu.VMEM((512, 128), BF), pltpu.VMEM((512, DM), BF)],
        compiler_params=pltpu.CompilerParams(vmem_limit_bytes=16 << 20),
        name="merge",
    )(parts, rest)


def share_kernel(terms_ref, att_ref, out_ref, total_ref):
    @pl.when(pl.program_id(0) == 0)
    def _():
        total = terms_ref[0].astype(F32)
        for n in range(1, 16):
            total = total + terms_ref[n].astype(F32)
        total_ref[...] = total.astype(BF)

    for n in range(out_ref.shape[0]):
        out_ref[n, :SHARE, :] = total_ref[...]
        out_ref[n, SHARE:, :] = att_ref[n]


def share_out(terms, att):
    step = 16
    return pl.pallas_call(
        share_kernel,
        grid=(64 // step,),
        in_specs=[
            pl.BlockSpec((16, SHARE, 128), lambda i: (0, 0, 0)),
            pl.BlockSpec((step, 16, 128), lambda i: (i, 0, 0)),
        ],
        out_specs=pl.BlockSpec((step, ROWS, 128), lambda i: (i, 0, 0)),
        out_shape=jax.ShapeDtypeStruct((64, ROWS, 128), BF),
        scratch_shapes=[pltpu.VMEM((SHARE, 128), BF)],
        compiler_params=pltpu.CompilerParams(vmem_limit_bytes=8 << 20),
        name="share",
    )(terms, att)


def finish_kernel(all_ref, tokens_ref, weight_ref, mixed_ref, grad_hbm, att_ref, grad_ref, sems):
    for h in range(SPLIT):
        for m in range(16):
            at = place(h, m // SPLIT, m % SPLIT)
            done = 0
            while done < SHARE:
                block, row = divmod(m * SHARE + done, GW)
                count = min(SHARE - done, (128 if row < 128 else GW) - row)
                dest = h * 128 + row if row < 128 else 512 + h * HD + row - 128
                grad_ref[dest : dest + count, block * 128 : (block + 1) * 128] = all_ref[
                    at, done : done + count, :
                ].astype(F32)
                done += count
    copies = [
        pltpu.make_async_copy(grad_ref.at[n * 384 : (n + 1) * 384], grad_hbm.at[n * 384 : (n + 1) * 384], sems.at[n])
        for n in range(2)
    ]
    for copy in copies:
        copy.start()
    lanes = lax.broadcasted_iota(jnp.int32, (8, 128), 1) < HD
    for a in range(SPLIT):
        for b in range(SPLIT):
            row = a * BLK + b * 8
            for h in range(SPLIT):
                att_ref[row : row + 8, h * 128 : (h + 1) * 128] = all_ref[place(h, a, b), SHARE : SHARE + 8, :]
            for h in range(0, SPLIT, 2):
                even = all_ref[place(h, a, b), SHARE + 8 :, :].astype(F32)
                odd = pltpu.roll(all_ref[place(h + 1, a, b), SHARE + 8 :, :].astype(F32), HD, 1)
                first = 512 + h * HD
                att_ref[row : row + 8, first : first + 128] = jnp.where(lanes, even, odd).astype(BF)
    mixed_ref[...] = (
        tokens_ref[...].astype(F32) + jnp.dot(att_ref[...], weight_ref[...], preferred_element_type=F32)
    ).astype(BF)
    for copy in copies:
        copy.wait()


def finish(received, tokens, weight):
    vmem = pl.BlockSpec(memory_space=pltpu.VMEM)
    return pl.pallas_call(
        finish_kernel,
        in_specs=[vmem] * 3,
        out_specs=(vmem, pl.BlockSpec(memory_space=pl.ANY)),
        out_shape=(
            jax.ShapeDtypeStruct((128, DM), BF),
            jax.ShapeDtypeStruct((DM, DM), F32),
        ),
        scratch_shapes=[
            pltpu.VMEM((128, DM), BF),
            pltpu.VMEM((DM, DM), F32),
            pltpu.SemaphoreType.DMA((2,)),
        ],
        compiler_params=pltpu.CompilerParams(vmem_limit_bytes=12 << 20),
        name="finish",
    )(received, tokens, weight)


ZW = 48
Z0 = 8


def conv_kernel(features_ref, conv_ref, out_ref, left_ref, right_ref):
    for t in range(2):
        for y in range(32):
            for lt in range(2):
                slot = (t * 32 + y) * ZW
                left_ref[lt, slot : slot + Z0, :] = jnp.zeros((Z0, 128), F32)
                right_ref[lt, slot + Z0 + 32 : slot + ZW, :] = jnp.zeros((Z0, 128), F32)
        for y in range(0, 32, 8):
            zero = jnp.zeros((32, 256), BF)
            accs = []
            for dx in range(3):
                acc = jnp.zeros((256, 256), F32)
                for dy in range(3):
                    first = y + dy - 1
                    if first < 0:
                        rows = jnp.concatenate([zero, features_ref[t, :7].reshape(224, 256)], axis=0)
                    elif first + 8 > 32:
                        rows = jnp.concatenate([features_ref[t, first:].reshape(224, 256), zero], axis=0)
                    else:
                        rows = features_ref[t, first : first + 8].reshape(256, 256)
                    acc = acc + jnp.dot(rows, conv_ref[dy * 3 + dx], preferred_element_type=F32)
                accs.append(acc)
            for n in range(8):
                slot = (t * 32 + y + n) * ZW + Z0
                row = (t * 32 + y + n) * 32
                for lt in range(2):
                    part = (slice(n * 32, n * 32 + 32), slice(lt * 128, lt * 128 + 128))
                    left_ref[lt, slot : slot + 32, :] = accs[0][part]
                    right_ref[lt, slot : slot + 32, :] = accs[2][part]
                    out_ref[lt, row : row + 32, :] = (
                        accs[1][part]
                        + left_ref[lt, slot - 1 : slot + 31, :]
                        + right_ref[lt, slot + 1 : slot + 33, :]
                    )


def conv_inside(features, taps):
    vmem = pl.BlockSpec(memory_space=pltpu.VMEM)
    return pl.pallas_call(
        conv_kernel,
        in_specs=[vmem, vmem],
        out_specs=vmem,
        out_shape=jax.ShapeDtypeStruct((2, 2048, 128), F32),
        scratch_shapes=[pltpu.VMEM((2, 64 * ZW, 128), F32), pltpu.VMEM((2, 64 * ZW, 128), F32)],
        compiler_params=pltpu.CompilerParams(vmem_limit_bytes=16 << 20),
        name="conv_inside",
    )(features, taps)


def stem_kernel(
    halo_ref,
    conv_ref,
    cot_ref,
    inside_ref,
    patch_hbm,
    query_hbm,
    key_hbm,
    value_hbm,
    tokens_ref,
    packed_ref,
    rest_ref,
    side_ref,
    edge_ref,
    hid_ref,
    patch_ref,
    wq_ref,
    wk_ref,
    wv_ref,
    sems,
):
    pairs = ((patch_hbm, patch_ref), (query_hbm, wq_ref), (key_hbm, wk_ref), (value_hbm, wv_ref))
    loads = [pltpu.make_async_copy(src, dst, sems.at[n]) for n, (src, dst) in enumerate(pairs)]
    for load in loads:
        load.start()

    def halo_rows(t, first, count):
        total = halo_ref[0, t, first : first + count, :].astype(F32)
        for n in range(1, 8):
            total = total + halo_ref[n, t, first : first + count, :].astype(F32)
        return total

    for t in range(2):
        corner = halo_rows(t, 128, 8)
        for side in range(4):
            side_ref[side, t, Z0 : Z0 + 32, :] = halo_rows(t, 32 * side, 32)
            for end, row in enumerate((Z0 - 1, Z0 + 32)):
                if side < 2:
                    cell = corner[side * 2 + end : side * 2 + end + 1]
                else:
                    cell = jnp.zeros((1, 256), F32)
                side_ref[side, t, row : row + 1, :] = cell
    for side in range(4):
        edge = jnp.zeros((64, 256), F32)
        for k in range(3):
            part = jnp.concatenate(
                [side_ref[side, t, Z0 - 1 + k : Z0 + 31 + k, :].astype(BF) for t in range(2)], axis=0
            )
            tap = (k, 6 + k, 3 * k, 3 * k + 2)[side]
            edge = edge + jnp.dot(part, conv_ref[tap], preferred_element_type=F32)
        for lt in range(2):
            edge_ref[lt, side * 64 : side * 64 + 64, :] = edge[:, lt * 128 : lt * 128 + 128]

    sub = lax.broadcasted_iota(jnp.int32, (8, 128), 0)
    for r in range(4):
        for c in range(4):
            for t in range(2):
                for pr in range(8):
                    y = pr * 4 + r
                    row = (t * 8 + pr) * 8
                    for lt in range(2):
                        total = inside_ref[lt, pl.ds((t * 32 + y) * 32 + c, 8, stride=4), :]
                        if y == 0:
                            total = total + edge_ref[lt, pl.ds(t * 32 + c, 8, stride=4), :]
                        if y == 31:
                            total = total + edge_ref[lt, pl.ds(64 + t * 32 + c, 8, stride=4), :]
                        if c == 0 or c == 3:
                            at = (128 if c == 0 else 192) + t * 32 + y
                            cell = jnp.broadcast_to(edge_ref[lt, at : at + 1, :], (8, 128))
                            total = total + jnp.where(sub == (0 if c == 0 else 7), cell, 0.0)
                        col = (r * 4 + c) * 256 + lt * 128
                        hid_ref[row : row + 8, col : col + 128] = jax.nn.gelu(total).astype(BF)
    loads[0].wait()
    tokens = jnp.dot(hid_ref[...], patch_ref[...], preferred_element_type=F32).astype(BF)
    tokens_ref[...] = tokens
    for load in loads[1:]:
        load.wait()
    query = jnp.dot(tokens, wq_ref[...], preferred_element_type=F32)
    keys = jnp.dot(tokens, wk_ref[...], preferred_element_type=F32)
    values = jnp.dot(tokens, wv_ref[...], preferred_element_type=F32)
    low = lax.broadcasted_iota(jnp.int32, (128, 128), 1) < HD

    def pair_of(x, h):
        return x[:, h * 128 : (h + 1) * 128]

    for h in range(SPLIT):
        one = 4 + h // 2
        q1, k1, v1 = pair_of(query, one), pair_of(keys, one), pair_of(values, one)
        if h % 2 == 0:
            k1 = pltpu.roll(k1, HD, 1)
            v2 = pltpu.roll(v1, HD, 1)
        else:
            q1 = pltpu.roll(q1, HD, 1)
            v2 = v1
            v1 = pltpu.roll(v1, HD, 1)
        pieces = (pair_of(query, h).astype(BF), pair_of(keys, h).astype(BF), pair_of(values, h).astype(BF))
        for a in range(SPLIT):
            for b in range(SPLIT):
                at = place(h, a, b)
                qa, kb = slice(a * BLK, (a + 1) * BLK), slice(b * BLK, (b + 1) * BLK)
                packed_ref[at, 0:32, :] = pieces[0][qa]
                packed_ref[at, 32:64, :] = pieces[1][kb]
                packed_ref[at, 64:96, :] = pieces[2][kb]
                rest_ref[at, 0:32, :] = jnp.where(low[:BLK], q1[qa], k1[kb]).astype(BF)
                half = b * BLK + BLK // 2
                rest_ref[at, 32:48, :] = jnp.where(
                    low[: BLK // 2], v1[b * BLK : half], v2[half : (b + 1) * BLK]
                ).astype(BF)
                row = a * BLK + b * 8
                for c in range(DM // 128):
                    rest_ref[at, 48 + 8 * c : 56 + 8 * c, :] = cot_ref[row : row + 8, c * 128 : (c + 1) * 128]


def stem(halo, conv_weight, cotangent, inside, patch_weight, query_weight, key_weight, value_weight):
    hbm = pl.BlockSpec(memory_space=pl.ANY)
    vmem = pl.BlockSpec(memory_space=pltpu.VMEM)
    return pl.pallas_call(
        stem_kernel,
        in_specs=[vmem] * 4 + [hbm] * 4,
        out_specs=(vmem, vmem, vmem),
        out_shape=(
            jax.ShapeDtypeStruct((128, DM), BF),
            jax.ShapeDtypeStruct((64, CHUNK, 128), BF),
            jax.ShapeDtypeStruct((64, CHUNK, 128), BF),
        ),
        scratch_shapes=[
            pltpu.VMEM((4, 2, ZW, 256), F32),
            pltpu.VMEM((2, 256, 128), F32),
            pltpu.VMEM((128, 4096), BF),
            pltpu.VMEM((4096, DM), BF),
            pltpu.VMEM((DM, DM), BF),
            pltpu.VMEM((DM, DM), BF),
            pltpu.VMEM((DM, DM), BF),
            pltpu.SemaphoreType.DMA((4,)),
        ],
        compiler_params=pltpu.CompilerParams(vmem_limit_bytes=28 << 20),
        name="stem",
    )(halo, conv_weight, cotangent, inside, patch_weight, query_weight, key_weight, value_weight)


def in_hbm(x):
    return pltpu.with_memory_space_constraint(x, pltpu.HBM)


def local(
    features,
    neighbours,
    conv_weight,
    patch_weight,
    query_weight,
    key_weight,
    value_weight,
    output_weight,
    cotangent,
):
    _, inner = split_device(lax.axis_index("tile"))
    faces = gather_faces(neighbours, in_hbm(features))
    faces, inner = lax.optimization_barrier((faces, inner))
    faces = swap(faces, INNER).reshape(16, HALO, 256)
    tiles = faces[:, 128, :8].astype(jnp.int32)
    outer, goal = split_device(tiles >> 1)
    targets = jnp.where((tiles < 128) & (goal == inner), (outer & 7) * 2 + (tiles & 1), -1)
    routed, taps = lax.optimization_barrier((route(targets, faces), conv_weight.reshape(9, 256, 256)))
    halo = swap(routed, OUTER).reshape(8, 2, HALO, 256)
    inside = conv_inside(features, taps)
    tokens, packed, rest = stem(
        halo,
        taps,
        cotangent,
        inside,
        in_hbm(patch_weight),
        in_hbm(query_weight),
        in_hbm(key_weight),
        in_hbm(value_weight),
    )
    packed = swap(packed)
    packed, rest = lax.optimization_barrier((packed, rest))
    rest = swap(rest)
    parts = swap(attend_single(rest, in_hbm(attend_pair(packed))), KEY_GROUPS)
    att, grad = merge(parts, rest)
    terms = swap(grad.reshape(16, SHARE, 128), HEAD_GROUPS)
    received = swap(share_out(terms, att))
    return finish(received, tokens, output_weight)


def solution(mesh):
    in_specs = (
        P(("slide", "tile"), None, None, None),
        P(("slide", "tile"), None),
        P(),
        P(),
        P(),
        P(),
        P(),
        P(),
        P(("slide", "tile"), None),
    )
    out_specs = (P(("slide", "tile"), None), P("slide", None))
    return jax.shard_map(local, mesh=mesh, in_specs=in_specs, out_specs=out_specs, check_vma=False)
```

```python
import jax
import jax.numpy as jnp
from jax import lax
from jax.experimental import pallas as pl
from jax.experimental.pallas import tpu as pltpu
from jax.sharding import PartitionSpec as P

PATCH = 4
HEADS = 12
HD = 64
DM = 768
SPLIT = 4
HG = HEADS // SPLIT
GW = HG * HD
BLK = 32
CHUNK = 96
PARTS = 512 + 256 + 64
HALO = 136
BF = jnp.bfloat16
F32 = jnp.float32


def hi_bit(coord):
    return coord >> 1


def lo_bit(coord):
    return (coord ^ (coord >> 1)) & 1


def split_device(dev):
    z, y, x = dev >> 4, (dev >> 2) & 3, dev & 3
    outer = hi_bit(z) * 4 + hi_bit(y) * 2 + hi_bit(x)
    inner = lo_bit(z) * 4 + lo_bit(y) * 2 + lo_bit(x)
    return outer, inner


def device_groups():
    place = {}
    for dev in range(64):
        place[split_device(dev)] = dev
    inner_groups = [[place[(a, b)] for b in range(8)] for a in range(8)]
    outer_groups = [[place[(a, b)] for a in range(8)] for b in range(8)]
    return inner_groups, outer_groups


INNER, OUTER = device_groups()


def place(h, a, b):
    def coord(hi, lo):
        return hi * 2 + (hi ^ lo)

    return coord(a >> 1, b >> 1) * 16 + coord(a & 1, b & 1) * 4 + h


KEY_GROUPS = [[place(h, a, b) for b in range(SPLIT)] for h in range(SPLIT) for a in range(SPLIT)]
HEAD_GROUPS = [[place(h, a, b) for a in range(SPLIT) for b in range(SPLIT)] for h in range(SPLIT)]


def in_hbm(x):
    return pltpu.with_memory_space_constraint(x, pltpu.HBM)


def swap(x, groups=None):
    return lax.all_to_all(
        x, "tile", split_axis=0, concat_axis=0, tiled=True, axis_index_groups=groups
    )


def faces_kernel(links_ref, features_hbm, out_ref, sides_ref, cols_ref, faces_ref, sems):
    loads = []
    for t in range(2):
        for n, y in enumerate((0, 31)):
            loads.append((features_hbm.at[t, y], faces_ref.at[t, n * 32 : n * 32 + 32]))
        for n, x in enumerate((0, 24)):
            loads.append((features_hbm.at[t, :, x : x + 8], sides_ref.at[t, n]))
    loads = [pltpu.make_async_copy(src, dst, sems.at[n]) for n, (src, dst) in enumerate(loads)]
    for load in loads:
        load.start()
    lanes = lax.broadcasted_iota(jnp.int32, (8, 128), 1)
    for t in range(2):
        row = jnp.zeros((8, 128), F32)
        for d in range(8):
            row = jnp.where(lanes == d, links_ref[t, d].astype(F32), row)
        faces_ref[t, 128:HALO, :128] = row.astype(BF)
        faces_ref[t, 128:HALO, 128:] = jnp.zeros((8, 128), BF)
    for load in loads:
        load.wait()
    for t in range(2):
        for n, x in enumerate((0, 7)):
            for lt in range(2):
                cols_ref[...] = sides_ref[t, n, :, :, lt * 128 : lt * 128 + 128].astype(F32).reshape(256, 128)
                faces_ref[t, 64 + n * 32 : 96 + n * 32, lt * 128 : lt * 128 + 128] = cols_ref[
                    pl.ds(x, 32, stride=8), :
                ].astype(BF)
    for n in range(8):
        out_ref[n] = faces_ref[...]


def gather_faces(links, features):
    hbm = pl.BlockSpec(memory_space=pltpu.HBM)
    return pl.pallas_call(
        faces_kernel,
        in_specs=[pl.BlockSpec(memory_space=pltpu.SMEM), hbm],
        out_specs=pl.BlockSpec(memory_space=pltpu.VMEM),
        out_shape=jax.ShapeDtypeStruct((8, 2, HALO, 256), BF),
        scratch_shapes=[
            pltpu.VMEM((2, 2, 32, 8, 256), BF),
            pltpu.VMEM((256, 128), F32),
            pltpu.VMEM((2, HALO, 256), BF),
            pltpu.SemaphoreType.DMA((8,)),
        ],
        compiler_params=pltpu.CompilerParams(vmem_limit_bytes=6 << 20),
        name="faces",
    )(links, features)


EDGES = {1: (0, 32), 6: (32, 0), 3: (64, 96), 4: (96, 64)}
CORNERS = {0: (0, 3), 2: (31, 2), 5: (32, 1), 7: (63, 0)}


def route_kernel(targets_ref, faces_ref, out_ref):
    out_ref[...] = jnp.zeros(out_ref.shape, BF)
    row_ids = lax.broadcasted_iota(jnp.int32, (8, 256), 0)

    def per_tile(src, carry):
        for direction in range(8):
            target = targets_ref[src, direction]

            @pl.when(target >= 0)
            def _():
                if direction in EDGES:
                    first, dest = EDGES[direction]
                    out_ref[target, dest : dest + 32, :] = faces_ref[src, first : first + 32, :]
                else:
                    row, dest = CORNERS[direction]
                    base = row // 8 * 8
                    cell = faces_ref[src, base : base + 8, :].astype(F32)[row - base : row - base + 1, :]
                    old = out_ref[target, 128:HALO, :].astype(F32)
                    new = jnp.where(row_ids == dest, jnp.broadcast_to(cell, (8, 256)), old)
                    out_ref[target, 128:HALO, :] = new.astype(BF)

        return carry

    lax.fori_loop(0, 16, per_tile, 0)


def route(targets, faces):
    vmem = pl.BlockSpec(memory_space=pltpu.VMEM)
    return pl.pallas_call(
        route_kernel,
        in_specs=[pl.BlockSpec(memory_space=pltpu.SMEM), vmem],
        out_specs=vmem,
        out_shape=jax.ShapeDtypeStruct((16, HALO, 256), BF),
        compiler_params=pltpu.CompilerParams(vmem_limit_bytes=8 << 20),
        name="route",
    )(targets, faces)


def attend_heads(units):
    scores = [
        lax.dot_general(q * BF(HD ** -0.5), k, (((1,), (1,)), ((), ())), preferred_element_type=F32)
        for q, k, _ in units
    ]
    results = []
    for score, (_, _, value) in zip(scores, units):
        top = jnp.max(score, axis=1, keepdims=True)
        weights = jnp.exp(score - top).astype(BF)
        res = jnp.dot(weights, value, preferred_element_type=F32)
        total = res[:, HD : HD + 1]
        lse = top + jnp.log(total)
        one = lse.astype(BF).astype(F32)
        two = (lse - one).astype(BF).astype(F32)
        results.append((res[:, :HD] / total, (one, two, lse - one - two)))
    return results


def put_rows(row_ref, out_ref, first):
    for n in range(row_ref.shape[0] // BLK):
        for b in range(SPLIT):
            row = n * BLK + b * 8
            out_ref[b, first + n * 8 : first + n * 8 + 8, :] = row_ref[row : row + 8, :].astype(BF)


UNIT = 8


def pair_kernel(in_ref, all_ref, out_ref, lse_ref, key_ref, val_ref, row_ref, tail_ref):
    step = pl.program_id(0)

    @pl.when(step == 0)
    def _():
        ones = jnp.where(lax.broadcasted_iota(jnp.int32, (2048, HD), 1) == 0, 1.0, 0.0).astype(BF)
        for g in range(2):
            key_ref[g] = all_ref[:, 32:64, g * HD : (g + 1) * HD].reshape(2048, HD)
            val_ref[g, :, :HD] = all_ref[:, 64:96, g * HD : (g + 1) * HD].reshape(2048, HD)
            val_ref[g, :, HD:] = ones
        tail_ref[...] = jnp.zeros(tail_ref.shape, F32)

    count = in_ref.shape[0] // UNIT
    units = []
    for n in range(count):
        for g in range(2):
            query = in_ref[n * UNIT : (n + 1) * UNIT, :BLK, g * HD : (g + 1) * HD].reshape(UNIT * BLK, HD)
            units.append((query, key_ref[g], val_ref[g]))
    results = attend_heads(units)
    lanes = lax.broadcasted_iota(jnp.int32, tail_ref.shape, 1)
    tail = tail_ref[...]
    for n in range(count):
        rows = slice(n * UNIT * BLK, (n + 1) * UNIT * BLK)
        for g in range(2):
            out, parts = results[2 * n + g]
            row_ref[rows, g * HD : (g + 1) * HD] = out
            for i, part in enumerate(parts):
                tail = jnp.where(lanes == 16 * (step * count + n) + 3 * g + i, part, tail)
    tail_ref[...] = tail
    put_rows(row_ref, out_ref, 0)
    put_rows(tail_ref, lse_ref, 0)


def single_kernel(all_ref, part_ref, lse_ref, out_ref, key_ref, val_ref, row_ref, tail_ref):
    ones = jnp.where(lax.broadcasted_iota(jnp.int32, (2048, HD), 1) == 0, 1.0, 0.0).astype(BF)
    val_ref[:, HD:] = ones
    for g in range(2):
        rows = slice(g * 1024, (g + 1) * 1024)
        key_ref[rows, :] = all_ref[:, g * 16 : g * 16 + 16, HD:].reshape(1024, HD)
        val_ref[rows, :HD] = all_ref[:, 32:48, g * HD : (g + 1) * HD].reshape(1024, HD)

    count = 64 // UNIT
    units = []
    for n in range(count):
        query = all_ref[n * UNIT : (n + 1) * UNIT, :BLK, :HD].reshape(UNIT * BLK, HD)
        units.append((query, key_ref[...], val_ref[...]))
    results = attend_heads(units)
    lanes = lax.broadcasted_iota(jnp.int32, tail_ref.shape, 1)
    tail = jnp.zeros(tail_ref.shape, F32)
    for n, (out, parts) in enumerate(results):
        first = n % (count // 2) * UNIT * BLK
        lane = n // (count // 2) * HD
        row_ref[first : first + UNIT * BLK, lane : lane + HD] = out
        for i, part in enumerate(parts):
            tail = jnp.where(lanes == 16 * n + 6 + i, part, tail)
    tail_ref[...] = tail
    for b in range(SPLIT):
        out_ref[b, :512, :] = part_ref[b]
    put_rows(row_ref, out_ref, 512)
    for n in range(UNIT):
        for b in range(SPLIT):
            row = n * BLK + b * 8
            new = lse_ref[b, n * 8 : n * 8 + 8, :].astype(F32) + tail_ref[row : row + 8, :]
            out_ref[b, 768 + n * 8 : 776 + n * 8, :] = new.astype(BF)


def attend_pair(packed):
    srcs = 32
    return pl.pallas_call(
        pair_kernel,
        grid=(64 // srcs,),
        in_specs=[
            pl.BlockSpec((srcs, CHUNK, 128), lambda i: (i, 0, 0)),
            pl.BlockSpec((64, CHUNK, 128), lambda i: (0, 0, 0)),
        ],
        out_specs=(
            pl.BlockSpec((SPLIT, srcs * 8, 128), lambda i: (0, i, 0)),
            pl.BlockSpec((SPLIT, 64, 128), lambda i: (0, 0, 0)),
        ),
        out_shape=(pltpu.HBM((SPLIT, 512, 128), BF), pltpu.HBM((SPLIT, 64, 128), BF)),
        scratch_shapes=[
            pltpu.VMEM((2, 2048, HD), BF),
            pltpu.VMEM((2, 2048, 2 * HD), BF),
            pltpu.VMEM((srcs * BLK, 128), F32),
            pltpu.VMEM((UNIT * BLK, 128), F32),
        ],
        compiler_params=pltpu.CompilerParams(vmem_limit_bytes=38 << 20),
        name="attend_pair",
    )(packed, packed)


def attend_single(rest, parts, lses):
    vmem = pl.BlockSpec(memory_space=pltpu.VMEM)
    return pl.pallas_call(
        single_kernel,
        in_specs=[vmem] * 3,
        out_specs=vmem,
        out_shape=jax.ShapeDtypeStruct((SPLIT, PARTS, 128), BF),
        scratch_shapes=[
            pltpu.VMEM((2048, HD), BF),
            pltpu.VMEM((2048, 2 * HD), BF),
            pltpu.VMEM((1024, 128), F32),
            pltpu.VMEM((UNIT * BLK, 128), F32),
        ],
        compiler_params=pltpu.CompilerParams(vmem_limit_bytes=38 << 20),
        name="attend_single",
    )(rest, in_hbm(parts), in_hbm(lses))


SHARE = 72
ROWS = SHARE + 16


def merge_kernel(parts_ref, rest_ref, att_ref, grad_ref, pair_ref, single_ref, cot_ref):
    for c in range(DM // 128):
        cot_ref[:, c * 128 : (c + 1) * 128] = rest_ref[:, 48 + 8 * c : 56 + 8 * c, :].reshape(512, 128)
    tails = []
    for b in range(SPLIT):
        tile = parts_ref[b, 768:, :].astype(F32)
        tail = jnp.concatenate([tile] + [pltpu.roll(tile, 128 - 16 * j, 1) for j in range(1, 8)], axis=0)
        tails.append(tail + pltpu.roll(tail, 127, 1) + pltpu.roll(tail, 126, 1))
    top = jnp.maximum(jnp.maximum(tails[0], tails[1]), jnp.maximum(tails[2], tails[3]))
    ws = [jnp.exp(tail - top) for tail in tails]
    inverse = 1.0 / (ws[0] + ws[1] + ws[2] + ws[3])
    low = lax.broadcasted_iota(jnp.int32, (512, 128), 1) < HD
    pair = jnp.zeros((512, 128), F32)
    folded = jnp.zeros((256, 128), F32)
    for b in range(SPLIT):
        share = ws[b] * inverse
        w0, w1, w2 = (share[:, 3 * g : 3 * g + 1] for g in range(HG))
        pair = pair + jnp.where(low, w0, w1) * parts_ref[b, :512, :].astype(F32)
        folded = folded + jnp.where(low[:256], w2[:256], w2[256:]) * parts_ref[b, 512:768, :].astype(F32)
    single = jnp.where(low, jnp.concatenate([folded, pltpu.roll(folded, HD, 1)], axis=0), 0.0)
    pair_ref[...] = pair.astype(BF)
    single_ref[...] = single.astype(BF)
    for n in range(64):
        att_ref[n, :8, :] = pair[n * 8 : n * 8 + 8].astype(BF)
        att_ref[n, 8:, :] = single[n * 8 : n * 8 + 8].astype(BF)
    for first, ref, count in ((0, pair_ref, 128), (128, single_ref, 64)):
        grad = lax.dot_general(
            ref[...], cot_ref[...], (((0,), (0,)), ((), ())), preferred_element_type=F32
        )
        for c in range(DM // 128):
            grad_ref[c, first : first + count, :] = grad[:count, c * 128 : (c + 1) * 128].astype(BF)


def merge(parts, rest):
    return pl.pallas_call(
        merge_kernel,
        out_shape=(
            jax.ShapeDtypeStruct((64, 16, 128), BF),
            jax.ShapeDtypeStruct((DM // 128, GW, 128), BF),
        ),
        scratch_shapes=[pltpu.VMEM((512, 128), BF), pltpu.VMEM((512, 128), BF), pltpu.VMEM((512, DM), BF)],
        compiler_params=pltpu.CompilerParams(vmem_limit_bytes=16 << 20),
        name="merge",
    )(parts, rest)


def share_kernel(terms_ref, att_ref, out_ref, total_ref):
    @pl.when(pl.program_id(0) == 0)
    def _():
        total = terms_ref[0].astype(F32)
        for n in range(1, 16):
            total = total + terms_ref[n].astype(F32)
        total_ref[...] = total.astype(BF)

    for n in range(out_ref.shape[0]):
        out_ref[n, :SHARE, :] = total_ref[...]
        out_ref[n, SHARE:, :] = att_ref[n]


def share_out(terms, att):
    step = 16
    return pl.pallas_call(
        share_kernel,
        grid=(64 // step,),
        in_specs=[
            pl.BlockSpec((16, SHARE, 128), lambda i: (0, 0, 0)),
            pl.BlockSpec((step, 16, 128), lambda i: (i, 0, 0)),
        ],
        out_specs=pl.BlockSpec((step, ROWS, 128), lambda i: (i, 0, 0)),
        out_shape=jax.ShapeDtypeStruct((64, ROWS, 128), BF),
        scratch_shapes=[pltpu.VMEM((SHARE, 128), BF)],
        compiler_params=pltpu.CompilerParams(vmem_limit_bytes=8 << 20),
        name="share",
    )(terms, att)


def finish_kernel(all_ref, tokens_ref, weight_ref, mixed_ref, grad_hbm, att_ref, grad_ref, sems):
    for h in range(SPLIT):
        for m in range(16):
            at = place(h, m // SPLIT, m % SPLIT)
            done = 0
            while done < SHARE:
                block, row = divmod(m * SHARE + done, GW)
                count = min(SHARE - done, (128 if row < 128 else GW) - row)
                dest = h * 128 + row if row < 128 else 512 + h * HD + row - 128
                grad_ref[dest : dest + count, block * 128 : (block + 1) * 128] = all_ref[
                    at, done : done + count, :
                ].astype(F32)
                done += count
    copies = [
        pltpu.make_async_copy(grad_ref.at[n * 384 : (n + 1) * 384], grad_hbm.at[n * 384 : (n + 1) * 384], sems.at[n])
        for n in range(2)
    ]
    for copy in copies:
        copy.start()
    lanes = lax.broadcasted_iota(jnp.int32, (8, 128), 1) < HD
    for a in range(SPLIT):
        for b in range(SPLIT):
            row = a * BLK + b * 8
            for h in range(SPLIT):
                att_ref[row : row + 8, h * 128 : (h + 1) * 128] = all_ref[place(h, a, b), SHARE : SHARE + 8, :]
            for h in range(0, SPLIT, 2):
                even = all_ref[place(h, a, b), SHARE + 8 :, :].astype(F32)
                odd = pltpu.roll(all_ref[place(h + 1, a, b), SHARE + 8 :, :].astype(F32), HD, 1)
                first = 512 + h * HD
                att_ref[row : row + 8, first : first + 128] = jnp.where(lanes, even, odd).astype(BF)
    mixed_ref[...] = (
        tokens_ref[...].astype(F32) + jnp.dot(att_ref[...], weight_ref[...], preferred_element_type=F32)
    ).astype(BF)
    for copy in copies:
        copy.wait()


def finish(received, tokens, weight):
    vmem = pl.BlockSpec(memory_space=pltpu.VMEM)
    return pl.pallas_call(
        finish_kernel,
        in_specs=[vmem] * 3,
        out_specs=(vmem, pl.BlockSpec(memory_space=pl.ANY)),
        out_shape=(
            jax.ShapeDtypeStruct((128, DM), BF),
            jax.ShapeDtypeStruct((DM, DM), F32),
        ),
        scratch_shapes=[
            pltpu.VMEM((128, DM), BF),
            pltpu.VMEM((DM, DM), F32),
            pltpu.SemaphoreType.DMA((2,)),
        ],
        compiler_params=pltpu.CompilerParams(vmem_limit_bytes=12 << 20),
        name="finish",
    )(received, tokens, weight)


ZW = 48
Z0 = 8


def conv_kernel(features_ref, conv_ref, out_ref, left_ref, right_ref):
    for t in range(2):
        for y in range(32):
            for lt in range(2):
                slot = (t * 32 + y) * ZW
                left_ref[lt, slot : slot + Z0, :] = jnp.zeros((Z0, 128), F32)
                right_ref[lt, slot + Z0 + 32 : slot + ZW, :] = jnp.zeros((Z0, 128), F32)
        for y in range(0, 32, 8):
            zero = jnp.zeros((32, 256), BF)
            accs = []
            for dx in range(3):
                acc = jnp.zeros((256, 256), F32)
                for dy in range(3):
                    first = y + dy - 1
                    if first < 0:
                        rows = jnp.concatenate([zero, features_ref[t, :7].reshape(224, 256)], axis=0)
                    elif first + 8 > 32:
                        rows = jnp.concatenate([features_ref[t, first:].reshape(224, 256), zero], axis=0)
                    else:
                        rows = features_ref[t, first : first + 8].reshape(256, 256)
                    acc = acc + jnp.dot(rows, conv_ref[dy * 3 + dx], preferred_element_type=F32)
                accs.append(acc)
            for n in range(8):
                slot = (t * 32 + y + n) * ZW + Z0
                row = (t * 32 + y + n) * 32
                for lt in range(2):
                    part = (slice(n * 32, n * 32 + 32), slice(lt * 128, lt * 128 + 128))
                    left_ref[lt, slot : slot + 32, :] = accs[0][part]
                    right_ref[lt, slot : slot + 32, :] = accs[2][part]
                    out_ref[lt, row : row + 32, :] = (
                        accs[1][part]
                        + left_ref[lt, slot - 1 : slot + 31, :]
                        + right_ref[lt, slot + 1 : slot + 33, :]
                    )


def conv_inside(features, taps):
    vmem = pl.BlockSpec(memory_space=pltpu.VMEM)
    return pl.pallas_call(
        conv_kernel,
        in_specs=[vmem, vmem],
        out_specs=vmem,
        out_shape=jax.ShapeDtypeStruct((2, 2048, 128), F32),
        scratch_shapes=[pltpu.VMEM((2, 64 * ZW, 128), F32), pltpu.VMEM((2, 64 * ZW, 128), F32)],
        compiler_params=pltpu.CompilerParams(vmem_limit_bytes=16 << 20),
        name="conv_inside",
    )(features, taps)


def stem_kernel(
    halo_ref,
    conv_ref,
    cot_ref,
    inside_ref,
    patch_hbm,
    query_hbm,
    key_hbm,
    value_hbm,
    tokens_ref,
    packed_ref,
    rest_ref,
    side_ref,
    edge_ref,
    hid_ref,
    patch_ref,
    wq_ref,
    wk_ref,
    wv_ref,
    sems,
):
    pairs = ((patch_hbm, patch_ref), (query_hbm, wq_ref), (key_hbm, wk_ref), (value_hbm, wv_ref))
    loads = [pltpu.make_async_copy(src, dst, sems.at[n]) for n, (src, dst) in enumerate(pairs)]
    for load in loads:
        load.start()

    def halo_rows(t, first, count):
        total = halo_ref[0, t, first : first + count, :].astype(F32)
        for n in range(1, 8):
            total = total + halo_ref[n, t, first : first + count, :].astype(F32)
        return total

    for t in range(2):
        corner = halo_rows(t, 128, 8)
        for side in range(4):
            side_ref[side, t, Z0 : Z0 + 32, :] = halo_rows(t, 32 * side, 32)
            for end, row in enumerate((Z0 - 1, Z0 + 32)):
                if side < 2:
                    cell = corner[side * 2 + end : side * 2 + end + 1]
                else:
                    cell = jnp.zeros((1, 256), F32)
                side_ref[side, t, row : row + 1, :] = cell
    for side in range(4):
        edge = jnp.zeros((64, 256), F32)
        for k in range(3):
            part = jnp.concatenate(
                [side_ref[side, t, Z0 - 1 + k : Z0 + 31 + k, :].astype(BF) for t in range(2)], axis=0
            )
            tap = (k, 6 + k, 3 * k, 3 * k + 2)[side]
            edge = edge + jnp.dot(part, conv_ref[tap], preferred_element_type=F32)
        for lt in range(2):
            edge_ref[lt, side * 64 : side * 64 + 64, :] = edge[:, lt * 128 : lt * 128 + 128]

    sub = lax.broadcasted_iota(jnp.int32, (8, 128), 0)
    for r in range(4):
        for c in range(4):
            for t in range(2):
                for pr in range(8):
                    y = pr * 4 + r
                    row = (t * 8 + pr) * 8
                    for lt in range(2):
                        total = inside_ref[lt, pl.ds((t * 32 + y) * 32 + c, 8, stride=4), :]
                        if y == 0:
                            total = total + edge_ref[lt, pl.ds(t * 32 + c, 8, stride=4), :]
                        if y == 31:
                            total = total + edge_ref[lt, pl.ds(64 + t * 32 + c, 8, stride=4), :]
                        if c == 0 or c == 3:
                            at = (128 if c == 0 else 192) + t * 32 + y
                            cell = jnp.broadcast_to(edge_ref[lt, at : at + 1, :], (8, 128))
                            total = total + jnp.where(sub == (0 if c == 0 else 7), cell, 0.0)
                        col = (r * 4 + c) * 256 + lt * 128
                        hid_ref[row : row + 8, col : col + 128] = jax.nn.gelu(total).astype(BF)
    loads[0].wait()
    tokens = jnp.dot(hid_ref[...], patch_ref[...], preferred_element_type=F32).astype(BF)
    tokens_ref[...] = tokens
    for load in loads[1:]:
        load.wait()
    query = jnp.dot(tokens, wq_ref[...], preferred_element_type=F32)
    keys = jnp.dot(tokens, wk_ref[...], preferred_element_type=F32)
    values = jnp.dot(tokens, wv_ref[...], preferred_element_type=F32)
    low = lax.broadcasted_iota(jnp.int32, (128, 128), 1) < HD

    def pair_of(x, h):
        return x[:, h * 128 : (h + 1) * 128]

    for h in range(SPLIT):
        one = 4 + h // 2
        q1, k1, v1 = pair_of(query, one), pair_of(keys, one), pair_of(values, one)
        if h % 2 == 0:
            k1 = pltpu.roll(k1, HD, 1)
            v2 = pltpu.roll(v1, HD, 1)
        else:
            q1 = pltpu.roll(q1, HD, 1)
            v2 = v1
            v1 = pltpu.roll(v1, HD, 1)
        pieces = (pair_of(query, h).astype(BF), pair_of(keys, h).astype(BF), pair_of(values, h).astype(BF))
        for a in range(SPLIT):
            for b in range(SPLIT):
                at = place(h, a, b)
                qa, kb = slice(a * BLK, (a + 1) * BLK), slice(b * BLK, (b + 1) * BLK)
                packed_ref[at, 0:32, :] = pieces[0][qa]
                packed_ref[at, 32:64, :] = pieces[1][kb]
                packed_ref[at, 64:96, :] = pieces[2][kb]
                rest_ref[at, 0:32, :] = jnp.where(low[:BLK], q1[qa], k1[kb]).astype(BF)
                half = b * BLK + BLK // 2
                rest_ref[at, 32:48, :] = jnp.where(
                    low[: BLK // 2], v1[b * BLK : half], v2[half : (b + 1) * BLK]
                ).astype(BF)
                row = a * BLK + b * 8
                for c in range(DM // 128):
                    rest_ref[at, 48 + 8 * c : 56 + 8 * c, :] = cot_ref[row : row + 8, c * 128 : (c + 1) * 128]


def stem(halo, conv_weight, cotangent, inside, patch_weight, query_weight, key_weight, value_weight):
    hbm = pl.BlockSpec(memory_space=pl.ANY)
    vmem = pl.BlockSpec(memory_space=pltpu.VMEM)
    return pl.pallas_call(
        stem_kernel,
        in_specs=[vmem] * 4 + [hbm] * 4,
        out_specs=(vmem, vmem, vmem),
        out_shape=(
            jax.ShapeDtypeStruct((128, DM), BF),
            jax.ShapeDtypeStruct((64, CHUNK, 128), BF),
            jax.ShapeDtypeStruct((64, CHUNK, 128), BF),
        ),
        scratch_shapes=[
            pltpu.VMEM((4, 2, ZW, 256), F32),
            pltpu.VMEM((2, 256, 128), F32),
            pltpu.VMEM((128, 4096), BF),
            pltpu.VMEM((4096, DM), BF),
            pltpu.VMEM((DM, DM), BF),
            pltpu.VMEM((DM, DM), BF),
            pltpu.VMEM((DM, DM), BF),
            pltpu.SemaphoreType.DMA((4,)),
        ],
        compiler_params=pltpu.CompilerParams(vmem_limit_bytes=28 << 20),
        name="stem",
    )(halo, conv_weight, cotangent, inside, patch_weight, query_weight, key_weight, value_weight)


def local(
    features,
    neighbours,
    conv_weight,
    patch_weight,
    query_weight,
    key_weight,
    value_weight,
    output_weight,
    cotangent,
):
    _, inner = split_device(lax.axis_index("tile"))
    faces = gather_faces(in_hbm(neighbours), in_hbm(features))
    faces, inner = lax.optimization_barrier((faces, inner))
    faces = swap(faces, INNER).reshape(16, HALO, 256)
    tiles = faces[:, 128, :8].astype(jnp.int32)
    outer, goal = split_device(tiles >> 1)
    targets = jnp.where((tiles < 128) & (goal == inner), (outer & 7) * 2 + (tiles & 1), -1)
    routed, taps = lax.optimization_barrier((route(targets, faces), conv_weight.reshape(9, 256, 256)))
    halo = swap(routed, OUTER).reshape(8, 2, HALO, 256)
    inside = conv_inside(features, taps)
    tokens, packed, rest = stem(
        halo,
        taps,
        cotangent,
        inside,
        in_hbm(patch_weight),
        in_hbm(query_weight),
        in_hbm(key_weight),
        in_hbm(value_weight),
    )
    packed = swap(packed)
    packed, rest = lax.optimization_barrier((packed, rest))
    rest = swap(rest)
    parts = swap(attend_single(rest, *attend_pair(packed)), KEY_GROUPS)
    att, grad = merge(parts, rest)
    terms = swap(grad.reshape(16, SHARE, 128), HEAD_GROUPS)
    received = swap(share_out(terms, att))
    return finish(received, tokens, output_weight)


def solution(mesh):
    in_specs = (
        P(("slide", "tile"), None, None, None),
        P(("slide", "tile"), None),
        P(),
        P(),
        P(),
        P(),
        P(),
        P(),
        P(("slide", "tile"), None),
    )
    out_specs = (P(("slide", "tile"), None), P("slide", None))
    return jax.shard_map(local, mesh=mesh, in_specs=in_specs, out_specs=out_specs, check_vma=False)
```

```python
import jax
import jax.numpy as jnp
from jax import lax
from jax.experimental import pallas as pl
from jax.experimental.pallas import tpu as pltpu
from jax.sharding import PartitionSpec as P

PATCH = 4
HEADS = 12
HD = 64
DM = 768
SPLIT = 4
HG = HEADS // SPLIT
GW = HG * HD
BLK = 32
CHUNK = 96
PARTS = 512 + 256 + 64
FACES = 128
HALO = 264
BF = jnp.bfloat16
F32 = jnp.float32


def hi_bit(coord):
    return coord >> 1


def lo_bit(coord):
    return (coord ^ (coord >> 1)) & 1


def split_device(dev):
    z, y, x = dev >> 4, (dev >> 2) & 3, dev & 3
    outer = hi_bit(z) * 4 + hi_bit(y) * 2 + hi_bit(x)
    inner = lo_bit(z) * 4 + lo_bit(y) * 2 + lo_bit(x)
    return outer, inner


def device_groups():
    place = {}
    for dev in range(64):
        place[split_device(dev)] = dev
    inner_groups = [[place[(a, b)] for b in range(8)] for a in range(8)]
    outer_groups = [[place[(a, b)] for a in range(8)] for b in range(8)]
    return inner_groups, outer_groups


INNER, OUTER = device_groups()


def place(h, a, b):
    def coord(hi, lo):
        return hi * 2 + (hi ^ lo)

    return coord(a >> 1, b >> 1) * 16 + coord(a & 1, b & 1) * 4 + h


KEY_GROUPS = [[place(h, a, b) for b in range(SPLIT)] for h in range(SPLIT) for a in range(SPLIT)]
HEAD_GROUPS = [[place(h, a, b) for a in range(SPLIT) for b in range(SPLIT)] for h in range(SPLIT)]


def in_hbm(x):
    return pltpu.with_memory_space_constraint(x, pltpu.HBM)


def swap(x, groups=None):
    return lax.all_to_all(
        x, "tile", split_axis=0, concat_axis=0, tiled=True, axis_index_groups=groups
    )


def faces_kernel(links_ref, features_hbm, out_ref, sides_ref, cols_ref, faces_ref, sems):
    loads = []
    for t in range(2):
        for n, y in enumerate((0, 31)):
            loads.append((features_hbm.at[t, y], faces_ref.at[t, n * 32 : n * 32 + 32]))
        for n, x in enumerate((0, 24)):
            loads.append((features_hbm.at[t, :, x : x + 8], sides_ref.at[t, n]))
    loads = [pltpu.make_async_copy(src, dst, sems.at[n]) for n, (src, dst) in enumerate(loads)]
    for load in loads:
        load.start()
    for load in loads:
        load.wait()
    lanes = lax.broadcasted_iota(jnp.int32, (8, 128), 1)
    subs = lax.broadcasted_iota(jnp.int32, (8, 128), 0)
    for t in range(2):
        for n, x in enumerate((0, 7)):
            for lt in range(2):
                cols_ref[...] = sides_ref[t, n, :, :, lt * 128 : lt * 128 + 128].astype(F32).reshape(256, 128)
                faces_ref[t, 64 + n * 32 : 96 + n * 32, lt * 128 : lt * 128 + 128] = cols_ref[
                    pl.ds(x, 32, stride=8), :
                ].astype(BF)
    for t in range(2):
        row = faces_ref[t, 64:72, :128].astype(F32)
        for d in range(8):
            row = jnp.where((lanes == d) & (subs == 0), links_ref[t, d].astype(F32), row)
        faces_ref[t, 64:72, :128] = row.astype(BF)
    for n in range(8):
        out_ref[n] = faces_ref[...]


def gather_faces(links, features):
    hbm = pl.BlockSpec(memory_space=pltpu.HBM)
    return pl.pallas_call(
        faces_kernel,
        in_specs=[pl.BlockSpec(memory_space=pltpu.SMEM), hbm],
        out_specs=pl.BlockSpec(memory_space=pltpu.VMEM),
        out_shape=jax.ShapeDtypeStruct((8, 2, FACES, 256), BF),
        scratch_shapes=[
            pltpu.VMEM((2, 2, 32, 8, 256), BF),
            pltpu.VMEM((256, 128), F32),
            pltpu.VMEM((2, FACES, 256), BF),
            pltpu.SemaphoreType.DMA((8,)),
        ],
        compiler_params=pltpu.CompilerParams(vmem_limit_bytes=6 << 20),
        name="faces",
    )(links, features)


EDGES = {1: (0, 32), 6: (32, 0), 3: (64, 96), 4: (96, 64)}
CORNERS = {0: (0, 3), 2: (31, 2), 5: (32, 1), 7: (63, 0)}


def route_kernel(targets_ref, faces_ref, out_ref):
    out_ref[...] = jnp.zeros(out_ref.shape, BF)
    row_ids = lax.broadcasted_iota(jnp.int32, (8, 256), 0)

    def per_tile(src, carry):
        for direction in range(8):
            target = targets_ref[src, direction]

            @pl.when(target >= 0)
            def _():
                outer, slot = target >> 1, target & 1
                if direction in EDGES:
                    first, dest = EDGES[direction]
                    row = pl.multiple_of(slot * FACES + dest, 32)
                    out_ref[outer, pl.ds(row, 32), :] = faces_ref[src, first : first + 32, :]
                    if direction == 3:
                        tile = faces_ref[src, first : first + 8, :].astype(F32)
                        cell = faces_ref[src, 0:8, :].astype(F32)
                        out_ref[outer, pl.ds(row, 8), :] = jnp.where(row_ids == 0, cell, tile).astype(BF)
                else:
                    row, dest = CORNERS[direction]
                    base = row // 8 * 8
                    cell = faces_ref[src, base : base + 8, :].astype(F32)[row - base : row - base + 1, :]
                    old = out_ref[outer, 2 * FACES :, :].astype(F32)
                    new = jnp.where(row_ids == slot * 4 + dest, jnp.broadcast_to(cell, (8, 256)), old)
                    out_ref[outer, 2 * FACES :, :] = new.astype(BF)

        return carry

    lax.fori_loop(0, 16, per_tile, 0)


def route(targets, faces):
    vmem = pl.BlockSpec(memory_space=pltpu.VMEM)
    return pl.pallas_call(
        route_kernel,
        in_specs=[pl.BlockSpec(memory_space=pltpu.SMEM), vmem],
        out_specs=vmem,
        out_shape=jax.ShapeDtypeStruct((8, HALO, 256), BF),
        compiler_params=pltpu.CompilerParams(vmem_limit_bytes=8 << 20),
        name="route",
    )(targets, faces)


def attend_heads(units):
    scores = [
        lax.dot_general(q * BF(HD ** -0.5), k, (((1,), (1,)), ((), ())), preferred_element_type=F32)
        for q, k, _ in units
    ]
    results = []
    for score, (_, _, value) in zip(scores, units):
        top = jnp.max(score, axis=1, keepdims=True)
        weights = jnp.exp(score - top).astype(BF)
        res = jnp.dot(weights, value, preferred_element_type=F32)
        total = res[:, HD : HD + 1]
        lse = top + jnp.log(total)
        one = lse.astype(BF).astype(F32)
        two = (lse - one).astype(BF).astype(F32)
        results.append((res[:, :HD] / total, (one, two, lse - one - two)))
    return results


def put_rows(row_ref, out_ref, first):
    for n in range(row_ref.shape[0] // BLK):
        for b in range(SPLIT):
            row = n * BLK + b * 8
            out_ref[b, first + n * 8 : first + n * 8 + 8, :] = row_ref[row : row + 8, :].astype(BF)


UNIT = 8


def pair_kernel(in_ref, all_ref, out_ref, lse_ref, key_ref, val_ref, row_ref, tail_ref):
    step = pl.program_id(0)

    @pl.when(step == 0)
    def _():
        ones = jnp.where(lax.broadcasted_iota(jnp.int32, (2048, HD), 1) == 0, 1.0, 0.0).astype(BF)
        for g in range(2):
            key_ref[g] = all_ref[:, 32:64, g * HD : (g + 1) * HD].reshape(2048, HD)
            val_ref[g, :, :HD] = all_ref[:, 64:96, g * HD : (g + 1) * HD].reshape(2048, HD)
            val_ref[g, :, HD:] = ones
        tail_ref[...] = jnp.zeros(tail_ref.shape, F32)

    count = in_ref.shape[0] // UNIT
    units = []
    for n in range(count):
        for g in range(2):
            query = in_ref[n * UNIT : (n + 1) * UNIT, :BLK, g * HD : (g + 1) * HD].reshape(UNIT * BLK, HD)
            units.append((query, key_ref[g], val_ref[g]))
    results = attend_heads(units)
    lanes = lax.broadcasted_iota(jnp.int32, tail_ref.shape, 1)
    tail = tail_ref[...]
    for n in range(count):
        rows = slice(n * UNIT * BLK, (n + 1) * UNIT * BLK)
        for g in range(2):
            out, parts = results[2 * n + g]
            row_ref[rows, g * HD : (g + 1) * HD] = out
            for i, part in enumerate(parts):
                tail = jnp.where(lanes == 16 * (step * count + n) + 3 * g + i, part, tail)
    tail_ref[...] = tail
    put_rows(row_ref, out_ref, 0)
    put_rows(tail_ref, lse_ref, 0)


def single_kernel(all_ref, part_ref, lse_ref, out_ref, key_ref, val_ref, row_ref, tail_ref):
    ones = jnp.where(lax.broadcasted_iota(jnp.int32, (2048, HD), 1) == 0, 1.0, 0.0).astype(BF)
    val_ref[:, HD:] = ones
    for g in range(2):
        rows = slice(g * 1024, (g + 1) * 1024)
        key_ref[rows, :] = all_ref[:, g * 16 : g * 16 + 16, HD:].reshape(1024, HD)
        val_ref[rows, :HD] = all_ref[:, 32:48, g * HD : (g + 1) * HD].reshape(1024, HD)

    count = 64 // UNIT
    units = []
    for n in range(count):
        query = all_ref[n * UNIT : (n + 1) * UNIT, :BLK, :HD].reshape(UNIT * BLK, HD)
        units.append((query, key_ref[...], val_ref[...]))
    results = attend_heads(units)
    lanes = lax.broadcasted_iota(jnp.int32, tail_ref.shape, 1)
    tail = jnp.zeros(tail_ref.shape, F32)
    for n, (out, parts) in enumerate(results):
        first = n % (count // 2) * UNIT * BLK
        lane = n // (count // 2) * HD
        row_ref[first : first + UNIT * BLK, lane : lane + HD] = out
        for i, part in enumerate(parts):
            tail = jnp.where(lanes == 16 * n + 6 + i, part, tail)
    tail_ref[...] = tail
    for b in range(SPLIT):
        out_ref[b, :512, :] = part_ref[b]
    put_rows(row_ref, out_ref, 512)
    for n in range(UNIT):
        for b in range(SPLIT):
            row = n * BLK + b * 8
            new = lse_ref[b, n * 8 : n * 8 + 8, :].astype(F32) + tail_ref[row : row + 8, :]
            out_ref[b, 768 + n * 8 : 776 + n * 8, :] = new.astype(BF)


def attend_pair(packed):
    srcs = 32
    return pl.pallas_call(
        pair_kernel,
        grid=(64 // srcs,),
        in_specs=[
            pl.BlockSpec((srcs, CHUNK, 128), lambda i: (i, 0, 0)),
            pl.BlockSpec((64, CHUNK, 128), lambda i: (0, 0, 0)),
        ],
        out_specs=(
            pl.BlockSpec((SPLIT, srcs * 8, 128), lambda i: (0, i, 0)),
            pl.BlockSpec((SPLIT, 64, 128), lambda i: (0, 0, 0)),
        ),
        out_shape=(pltpu.HBM((SPLIT, 512, 128), BF), pltpu.HBM((SPLIT, 64, 128), BF)),
        scratch_shapes=[
            pltpu.VMEM((2, 2048, HD), BF),
            pltpu.VMEM((2, 2048, 2 * HD), BF),
            pltpu.VMEM((srcs * BLK, 128), F32),
            pltpu.VMEM((UNIT * BLK, 128), F32),
        ],
        compiler_params=pltpu.CompilerParams(vmem_limit_bytes=38 << 20),
        name="attend_pair",
    )(packed, packed)


def attend_single(rest, parts, lses):
    vmem = pl.BlockSpec(memory_space=pltpu.VMEM)
    return pl.pallas_call(
        single_kernel,
        in_specs=[vmem] * 3,
        out_specs=vmem,
        out_shape=jax.ShapeDtypeStruct((SPLIT, PARTS, 128), BF),
        scratch_shapes=[
            pltpu.VMEM((2048, HD), BF),
            pltpu.VMEM((2048, 2 * HD), BF),
            pltpu.VMEM((1024, 128), F32),
            pltpu.VMEM((UNIT * BLK, 128), F32),
        ],
        compiler_params=pltpu.CompilerParams(vmem_limit_bytes=38 << 20),
        name="attend_single",
    )(rest, in_hbm(parts), in_hbm(lses))


SHARE = 72
ROWS = SHARE + 16


def merge_kernel(parts_ref, rest_ref, att_ref, grad_ref, pair_ref, single_ref, cot_ref):
    for c in range(DM // 128):
        cot_ref[:, c * 128 : (c + 1) * 128] = rest_ref[:, 48 + 8 * c : 56 + 8 * c, :].reshape(512, 128)
    tails = []
    for b in range(SPLIT):
        tile = parts_ref[b, 768:, :].astype(F32)
        tail = jnp.concatenate([tile] + [pltpu.roll(tile, 128 - 16 * j, 1) for j in range(1, 8)], axis=0)
        tails.append(tail + pltpu.roll(tail, 127, 1) + pltpu.roll(tail, 126, 1))
    top = jnp.maximum(jnp.maximum(tails[0], tails[1]), jnp.maximum(tails[2], tails[3]))
    ws = [jnp.exp(tail - top) for tail in tails]
    inverse = 1.0 / (ws[0] + ws[1] + ws[2] + ws[3])
    low = lax.broadcasted_iota(jnp.int32, (512, 128), 1) < HD
    pair = jnp.zeros((512, 128), F32)
    folded = jnp.zeros((256, 128), F32)
    for b in range(SPLIT):
        share = ws[b] * inverse
        w0, w1, w2 = (share[:, 3 * g : 3 * g + 1] for g in range(HG))
        pair = pair + jnp.where(low, w0, w1) * parts_ref[b, :512, :].astype(F32)
        folded = folded + jnp.where(low[:256], w2[:256], w2[256:]) * parts_ref[b, 512:768, :].astype(F32)
    single = jnp.where(low, jnp.concatenate([folded, pltpu.roll(folded, HD, 1)], axis=0), 0.0)
    pair_ref[...] = pair.astype(BF)
    single_ref[...] = single.astype(BF)
    for n in range(64):
        att_ref[n, :8, :] = pair[n * 8 : n * 8 + 8].astype(BF)
        att_ref[n, 8:, :] = single[n * 8 : n * 8 + 8].astype(BF)
    for first, ref, count in ((0, pair_ref, 128), (128, single_ref, 64)):
        grad = lax.dot_general(
            ref[...], cot_ref[...], (((0,), (0,)), ((), ())), preferred_element_type=F32
        )
        for c in range(DM // 128):
            grad_ref[c, first : first + count, :] = grad[:count, c * 128 : (c + 1) * 128].astype(BF)


def merge(parts, rest):
    return pl.pallas_call(
        merge_kernel,
        out_shape=(
            jax.ShapeDtypeStruct((64, 16, 128), BF),
            jax.ShapeDtypeStruct((DM // 128, GW, 128), BF),
        ),
        scratch_shapes=[pltpu.VMEM((512, 128), BF), pltpu.VMEM((512, 128), BF), pltpu.VMEM((512, DM), BF)],
        compiler_params=pltpu.CompilerParams(vmem_limit_bytes=16 << 20),
        name="merge",
    )(parts, rest)


def share_kernel(terms_ref, att_ref, out_ref, total_ref):
    @pl.when(pl.program_id(0) == 0)
    def _():
        total = terms_ref[0].astype(F32)
        for n in range(1, 16):
            total = total + terms_ref[n].astype(F32)
        total_ref[...] = total.astype(BF)

    for n in range(out_ref.shape[0]):
        out_ref[n, :SHARE, :] = total_ref[...]
        out_ref[n, SHARE:, :] = att_ref[n]


def share_out(terms, att):
    step = 16
    return pl.pallas_call(
        share_kernel,
        grid=(64 // step,),
        in_specs=[
            pl.BlockSpec((16, SHARE, 128), lambda i: (0, 0, 0)),
            pl.BlockSpec((step, 16, 128), lambda i: (i, 0, 0)),
        ],
        out_specs=pl.BlockSpec((step, ROWS, 128), lambda i: (i, 0, 0)),
        out_shape=jax.ShapeDtypeStruct((64, ROWS, 128), BF),
        scratch_shapes=[pltpu.VMEM((SHARE, 128), BF)],
        compiler_params=pltpu.CompilerParams(vmem_limit_bytes=8 << 20),
        name="share",
    )(terms, att)


def finish_kernel(all_ref, tokens_ref, weight_ref, mixed_ref, grad_hbm, att_ref, grad_ref, sems):
    copies = []
    for h in range(SPLIT):
        for m in range(16):
            at = place(h, m // SPLIT, m % SPLIT)
            done = 0
            while done < SHARE:
                block, row = divmod(m * SHARE + done, GW)
                count = min(SHARE - done, (128 if row < 128 else GW) - row)
                dest = h * 128 + row if row < 128 else 512 + h * HD + row - 128
                grad_ref[dest : dest + count, block * 128 : (block + 1) * 128] = all_ref[
                    at, done : done + count, :
                ].astype(F32)
                done += count
        for n, (first, count) in enumerate(((h * 128, 128), (512 + h * HD, HD))):
            rows = slice(first, first + count)
            copy = pltpu.make_async_copy(grad_ref.at[rows], grad_hbm.at[rows], sems.at[2 * h + n])
            copy.start()
            copies.append(copy)
    lanes = lax.broadcasted_iota(jnp.int32, (8, 128), 1) < HD
    for a in range(SPLIT):
        for b in range(SPLIT):
            row = a * BLK + b * 8
            for h in range(SPLIT):
                att_ref[row : row + 8, h * 128 : (h + 1) * 128] = all_ref[place(h, a, b), SHARE : SHARE + 8, :]
            for h in range(0, SPLIT, 2):
                even = all_ref[place(h, a, b), SHARE + 8 :, :].astype(F32)
                odd = pltpu.roll(all_ref[place(h + 1, a, b), SHARE + 8 :, :].astype(F32), HD, 1)
                first = 512 + h * HD
                att_ref[row : row + 8, first : first + 128] = jnp.where(lanes, even, odd).astype(BF)
    mixed_ref[...] = (
        tokens_ref[...].astype(F32) + jnp.dot(att_ref[...], weight_ref[...], preferred_element_type=F32)
    ).astype(BF)
    for copy in copies:
        copy.wait()


def finish(received, tokens, weight):
    vmem = pl.BlockSpec(memory_space=pltpu.VMEM)
    return pl.pallas_call(
        finish_kernel,
        in_specs=[vmem] * 3,
        out_specs=(vmem, pl.BlockSpec(memory_space=pl.ANY)),
        out_shape=(
            jax.ShapeDtypeStruct((128, DM), BF),
            jax.ShapeDtypeStruct((DM, DM), F32),
        ),
        scratch_shapes=[
            pltpu.VMEM((128, DM), BF),
            pltpu.VMEM((DM, DM), F32),
            pltpu.SemaphoreType.DMA((8,)),
        ],
        compiler_params=pltpu.CompilerParams(vmem_limit_bytes=12 << 20),
        name="finish",
    )(received, tokens, weight)


ZW = 48
Z0 = 8


def conv_kernel(features_ref, conv_ref, out_ref, left_ref, right_ref):
    for t in range(2):
        for y in range(32):
            for lt in range(2):
                slot = (t * 32 + y) * ZW
                left_ref[lt, slot : slot + Z0, :] = jnp.zeros((Z0, 128), F32)
                right_ref[lt, slot + Z0 + 32 : slot + ZW, :] = jnp.zeros((Z0, 128), F32)
        for y in range(0, 32, 8):
            zero = jnp.zeros((32, 256), BF)
            accs = []
            for dx in range(3):
                acc = jnp.zeros((256, 256), F32)
                for dy in range(3):
                    first = y + dy - 1
                    if first < 0:
                        rows = jnp.concatenate([zero, features_ref[t, :7].reshape(224, 256)], axis=0)
                    elif first + 8 > 32:
                        rows = jnp.concatenate([features_ref[t, first:].reshape(224, 256), zero], axis=0)
                    else:
                        rows = features_ref[t, first : first + 8].reshape(256, 256)
                    acc = acc + jnp.dot(rows, conv_ref[dy * 3 + dx], preferred_element_type=F32)
                accs.append(acc)
            for n in range(8):
                slot = (t * 32 + y + n) * ZW + Z0
                row = (t * 32 + y + n) * 32
                for lt in range(2):
                    part = (slice(n * 32, n * 32 + 32), slice(lt * 128, lt * 128 + 128))
                    left_ref[lt, slot : slot + 32, :] = accs[0][part]
                    right_ref[lt, slot : slot + 32, :] = accs[2][part]
                    out_ref[lt, row : row + 32, :] = (
                        accs[1][part]
                        + left_ref[lt, slot - 1 : slot + 31, :]
                        + right_ref[lt, slot + 1 : slot + 33, :]
                    )


def conv_inside(features, taps):
    vmem = pl.BlockSpec(memory_space=pltpu.VMEM)
    return pl.pallas_call(
        conv_kernel,
        in_specs=[vmem, vmem],
        out_specs=vmem,
        out_shape=jax.ShapeDtypeStruct((2, 2048, 128), F32),
        scratch_shapes=[pltpu.VMEM((2, 64 * ZW, 128), F32), pltpu.VMEM((2, 64 * ZW, 128), F32)],
        compiler_params=pltpu.CompilerParams(vmem_limit_bytes=16 << 20),
        name="conv_inside",
    )(features, taps)


def stem_kernel(
    halo_ref,
    conv_ref,
    cot_ref,
    inside_ref,
    patch_hbm,
    query_hbm,
    key_hbm,
    value_hbm,
    tokens_ref,
    packed_ref,
    rest_ref,
    side_ref,
    edge_ref,
    hid_ref,
    patch_ref,
    wq_ref,
    wk_ref,
    wv_ref,
    sems,
):
    pairs = [(patch_hbm.at[r * 1024 : r * 1024 + 1024], patch_ref.at[r * 1024 : r * 1024 + 1024]) for r in range(4)]
    pairs += [(query_hbm, wq_ref), (key_hbm, wk_ref), (value_hbm, wv_ref)]
    loads = [pltpu.make_async_copy(src, dst, sems.at[n]) for n, (src, dst) in enumerate(pairs)]
    for load in loads:
        load.start()

    def halo_rows(t, first, count):
        first = t * FACES + first
        total = halo_ref[0, first : first + count, :].astype(F32)
        for n in range(1, 8):
            total = total + halo_ref[n, first : first + count, :].astype(F32)
        return total

    corner = halo_rows(2, 0, 8)
    for t in range(2):
        for side in range(4):
            side_ref[side, t, Z0 : Z0 + 32, :] = halo_rows(t, 32 * side, 32)
            for end, row in enumerate((Z0 - 1, Z0 + 32)):
                if side < 2:
                    cell = corner[t * 4 + side * 2 + end : t * 4 + side * 2 + end + 1]
                else:
                    cell = jnp.zeros((1, 256), F32)
                side_ref[side, t, row : row + 1, :] = cell
    for side in range(4):
        edge = jnp.zeros((64, 256), F32)
        for k in range(3):
            part = jnp.concatenate(
                [side_ref[side, t, Z0 - 1 + k : Z0 + 31 + k, :].astype(BF) for t in range(2)], axis=0
            )
            tap = (k, 6 + k, 3 * k, 3 * k + 2)[side]
            edge = edge + jnp.dot(part, conv_ref[tap], preferred_element_type=F32)
        for lt in range(2):
            edge_ref[lt, side * 64 : side * 64 + 64, :] = edge[:, lt * 128 : lt * 128 + 128]

    sub = lax.broadcasted_iota(jnp.int32, (8, 128), 0)
    embedded = jnp.zeros((128, DM), F32)
    for r in range(4):
        for c in range(4):
            for t in range(2):
                for pr in range(8):
                    y = pr * 4 + r
                    row = (t * 8 + pr) * 8
                    for lt in range(2):
                        total = inside_ref[lt, pl.ds((t * 32 + y) * 32 + c, 8, stride=4), :]
                        if y == 0:
                            total = total + edge_ref[lt, pl.ds(t * 32 + c, 8, stride=4), :]
                        if y == 31:
                            total = total + edge_ref[lt, pl.ds(64 + t * 32 + c, 8, stride=4), :]
                        if c == 0 or c == 3:
                            at = (128 if c == 0 else 192) + t * 32 + y
                            cell = jnp.broadcast_to(edge_ref[lt, at : at + 1, :], (8, 128))
                            total = total + jnp.where(sub == (0 if c == 0 else 7), cell, 0.0)
                        col = (r * 4 + c) * 256 + lt * 128
                        hid_ref[row : row + 8, col : col + 128] = jax.nn.gelu(total).astype(BF)
        loads[r].wait()
        part = slice(r * 1024, r * 1024 + 1024)
        embedded = embedded + jnp.dot(hid_ref[:, part], patch_ref[part, :], preferred_element_type=F32)
    tokens = embedded.astype(BF)
    tokens_ref[...] = tokens
    for load in loads[4:]:
        load.wait()
    query = jnp.dot(tokens, wq_ref[...], preferred_element_type=F32)
    keys = jnp.dot(tokens, wk_ref[...], preferred_element_type=F32)
    values = jnp.dot(tokens, wv_ref[...], preferred_element_type=F32)
    low = lax.broadcasted_iota(jnp.int32, (128, 128), 1) < HD

    def pair_of(x, h):
        return x[:, h * 128 : (h + 1) * 128]

    for h in range(SPLIT):
        one = 4 + h // 2
        q1, k1, v1 = pair_of(query, one), pair_of(keys, one), pair_of(values, one)
        if h % 2 == 0:
            k1 = pltpu.roll(k1, HD, 1)
            v2 = pltpu.roll(v1, HD, 1)
        else:
            q1 = pltpu.roll(q1, HD, 1)
            v2 = v1
            v1 = pltpu.roll(v1, HD, 1)
        pieces = (pair_of(query, h).astype(BF), pair_of(keys, h).astype(BF), pair_of(values, h).astype(BF))
        for a in range(SPLIT):
            for b in range(SPLIT):
                at = place(h, a, b)
                qa, kb = slice(a * BLK, (a + 1) * BLK), slice(b * BLK, (b + 1) * BLK)
                packed_ref[at, 0:32, :] = pieces[0][qa]
                packed_ref[at, 32:64, :] = pieces[1][kb]
                packed_ref[at, 64:96, :] = pieces[2][kb]
                rest_ref[at, 0:32, :] = jnp.where(low[:BLK], q1[qa], k1[kb]).astype(BF)
                half = b * BLK + BLK // 2
                rest_ref[at, 32:48, :] = jnp.where(
                    low[: BLK // 2], v1[b * BLK : half], v2[half : (b + 1) * BLK]
                ).astype(BF)
                row = a * BLK + b * 8
                for c in range(DM // 128):
                    rest_ref[at, 48 + 8 * c : 56 + 8 * c, :] = cot_ref[row : row + 8, c * 128 : (c + 1) * 128]


def stem(halo, conv_weight, cotangent, inside, patch_weight, query_weight, key_weight, value_weight):
    hbm = pl.BlockSpec(memory_space=pl.ANY)
    vmem = pl.BlockSpec(memory_space=pltpu.VMEM)
    return pl.pallas_call(
        stem_kernel,
        in_specs=[vmem] * 4 + [hbm] * 4,
        out_specs=(vmem, vmem, vmem),
        out_shape=(
            jax.ShapeDtypeStruct((128, DM), BF),
            jax.ShapeDtypeStruct((64, CHUNK, 128), BF),
            jax.ShapeDtypeStruct((64, CHUNK, 128), BF),
        ),
        scratch_shapes=[
            pltpu.VMEM((4, 2, ZW, 256), F32),
            pltpu.VMEM((2, 256, 128), F32),
            pltpu.VMEM((128, 4096), BF),
            pltpu.VMEM((4096, DM), BF),
            pltpu.VMEM((DM, DM), BF),
            pltpu.VMEM((DM, DM), BF),
            pltpu.VMEM((DM, DM), BF),
            pltpu.SemaphoreType.DMA((7,)),
        ],
        compiler_params=pltpu.CompilerParams(vmem_limit_bytes=28 << 20),
        name="stem",
    )(halo, conv_weight, cotangent, inside, patch_weight, query_weight, key_weight, value_weight)


def local(
    features,
    neighbours,
    conv_weight,
    patch_weight,
    query_weight,
    key_weight,
    value_weight,
    output_weight,
    cotangent,
):
    _, inner = split_device(lax.axis_index("tile"))
    faces = gather_faces(in_hbm(neighbours), in_hbm(features))
    faces, inner = lax.optimization_barrier((faces, inner))
    faces = swap(faces, INNER).reshape(16, FACES, 256)
    tiles = faces[:, 64, :8].astype(jnp.int32)
    outer, goal = split_device(tiles >> 1)
    targets = jnp.where((tiles < 128) & (goal == inner), (outer & 7) * 2 + (tiles & 1), -1)
    routed, taps = lax.optimization_barrier((route(targets, faces), conv_weight.reshape(9, 256, 256)))
    halo = swap(routed, OUTER)
    inside = conv_inside(features, taps)
    tokens, packed, rest = stem(
        halo,
        taps,
        cotangent,
        inside,
        in_hbm(patch_weight),
        in_hbm(query_weight),
        in_hbm(key_weight),
        in_hbm(value_weight),
    )
    packed = swap(packed)
    packed, rest = lax.optimization_barrier((packed, rest))
    rest = swap(rest)
    parts = swap(attend_single(rest, *attend_pair(packed)), KEY_GROUPS)
    att, grad = merge(parts, rest)
    terms = swap(grad.reshape(16, SHARE, 128), HEAD_GROUPS)
    received = swap(share_out(terms, att))
    return finish(received, tokens, output_weight)


def solution(mesh):
    in_specs = (
        P(("slide", "tile"), None, None, None),
        P(("slide", "tile"), None),
        P(),
        P(),
        P(),
        P(),
        P(),
        P(),
        P(("slide", "tile"), None),
    )
    out_specs = (P(("slide", "tile"), None), P("slide", None))
    return jax.shard_map(local, mesh=mesh, in_specs=in_specs, out_specs=out_specs, check_vma=False)
```

```python
import jax
import jax.numpy as jnp
from jax import lax
from jax.experimental import pallas as pl
from jax.experimental.pallas import tpu as pltpu
from jax.sharding import PartitionSpec as P

PATCH = 4
HEADS = 12
HD = 64
DM = 768
SPLIT = 4
HG = HEADS // SPLIT
GW = HG * HD
BLK = 32
CHUNK = 96
PARTS = 512 + 256 + 64
FACES = 128
HALO = 264
BF = jnp.bfloat16
F32 = jnp.float32


def hi_bit(coord):
    return coord >> 1


def lo_bit(coord):
    return (coord ^ (coord >> 1)) & 1


def split_device(dev):
    z, y, x = dev >> 4, (dev >> 2) & 3, dev & 3
    outer = hi_bit(z) * 4 + hi_bit(y) * 2 + hi_bit(x)
    inner = lo_bit(z) * 4 + lo_bit(y) * 2 + lo_bit(x)
    return outer, inner


def device_groups():
    place = {}
    for dev in range(64):
        place[split_device(dev)] = dev
    inner_groups = [[place[(a, b)] for b in range(8)] for a in range(8)]
    outer_groups = [[place[(a, b)] for a in range(8)] for b in range(8)]
    return inner_groups, outer_groups


INNER, OUTER = device_groups()


def place(h, a, b):
    def coord(hi, lo):
        return hi * 2 + (hi ^ lo)

    return coord(a >> 1, b >> 1) * 16 + coord(a & 1, b & 1) * 4 + h


KEY_GROUPS = [[place(h, a, b) for b in range(SPLIT)] for h in range(SPLIT) for a in range(SPLIT)]
HEAD_GROUPS = [[place(h, a, b) for a in range(SPLIT) for b in range(SPLIT)] for h in range(SPLIT)]


def in_hbm(x):
    return pltpu.with_memory_space_constraint(x, pltpu.HBM)


def swap(x, groups=None):
    return lax.all_to_all(
        x, "tile", split_axis=0, concat_axis=0, tiled=True, axis_index_groups=groups
    )


def faces_kernel(links_ref, features_hbm, out_ref, sides_ref, cols_ref, faces_ref, sems):
    loads = []
    for t in range(2):
        for n, y in enumerate((0, 31)):
            loads.append((features_hbm.at[t, y], faces_ref.at[t, n * 32 : n * 32 + 32]))
        for n, x in enumerate((0, 24)):
            loads.append((features_hbm.at[t, :, x : x + 8], sides_ref.at[t, n]))
    loads = [pltpu.make_async_copy(src, dst, sems.at[n]) for n, (src, dst) in enumerate(loads)]
    for load in loads:
        load.start()
    for load in loads:
        load.wait()
    lanes = lax.broadcasted_iota(jnp.int32, (8, 128), 1)
    subs = lax.broadcasted_iota(jnp.int32, (8, 128), 0)
    for t in range(2):
        for n, x in enumerate((0, 7)):
            for lt in range(2):
                cols_ref[...] = sides_ref[t, n, :, :, lt * 128 : lt * 128 + 128].astype(F32).reshape(256, 128)
                faces_ref[t, 64 + n * 32 : 96 + n * 32, lt * 128 : lt * 128 + 128] = cols_ref[
                    pl.ds(x, 32, stride=8), :
                ].astype(BF)
    for t in range(2):
        row = faces_ref[t, 64:72, :128].astype(F32)
        for d in range(8):
            row = jnp.where((lanes == d) & (subs == 0), links_ref[t, d].astype(F32), row)
        faces_ref[t, 64:72, :128] = row.astype(BF)
    for n in range(8):
        out_ref[n] = faces_ref[...]


def gather_faces(links, features):
    hbm = pl.BlockSpec(memory_space=pltpu.HBM)
    return pl.pallas_call(
        faces_kernel,
        in_specs=[pl.BlockSpec(memory_space=pltpu.SMEM), hbm],
        out_specs=pl.BlockSpec(memory_space=pltpu.VMEM),
        out_shape=jax.ShapeDtypeStruct((8, 2, FACES, 256), BF),
        scratch_shapes=[
            pltpu.VMEM((2, 2, 32, 8, 256), BF),
            pltpu.VMEM((256, 128), F32),
            pltpu.VMEM((2, FACES, 256), BF),
            pltpu.SemaphoreType.DMA((8,)),
        ],
        compiler_params=pltpu.CompilerParams(vmem_limit_bytes=6 << 20),
        name="faces",
    )(links, features)


EDGES = {1: (0, 32), 6: (32, 0), 3: (64, 96), 4: (96, 64)}
CORNERS = {0: (0, 3), 2: (31, 2), 5: (32, 1), 7: (63, 0)}


def route_kernel(targets_ref, faces_ref, out_ref):
    out_ref[...] = jnp.zeros(out_ref.shape, BF)
    row_ids = lax.broadcasted_iota(jnp.int32, (8, 256), 0)

    def per_tile(src, carry):
        for direction in range(8):
            target = targets_ref[src, direction]

            @pl.when(target >= 0)
            def _():
                outer, slot = target >> 1, target & 1
                if direction in EDGES:
                    first, dest = EDGES[direction]
                    row = pl.multiple_of(slot * FACES + dest, 32)
                    out_ref[outer, pl.ds(row, 32), :] = faces_ref[src, first : first + 32, :]
                    if direction == 3:
                        tile = faces_ref[src, first : first + 8, :].astype(F32)
                        cell = faces_ref[src, 0:8, :].astype(F32)
                        out_ref[outer, pl.ds(row, 8), :] = jnp.where(row_ids == 0, cell, tile).astype(BF)
                else:
                    row, dest = CORNERS[direction]
                    base = row // 8 * 8
                    cell = faces_ref[src, base : base + 8, :].astype(F32)[row - base : row - base + 1, :]
                    old = out_ref[outer, 2 * FACES :, :].astype(F32)
                    new = jnp.where(row_ids == slot * 4 + dest, jnp.broadcast_to(cell, (8, 256)), old)
                    out_ref[outer, 2 * FACES :, :] = new.astype(BF)

        return carry

    lax.fori_loop(0, 16, per_tile, 0)


def route(targets, faces):
    vmem = pl.BlockSpec(memory_space=pltpu.VMEM)
    return pl.pallas_call(
        route_kernel,
        in_specs=[pl.BlockSpec(memory_space=pltpu.SMEM), vmem],
        out_specs=vmem,
        out_shape=jax.ShapeDtypeStruct((8, HALO, 256), BF),
        compiler_params=pltpu.CompilerParams(vmem_limit_bytes=8 << 20),
        name="route",
    )(targets, faces)


def attend_heads(units):
    scores = [
        lax.dot_general(q * BF(HD ** -0.5), k, (((1,), (1,)), ((), ())), preferred_element_type=F32)
        for q, k, _ in units
    ]
    results = []
    for score, (_, _, value) in zip(scores, units):
        top = jnp.max(score, axis=1, keepdims=True)
        weights = jnp.exp(score - top).astype(BF)
        res = jnp.dot(weights, value, preferred_element_type=F32)
        total = res[:, HD : HD + 1]
        lse = top + jnp.log(total)
        one = lse.astype(BF).astype(F32)
        two = (lse - one).astype(BF).astype(F32)
        results.append((res[:, :HD] / total, (one, two, lse - one - two)))
    return results


def put_rows(row_ref, out_ref, first):
    for n in range(row_ref.shape[0] // BLK):
        for b in range(SPLIT):
            row = n * BLK + b * 8
            out_ref[b, first + n * 8 : first + n * 8 + 8, :] = row_ref[row : row + 8, :].astype(BF)


UNIT = 8


def pair_kernel(in_ref, all_ref, out_ref, lse_ref, key_ref, val_ref, row_ref, tail_ref):
    step = pl.program_id(0)

    @pl.when(step == 0)
    def _():
        ones = jnp.where(lax.broadcasted_iota(jnp.int32, (2048, HD), 1) == 0, 1.0, 0.0).astype(BF)
        for g in range(2):
            key_ref[g] = all_ref[:, 32:64, g * HD : (g + 1) * HD].reshape(2048, HD)
            val_ref[g, :, :HD] = all_ref[:, 64:96, g * HD : (g + 1) * HD].reshape(2048, HD)
            val_ref[g, :, HD:] = ones
        tail_ref[...] = jnp.zeros(tail_ref.shape, F32)

    count = in_ref.shape[0] // UNIT
    units = []
    for n in range(count):
        for g in range(2):
            query = in_ref[n * UNIT : (n + 1) * UNIT, :BLK, g * HD : (g + 1) * HD].reshape(UNIT * BLK, HD)
            units.append((query, key_ref[g], val_ref[g]))
    results = attend_heads(units)
    lanes = lax.broadcasted_iota(jnp.int32, tail_ref.shape, 1)
    tail = tail_ref[...]
    for n in range(count):
        rows = slice(n * UNIT * BLK, (n + 1) * UNIT * BLK)
        for g in range(2):
            out, parts = results[2 * n + g]
            row_ref[rows, g * HD : (g + 1) * HD] = out
            for i, part in enumerate(parts):
                tail = jnp.where(lanes == 16 * (step * count + n) + 3 * g + i, part, tail)
    tail_ref[...] = tail
    put_rows(row_ref, out_ref, 0)
    put_rows(tail_ref, lse_ref, 0)


def single_kernel(all_ref, part_ref, lse_ref, out_ref, key_ref, val_ref, row_ref, tail_ref):
    ones = jnp.where(lax.broadcasted_iota(jnp.int32, (2048, HD), 1) == 0, 1.0, 0.0).astype(BF)
    val_ref[:, HD:] = ones
    for g in range(2):
        rows = slice(g * 1024, (g + 1) * 1024)
        key_ref[rows, :] = all_ref[:, g * 16 : g * 16 + 16, HD:].reshape(1024, HD)
        val_ref[rows, :HD] = all_ref[:, 32:48, g * HD : (g + 1) * HD].reshape(1024, HD)

    count = 64 // UNIT
    units = []
    for n in range(count):
        query = all_ref[n * UNIT : (n + 1) * UNIT, :BLK, :HD].reshape(UNIT * BLK, HD)
        units.append((query, key_ref[...], val_ref[...]))
    results = attend_heads(units)
    lanes = lax.broadcasted_iota(jnp.int32, tail_ref.shape, 1)
    tail = jnp.zeros(tail_ref.shape, F32)
    for n, (out, parts) in enumerate(results):
        first = n % (count // 2) * UNIT * BLK
        lane = n // (count // 2) * HD
        row_ref[first : first + UNIT * BLK, lane : lane + HD] = out
        for i, part in enumerate(parts):
            tail = jnp.where(lanes == 16 * n + 6 + i, part, tail)
    tail_ref[...] = tail
    for b in range(SPLIT):
        out_ref[b, :512, :] = part_ref[b]
    put_rows(row_ref, out_ref, 512)
    for n in range(UNIT):
        for b in range(SPLIT):
            row = n * BLK + b * 8
            new = lse_ref[b, n * 8 : n * 8 + 8, :].astype(F32) + tail_ref[row : row + 8, :]
            out_ref[b, 768 + n * 8 : 776 + n * 8, :] = new.astype(BF)


def attend_pair(packed):
    srcs = 32
    return pl.pallas_call(
        pair_kernel,
        grid=(64 // srcs,),
        in_specs=[
            pl.BlockSpec((srcs, CHUNK, 128), lambda i: (i, 0, 0)),
            pl.BlockSpec((64, CHUNK, 128), lambda i: (0, 0, 0)),
        ],
        out_specs=(
            pl.BlockSpec((SPLIT, srcs * 8, 128), lambda i: (0, i, 0)),
            pl.BlockSpec((SPLIT, 64, 128), lambda i: (0, 0, 0)),
        ),
        out_shape=(pltpu.HBM((SPLIT, 512, 128), BF), pltpu.HBM((SPLIT, 64, 128), BF)),
        scratch_shapes=[
            pltpu.VMEM((2, 2048, HD), BF),
            pltpu.VMEM((2, 2048, 2 * HD), BF),
            pltpu.VMEM((srcs * BLK, 128), F32),
            pltpu.VMEM((UNIT * BLK, 128), F32),
        ],
        compiler_params=pltpu.CompilerParams(vmem_limit_bytes=38 << 20),
        name="attend_pair",
    )(packed, packed)


def attend_single(rest, parts, lses):
    vmem = pl.BlockSpec(memory_space=pltpu.VMEM)
    return pl.pallas_call(
        single_kernel,
        in_specs=[vmem] * 3,
        out_specs=vmem,
        out_shape=jax.ShapeDtypeStruct((SPLIT, PARTS, 128), BF),
        scratch_shapes=[
            pltpu.VMEM((2048, HD), BF),
            pltpu.VMEM((2048, 2 * HD), BF),
            pltpu.VMEM((1024, 128), F32),
            pltpu.VMEM((UNIT * BLK, 128), F32),
        ],
        compiler_params=pltpu.CompilerParams(vmem_limit_bytes=38 << 20),
        name="attend_single",
    )(rest, in_hbm(parts), in_hbm(lses))


SHARE = 72
ROWS = SHARE + 16


def merge_kernel(parts_ref, rest_ref, att_ref, grad_ref, pair_ref, single_ref, cot_ref):
    for c in range(DM // 128):
        cot_ref[:, c * 128 : (c + 1) * 128] = rest_ref[:, 48 + 8 * c : 56 + 8 * c, :].reshape(512, 128)
    tails = []
    for b in range(SPLIT):
        tile = parts_ref[b, 768:, :].astype(F32)
        tail = jnp.concatenate([tile] + [pltpu.roll(tile, 128 - 16 * j, 1) for j in range(1, 8)], axis=0)
        tails.append(tail + pltpu.roll(tail, 127, 1) + pltpu.roll(tail, 126, 1))
    top = jnp.maximum(jnp.maximum(tails[0], tails[1]), jnp.maximum(tails[2], tails[3]))
    ws = [jnp.exp(tail - top) for tail in tails]
    inverse = 1.0 / (ws[0] + ws[1] + ws[2] + ws[3])
    low = lax.broadcasted_iota(jnp.int32, (512, 128), 1) < HD
    pair = jnp.zeros((512, 128), F32)
    folded = jnp.zeros((256, 128), F32)
    for b in range(SPLIT):
        share = ws[b] * inverse
        w0, w1, w2 = (share[:, 3 * g : 3 * g + 1] for g in range(HG))
        pair = pair + jnp.where(low, w0, w1) * parts_ref[b, :512, :].astype(F32)
        folded = folded + jnp.where(low[:256], w2[:256], w2[256:]) * parts_ref[b, 512:768, :].astype(F32)
    single = jnp.where(low, jnp.concatenate([folded, pltpu.roll(folded, HD, 1)], axis=0), 0.0)
    pair_ref[...] = pair.astype(BF)
    single_ref[...] = single.astype(BF)
    for n in range(64):
        att_ref[n, :8, :] = pair[n * 8 : n * 8 + 8].astype(BF)
        att_ref[n, 8:, :] = single[n * 8 : n * 8 + 8].astype(BF)
    for first, ref, count in ((0, pair_ref, 128), (128, single_ref, 64)):
        grad = lax.dot_general(
            ref[...], cot_ref[...], (((0,), (0,)), ((), ())), preferred_element_type=F32
        )
        for c in range(DM // 128):
            grad_ref[c, first : first + count, :] = grad[:count, c * 128 : (c + 1) * 128].astype(BF)


def merge(parts, rest):
    return pl.pallas_call(
        merge_kernel,
        out_shape=(
            jax.ShapeDtypeStruct((64, 16, 128), BF),
            jax.ShapeDtypeStruct((DM // 128, GW, 128), BF),
        ),
        scratch_shapes=[pltpu.VMEM((512, 128), BF), pltpu.VMEM((512, 128), BF), pltpu.VMEM((512, DM), BF)],
        compiler_params=pltpu.CompilerParams(vmem_limit_bytes=16 << 20),
        name="merge",
    )(parts, rest)


def share_kernel(terms_ref, att_ref, out_ref, total_ref):
    @pl.when(pl.program_id(0) == 0)
    def _():
        total = terms_ref[0].astype(F32)
        for n in range(1, 16):
            total = total + terms_ref[n].astype(F32)
        total_ref[...] = total.astype(BF)

    for n in range(out_ref.shape[0]):
        out_ref[n, :SHARE, :] = total_ref[...]
        out_ref[n, SHARE:, :] = att_ref[n]


def share_out(terms, att):
    step = 16
    return pl.pallas_call(
        share_kernel,
        grid=(64 // step,),
        in_specs=[
            pl.BlockSpec((16, SHARE, 128), lambda i: (0, 0, 0)),
            pl.BlockSpec((step, 16, 128), lambda i: (i, 0, 0)),
        ],
        out_specs=pl.BlockSpec((step, ROWS, 128), lambda i: (i, 0, 0)),
        out_shape=jax.ShapeDtypeStruct((64, ROWS, 128), BF),
        scratch_shapes=[pltpu.VMEM((SHARE, 128), BF)],
        compiler_params=pltpu.CompilerParams(vmem_limit_bytes=8 << 20),
        name="share",
    )(terms, att)


def finish_kernel(all_ref, tokens_ref, weight_ref, mixed_ref, grad_hbm, att_ref, grad_ref, sems):
    copies = []
    for h in range(SPLIT):
        for m in range(16):
            at = place(h, m // SPLIT, m % SPLIT)
            done = 0
            while done < SHARE:
                block, row = divmod(m * SHARE + done, GW)
                count = min(SHARE - done, (128 if row < 128 else GW) - row)
                dest = h * 128 + row if row < 128 else 512 + h * HD + row - 128
                grad_ref[dest : dest + count, block * 128 : (block + 1) * 128] = all_ref[
                    at, done : done + count, :
                ].astype(F32)
                done += count
        for n, (first, count) in enumerate(((h * 128, 128), (512 + h * HD, HD))):
            rows = slice(first, first + count)
            copy = pltpu.make_async_copy(grad_ref.at[rows], grad_hbm.at[rows], sems.at[2 * h + n])
            copy.start()
            copies.append(copy)
    lanes = lax.broadcasted_iota(jnp.int32, (8, 128), 1) < HD
    for a in range(SPLIT):
        for b in range(SPLIT):
            row = a * BLK + b * 8
            for h in range(SPLIT):
                att_ref[row : row + 8, h * 128 : (h + 1) * 128] = all_ref[place(h, a, b), SHARE : SHARE + 8, :]
            for h in range(0, SPLIT, 2):
                even = all_ref[place(h, a, b), SHARE + 8 :, :].astype(F32)
                odd = pltpu.roll(all_ref[place(h + 1, a, b), SHARE + 8 :, :].astype(F32), HD, 1)
                first = 512 + h * HD
                att_ref[row : row + 8, first : first + 128] = jnp.where(lanes, even, odd).astype(BF)
    mixed_ref[...] = (
        tokens_ref[...].astype(F32) + jnp.dot(att_ref[...], weight_ref[...], preferred_element_type=F32)
    ).astype(BF)
    for copy in copies:
        copy.wait()


def finish(received, tokens, weight):
    vmem = pl.BlockSpec(memory_space=pltpu.VMEM)
    return pl.pallas_call(
        finish_kernel,
        in_specs=[vmem] * 3,
        out_specs=(vmem, pl.BlockSpec(memory_space=pl.ANY)),
        out_shape=(
            jax.ShapeDtypeStruct((128, DM), BF),
            jax.ShapeDtypeStruct((DM, DM), F32),
        ),
        scratch_shapes=[
            pltpu.VMEM((128, DM), BF),
            pltpu.VMEM((DM, DM), F32),
            pltpu.SemaphoreType.DMA((8,)),
        ],
        compiler_params=pltpu.CompilerParams(vmem_limit_bytes=12 << 20),
        name="finish",
    )(received, tokens, weight)


ZW = 48
Z0 = 8


def stem_kernel(
    halo_ref,
    conv_ref,
    cot_ref,
    features_hbm,
    patch_hbm,
    wq_ref,
    wk_ref,
    wv_ref,
    tokens_ref,
    packed_ref,
    rest_ref,
    maps_ref,
    side_ref,
    left_ref,
    mid_ref,
    right_ref,
    hid_ref,
    patch_ref,
    sems,
):
    loads = [pltpu.make_async_copy(features_hbm.at[t], maps_ref.at[t, 1:33], sems.at[t]) for t in range(2)]
    parts = [slice(r * 1024, r * 1024 + 1024) for r in range(4)]
    loads += [pltpu.make_async_copy(patch_hbm.at[p], patch_ref.at[p], sems.at[2 + r]) for r, p in enumerate(parts)]
    for load in loads:
        load.start()
    zrefs = (left_ref, mid_ref, right_ref)

    def halo_rows(t, first, count):
        first = t * FACES + first
        total = halo_ref[0, first : first + count, :].astype(F32)
        for n in range(1, 8):
            total = total + halo_ref[n, first : first + count, :].astype(F32)
        return total

    corner = halo_rows(2, 0, 8)
    for t in range(2):
        maps_ref[t, 0] = halo_rows(t, 0, 32).astype(BF)
        maps_ref[t, 33] = halo_rows(t, 32, 32).astype(BF)
        for side in range(2):
            side_ref[side, t, Z0 : Z0 + 32, :] = halo_rows(t, 64 + 32 * side, 32)
            for end, row in enumerate((Z0 - 1, Z0 + 32)):
                cell = t * 4 + 2 * end + side
                side_ref[side, t, row : row + 1, :] = corner[cell : cell + 1]
    for t in range(2):
        for side in range(2):
            edge = jnp.zeros((32, 256), F32)
            for dy in range(3):
                part = side_ref[side, t, Z0 - 1 + dy : Z0 + 31 + dy, :].astype(BF)
                edge = edge + jnp.dot(part, conv_ref[dy * 3 + side * 2], preferred_element_type=F32)
            dest, first = ((left_ref, Z0 - 1), (right_ref, Z0 + 32))[side]
            for lt in range(2):
                dest[lt, pl.ds(t * 32 * ZW + first, 32, stride=ZW), :] = edge[:, lt * 128 : lt * 128 + 128]
    for t in range(2):
        loads[t].wait()
        for y in range(0, 32, 8):
            for dx in range(3):
                acc = jnp.zeros((256, 256), F32)
                for dy in range(3):
                    rows = maps_ref[t, y + dy : y + dy + 8].reshape(256, 256)
                    acc = acc + jnp.dot(rows, conv_ref[dy * 3 + dx], preferred_element_type=F32)
                for n in range(8):
                    first = (t * 32 + y + n) * ZW + Z0
                    for lt in range(2):
                        zrefs[dx][lt, first : first + 32, :] = acc[n * 32 : n * 32 + 32, lt * 128 : lt * 128 + 128]

    embedded = jnp.zeros((128, DM), F32)
    for r in range(4):
        for c in range(4):
            for t in range(2):
                for pr in range(8):
                    first = (t * 32 + pr * 4 + r) * ZW + Z0 + c
                    row = (t * 8 + pr) * 8
                    for lt in range(2):
                        total = (
                            mid_ref[lt, pl.ds(first, 8, stride=4), :]
                            + left_ref[lt, pl.ds(first - 1, 8, stride=4), :]
                            + right_ref[lt, pl.ds(first + 1, 8, stride=4), :]
                        )
                        col = (r * 4 + c) * 256 + lt * 128
                        hid_ref[row : row + 8, col : col + 128] = jax.nn.gelu(total).astype(BF)
        loads[2 + r].wait()
        embedded = embedded + jnp.dot(hid_ref[:, parts[r]], patch_ref[parts[r], :], preferred_element_type=F32)
    tokens = embedded.astype(BF)
    tokens_ref[...] = tokens
    query = jnp.dot(tokens, wq_ref[...], preferred_element_type=F32)
    keys = jnp.dot(tokens, wk_ref[...], preferred_element_type=F32)
    values = jnp.dot(tokens, wv_ref[...], preferred_element_type=F32)
    low = lax.broadcasted_iota(jnp.int32, (128, 128), 1) < HD

    def pair_of(x, h):
        return x[:, h * 128 : (h + 1) * 128]

    for h in range(SPLIT):
        one = 4 + h // 2
        q1, k1, v1 = pair_of(query, one), pair_of(keys, one), pair_of(values, one)
        if h % 2 == 0:
            k1 = pltpu.roll(k1, HD, 1)
            v2 = pltpu.roll(v1, HD, 1)
        else:
            q1 = pltpu.roll(q1, HD, 1)
            v2 = v1
            v1 = pltpu.roll(v1, HD, 1)
        pieces = (pair_of(query, h).astype(BF), pair_of(keys, h).astype(BF), pair_of(values, h).astype(BF))
        for a in range(SPLIT):
            for b in range(SPLIT):
                at = place(h, a, b)
                qa, kb = slice(a * BLK, (a + 1) * BLK), slice(b * BLK, (b + 1) * BLK)
                packed_ref[at, 0:32, :] = pieces[0][qa]
                packed_ref[at, 32:64, :] = pieces[1][kb]
                packed_ref[at, 64:96, :] = pieces[2][kb]
                rest_ref[at, 0:32, :] = jnp.where(low[:BLK], q1[qa], k1[kb]).astype(BF)
                half = b * BLK + BLK // 2
                rest_ref[at, 32:48, :] = jnp.where(
                    low[: BLK // 2], v1[b * BLK : half], v2[half : (b + 1) * BLK]
                ).astype(BF)
                row = a * BLK + b * 8
                for c in range(DM // 128):
                    rest_ref[at, 48 + 8 * c : 56 + 8 * c, :] = cot_ref[row : row + 8, c * 128 : (c + 1) * 128]


def stem(halo, conv_weight, cotangent, features, patch_weight, query_weight, key_weight, value_weight):
    hbm = pl.BlockSpec(memory_space=pl.ANY)
    vmem = pl.BlockSpec(memory_space=pltpu.VMEM)
    return pl.pallas_call(
        stem_kernel,
        in_specs=[vmem] * 3 + [hbm] * 2 + [vmem] * 3,
        out_specs=(vmem, vmem, vmem),
        out_shape=(
            jax.ShapeDtypeStruct((128, DM), BF),
            jax.ShapeDtypeStruct((64, CHUNK, 128), BF),
            jax.ShapeDtypeStruct((64, CHUNK, 128), BF),
        ),
        scratch_shapes=[
            pltpu.VMEM((2, 34, 32, 256), BF),
            pltpu.VMEM((2, 2, ZW, 256), F32),
            pltpu.VMEM((2, 64 * ZW, 128), F32),
            pltpu.VMEM((2, 64 * ZW, 128), F32),
            pltpu.VMEM((2, 64 * ZW, 128), F32),
            pltpu.VMEM((128, 4096), BF),
            pltpu.VMEM((4096, DM), BF),
            pltpu.SemaphoreType.DMA((6,)),
        ],
        compiler_params=pltpu.CompilerParams(vmem_limit_bytes=26 << 20),
        name="stem",
    )(halo, conv_weight, cotangent, features, patch_weight, query_weight, key_weight, value_weight)


def local(
    features,
    neighbours,
    conv_weight,
    patch_weight,
    query_weight,
    key_weight,
    value_weight,
    output_weight,
    cotangent,
):
    _, inner = split_device(lax.axis_index("tile"))
    faces = gather_faces(in_hbm(neighbours), in_hbm(features))
    faces, inner = lax.optimization_barrier((faces, inner))
    faces = swap(faces, INNER).reshape(16, FACES, 256)
    tiles = faces[:, 64, :8].astype(jnp.int32)
    outer, goal = split_device(tiles >> 1)
    targets = jnp.where((tiles < 128) & (goal == inner), (outer & 7) * 2 + (tiles & 1), -1)
    halo = swap(route(targets, faces), OUTER)
    tokens, packed, rest = stem(
        halo,
        conv_weight.reshape(9, 256, 256),
        cotangent,
        features,
        in_hbm(patch_weight),
        query_weight,
        key_weight,
        value_weight,
    )
    packed = swap(packed)
    packed, rest = lax.optimization_barrier((packed, rest))
    rest = swap(rest)
    parts = swap(attend_single(rest, *attend_pair(packed)), KEY_GROUPS)
    att, grad = merge(parts, rest)
    terms = swap(grad.reshape(16, SHARE, 128), HEAD_GROUPS)
    received = swap(share_out(terms, att))
    return finish(received, tokens, output_weight)


def solution(mesh):
    in_specs = (
        P(("slide", "tile"), None, None, None),
        P(("slide", "tile"), None),
        P(),
        P(),
        P(),
        P(),
        P(),
        P(),
        P(("slide", "tile"), None),
    )
    out_specs = (P(("slide", "tile"), None), P("slide", None))
    return jax.shard_map(local, mesh=mesh, in_specs=in_specs, out_specs=out_specs, check_vma=False)
```

```python
import jax
import jax.numpy as jnp
from jax import lax
from jax.experimental import pallas as pl
from jax.experimental.pallas import tpu as pltpu
from jax.sharding import PartitionSpec as P

PATCH = 4
HEADS = 12
HD = 64
DM = 768
SPLIT = 4
HG = HEADS // SPLIT
GW = HG * HD
BLK = 32
CHUNK = 96
PARTS = 512 + 256 + 64
FACES = 128
HALO = 264
BF = jnp.bfloat16
F32 = jnp.float32


def hi_bit(coord):
    return coord >> 1


def lo_bit(coord):
    return (coord ^ (coord >> 1)) & 1


def split_device(dev):
    z, y, x = dev >> 4, (dev >> 2) & 3, dev & 3
    outer = hi_bit(z) * 4 + hi_bit(y) * 2 + hi_bit(x)
    inner = lo_bit(z) * 4 + lo_bit(y) * 2 + lo_bit(x)
    return outer, inner


def device_groups():
    place = {}
    for dev in range(64):
        place[split_device(dev)] = dev
    inner_groups = [[place[(a, b)] for b in range(8)] for a in range(8)]
    outer_groups = [[place[(a, b)] for a in range(8)] for b in range(8)]
    return inner_groups, outer_groups


INNER, OUTER = device_groups()


def place(h, a, b):
    def coord(hi, lo):
        return hi * 2 + (hi ^ lo)

    return coord(a >> 1, b >> 1) * 16 + coord(a & 1, b & 1) * 4 + h


KEY_GROUPS = [[place(h, a, b) for b in range(SPLIT)] for h in range(SPLIT) for a in range(SPLIT)]
HEAD_GROUPS = [[place(h, a, b) for a in range(SPLIT) for b in range(SPLIT)] for h in range(SPLIT)]


def in_hbm(x):
    return pltpu.with_memory_space_constraint(x, pltpu.HBM)


def swap(x, groups=None):
    return lax.all_to_all(
        x, "tile", split_axis=0, concat_axis=0, tiled=True, axis_index_groups=groups
    )


def faces_kernel(links_ref, features_hbm, out_ref, sides_ref, cols_ref, faces_ref, sems):
    loads = []
    for t in range(2):
        for n, y in enumerate((0, 31)):
            loads.append((features_hbm.at[t, y], faces_ref.at[t, n * 32 : n * 32 + 32]))
        for n, x in enumerate((0, 24)):
            loads.append((features_hbm.at[t, :, x : x + 8], sides_ref.at[t, n]))
    loads = [pltpu.make_async_copy(src, dst, sems.at[n]) for n, (src, dst) in enumerate(loads)]
    for load in loads:
        load.start()
    for load in loads:
        load.wait()
    lanes = lax.broadcasted_iota(jnp.int32, (8, 128), 1)
    subs = lax.broadcasted_iota(jnp.int32, (8, 128), 0)
    for t in range(2):
        for n, x in enumerate((0, 7)):
            for lt in range(2):
                cols_ref[:256] = sides_ref[t, n, :, :, lt * 128 : lt * 128 + 128].astype(F32).reshape(256, 128)
                faces_ref[t, 64 + n * 32 : 96 + n * 32, lt * 128 : lt * 128 + 128] = cols_ref[
                    pl.ds(x, 32, stride=8), :
                ].astype(BF)
    for t in range(2):
        row = faces_ref[t, 64:72, :128].astype(F32)
        for d in range(8):
            row = jnp.where((lanes == d) & (subs == 0), links_ref[t, d].astype(F32), row)
        faces_ref[t, 64:72, :128] = row.astype(BF)
    for n in range(8):
        out_ref[n] = faces_ref[...]


def gather_faces(links, features):
    hbm = pl.BlockSpec(memory_space=pltpu.HBM)
    return pl.pallas_call(
        faces_kernel,
        in_specs=[pl.BlockSpec(memory_space=pltpu.SMEM), hbm],
        out_specs=pl.BlockSpec(memory_space=pltpu.VMEM),
        out_shape=jax.ShapeDtypeStruct((8, 2, FACES, 256), BF),
        scratch_shapes=[
            pltpu.VMEM((2, 2, 32, 8, 256), BF),
            pltpu.VMEM((264, 128), F32),
            pltpu.VMEM((2, FACES, 256), BF),
            pltpu.SemaphoreType.DMA((8,)),
        ],
        compiler_params=pltpu.CompilerParams(vmem_limit_bytes=6 << 20),
        name="faces",
    )(links, features)


EDGES = {1: (0, 32), 6: (32, 0), 3: (64, 96), 4: (96, 64)}
CORNERS = {0: (0, 3), 2: (31, 2), 5: (32, 1), 7: (63, 0)}


def route_kernel(targets_ref, faces_ref, out_ref):
    out_ref[...] = jnp.zeros(out_ref.shape, BF)
    row_ids = lax.broadcasted_iota(jnp.int32, (8, 256), 0)

    def per_tile(src, carry):
        for direction in range(8):
            target = targets_ref[src, direction]

            @pl.when(target >= 0)
            def _():
                outer, slot = target >> 1, target & 1
                if direction in EDGES:
                    first, dest = EDGES[direction]
                    row = pl.multiple_of(slot * FACES + dest, 32)
                    out_ref[outer, pl.ds(row, 32), :] = faces_ref[src, first : first + 32, :]
                    if direction == 3:
                        tile = faces_ref[src, first : first + 8, :].astype(F32)
                        cell = faces_ref[src, 0:8, :].astype(F32)
                        out_ref[outer, pl.ds(row, 8), :] = jnp.where(row_ids == 0, cell, tile).astype(BF)
                else:
                    row, dest = CORNERS[direction]
                    base = row // 8 * 8
                    cell = faces_ref[src, base : base + 8, :].astype(F32)[row - base : row - base + 1, :]
                    old = out_ref[outer, 2 * FACES :, :].astype(F32)
                    new = jnp.where(row_ids == slot * 4 + dest, jnp.broadcast_to(cell, (8, 256)), old)
                    out_ref[outer, 2 * FACES :, :] = new.astype(BF)

        return carry

    lax.fori_loop(0, 16, per_tile, 0)


def route(targets, faces):
    vmem = pl.BlockSpec(memory_space=pltpu.VMEM)
    return pl.pallas_call(
        route_kernel,
        in_specs=[pl.BlockSpec(memory_space=pltpu.SMEM), vmem],
        out_specs=vmem,
        out_shape=jax.ShapeDtypeStruct((8, HALO, 256), BF),
        compiler_params=pltpu.CompilerParams(vmem_limit_bytes=8 << 20),
        name="route",
    )(targets, faces)


def attend_heads(units):
    scores = [
        lax.dot_general(q * BF(HD ** -0.5), k, (((1,), (1,)), ((), ())), preferred_element_type=F32)
        for q, k, _ in units
    ]
    results = []
    for score, (_, _, value) in zip(scores, units):
        top = jnp.max(score, axis=1, keepdims=True)
        weights = jnp.exp(score - top).astype(BF)
        res = jnp.dot(weights, value, preferred_element_type=F32)
        total = res[:, HD : HD + 1]
        lse = top + jnp.log(total)
        one = lse.astype(BF).astype(F32)
        two = (lse - one).astype(BF).astype(F32)
        results.append((res[:, :HD] / total, (one, two, lse - one - two)))
    return results


def put_rows(row_ref, out_ref, first):
    for n in range(row_ref.shape[0] // BLK):
        for b in range(SPLIT):
            row = n * BLK + b * 8
            out_ref[b, first + n * 8 : first + n * 8 + 8, :] = row_ref[row : row + 8, :].astype(BF)


UNIT = 8


def pair_kernel(in_ref, all_ref, out_ref, lse_ref, key_ref, val_ref, row_ref, tail_ref):
    step = pl.program_id(0)

    @pl.when(step == 0)
    def _():
        ones = jnp.where(lax.broadcasted_iota(jnp.int32, (2048, HD), 1) == 0, 1.0, 0.0).astype(BF)
        for g in range(2):
            key_ref[g] = all_ref[:, 32:64, g * HD : (g + 1) * HD].reshape(2048, HD)
            val_ref[g, :, :HD] = all_ref[:, 64:96, g * HD : (g + 1) * HD].reshape(2048, HD)
            val_ref[g, :, HD:] = ones
        tail_ref[...] = jnp.zeros(tail_ref.shape, F32)

    count = in_ref.shape[0] // UNIT
    units = []
    for n in range(count):
        for g in range(2):
            query = in_ref[n * UNIT : (n + 1) * UNIT, :BLK, g * HD : (g + 1) * HD].reshape(UNIT * BLK, HD)
            units.append((query, key_ref[g], val_ref[g]))
    results = attend_heads(units)
    lanes = lax.broadcasted_iota(jnp.int32, tail_ref.shape, 1)
    tail = tail_ref[...]
    for n in range(count):
        rows = slice(n * UNIT * BLK, (n + 1) * UNIT * BLK)
        for g in range(2):
            out, parts = results[2 * n + g]
            row_ref[rows, g * HD : (g + 1) * HD] = out
            for i, part in enumerate(parts):
                tail = jnp.where(lanes == 16 * (step * count + n) + 3 * g + i, part, tail)
    tail_ref[...] = tail
    put_rows(row_ref, out_ref, 0)
    put_rows(tail_ref, lse_ref, 0)


def single_kernel(all_ref, part_hbm, lse_ref, out_ref, key_ref, val_ref, row_ref, tail_ref, sems):
    copies = [
        pltpu.make_async_copy(part_hbm.at[b], out_ref.at[b, :512], sems.at[b]) for b in range(SPLIT)
    ]
    for copy in copies:
        copy.start()
    ones = jnp.where(lax.broadcasted_iota(jnp.int32, (2048, HD), 1) == 0, 1.0, 0.0).astype(BF)
    val_ref[:, HD:] = ones
    for g in range(2):
        rows = slice(g * 1024, (g + 1) * 1024)
        key_ref[rows, :] = all_ref[:, g * 16 : g * 16 + 16, HD:].reshape(1024, HD)
        val_ref[rows, :HD] = all_ref[:, 32:48, g * HD : (g + 1) * HD].reshape(1024, HD)

    count = 64 // UNIT
    units = []
    for n in range(count):
        query = all_ref[n * UNIT : (n + 1) * UNIT, :BLK, :HD].reshape(UNIT * BLK, HD)
        units.append((query, key_ref[...], val_ref[...]))
    results = attend_heads(units)
    lanes = lax.broadcasted_iota(jnp.int32, tail_ref.shape, 1)
    tail = jnp.zeros(tail_ref.shape, F32)
    for n, (out, parts) in enumerate(results):
        first = n % (count // 2) * UNIT * BLK
        lane = n // (count // 2) * HD
        row_ref[first : first + UNIT * BLK, lane : lane + HD] = out
        for i, part in enumerate(parts):
            tail = jnp.where(lanes == 16 * n + 6 + i, part, tail)
    tail_ref[...] = tail
    put_rows(row_ref, out_ref, 512)
    for n in range(UNIT):
        for b in range(SPLIT):
            row = n * BLK + b * 8
            new = lse_ref[b, n * 8 : n * 8 + 8, :].astype(F32) + tail_ref[row : row + 8, :]
            out_ref[b, 768 + n * 8 : 776 + n * 8, :] = new.astype(BF)
    for copy in copies:
        copy.wait()


def attend_pair(packed):
    srcs = 32
    return pl.pallas_call(
        pair_kernel,
        grid=(64 // srcs,),
        in_specs=[
            pl.BlockSpec((srcs, CHUNK, 128), lambda i: (i, 0, 0)),
            pl.BlockSpec((64, CHUNK, 128), lambda i: (0, 0, 0)),
        ],
        out_specs=(
            pl.BlockSpec((SPLIT, srcs * 8, 128), lambda i: (0, i, 0)),
            pl.BlockSpec((SPLIT, 64, 128), lambda i: (0, 0, 0)),
        ),
        out_shape=(pltpu.HBM((SPLIT, 512, 128), BF), pltpu.HBM((SPLIT, 64, 128), BF)),
        scratch_shapes=[
            pltpu.VMEM((2, 2048, HD), BF),
            pltpu.VMEM((2, 2048, 2 * HD), BF),
            pltpu.VMEM((srcs * BLK, 128), F32),
            pltpu.VMEM((UNIT * BLK, 128), F32),
        ],
        compiler_params=pltpu.CompilerParams(vmem_limit_bytes=38 << 20),
        name="attend_pair",
    )(packed, packed)


def attend_single(rest, parts, lses):
    vmem = pl.BlockSpec(memory_space=pltpu.VMEM)
    return pl.pallas_call(
        single_kernel,
        in_specs=[vmem, pl.BlockSpec(memory_space=pltpu.HBM), vmem],
        out_specs=vmem,
        out_shape=jax.ShapeDtypeStruct((SPLIT, PARTS, 128), BF),
        scratch_shapes=[
            pltpu.VMEM((2048, HD), BF),
            pltpu.VMEM((2048, 2 * HD), BF),
            pltpu.VMEM((1024, 128), F32),
            pltpu.VMEM((UNIT * BLK, 128), F32),
            pltpu.SemaphoreType.DMA((SPLIT,)),
        ],
        compiler_params=pltpu.CompilerParams(vmem_limit_bytes=38 << 20),
        name="attend_single",
    )(rest, in_hbm(parts), in_hbm(lses))


SHARE = 72
ROWS = SHARE + 16


def merge_kernel(parts_ref, rest_ref, att_ref, grad_ref, pair_ref, single_ref, cot_ref):
    for c in range(DM // 128):
        cot_ref[:, c * 128 : (c + 1) * 128] = rest_ref[:, 48 + 8 * c : 56 + 8 * c, :].reshape(512, 128)
    tails = []
    for b in range(SPLIT):
        tile = parts_ref[b, 768:, :].astype(F32)
        tail = jnp.concatenate([tile] + [pltpu.roll(tile, 128 - 16 * j, 1) for j in range(1, 8)], axis=0)
        tails.append(tail + pltpu.roll(tail, 127, 1) + pltpu.roll(tail, 126, 1))
    top = jnp.maximum(jnp.maximum(tails[0], tails[1]), jnp.maximum(tails[2], tails[3]))
    ws = [jnp.exp(tail - top) for tail in tails]
    inverse = 1.0 / (ws[0] + ws[1] + ws[2] + ws[3])
    low = lax.broadcasted_iota(jnp.int32, (512, 128), 1) < HD
    pair = jnp.zeros((512, 128), F32)
    folded = jnp.zeros((256, 128), F32)
    for b in range(SPLIT):
        share = ws[b] * inverse
        w0, w1, w2 = (share[:, 3 * g : 3 * g + 1] for g in range(HG))
        pair = pair + jnp.where(low, w0, w1) * parts_ref[b, :512, :].astype(F32)
        folded = folded + jnp.where(low[:256], w2[:256], w2[256:]) * parts_ref[b, 512:768, :].astype(F32)
    single = jnp.where(low, jnp.concatenate([folded, pltpu.roll(folded, HD, 1)], axis=0), 0.0)
    pair_ref[...] = pair.astype(BF)
    single_ref[...] = single.astype(BF)
    for n in range(64):
        att_ref[n, :8, :] = pair[n * 8 : n * 8 + 8].astype(BF)
        att_ref[n, 8:, :] = single[n * 8 : n * 8 + 8].astype(BF)
    for first, ref, count in ((0, pair_ref, 128), (128, single_ref, 64)):
        grad = lax.dot_general(
            ref[...], cot_ref[...], (((0,), (0,)), ((), ())), preferred_element_type=F32
        )
        for c in range(DM // 128):
            grad_ref[c, first : first + count, :] = grad[:count, c * 128 : (c + 1) * 128].astype(BF)


def merge(parts, rest):
    return pl.pallas_call(
        merge_kernel,
        out_shape=(
            jax.ShapeDtypeStruct((64, 16, 128), BF),
            jax.ShapeDtypeStruct((DM // 128, GW, 128), BF),
        ),
        scratch_shapes=[pltpu.VMEM((512, 128), BF), pltpu.VMEM((512, 128), BF), pltpu.VMEM((512, DM), BF)],
        compiler_params=pltpu.CompilerParams(vmem_limit_bytes=16 << 20),
        name="merge",
    )(parts, rest)


def share_kernel(terms_ref, att_ref, out_ref, total_ref):
    @pl.when(pl.program_id(0) == 0)
    def _():
        total = terms_ref[0].astype(F32)
        for n in range(1, 16):
            total = total + terms_ref[n].astype(F32)
        total_ref[...] = total.astype(BF)

    for n in range(out_ref.shape[0]):
        out_ref[n, :SHARE, :] = total_ref[...]
        out_ref[n, SHARE:, :] = att_ref[n]


def share_out(terms, att):
    step = 16
    return pl.pallas_call(
        share_kernel,
        grid=(64 // step,),
        in_specs=[
            pl.BlockSpec((16, SHARE, 128), lambda i: (0, 0, 0)),
            pl.BlockSpec((step, 16, 128), lambda i: (i, 0, 0)),
        ],
        out_specs=pl.BlockSpec((step, ROWS, 128), lambda i: (i, 0, 0)),
        out_shape=jax.ShapeDtypeStruct((64, ROWS, 128), BF),
        scratch_shapes=[pltpu.VMEM((SHARE, 128), BF)],
        compiler_params=pltpu.CompilerParams(vmem_limit_bytes=8 << 20),
        name="share",
    )(terms, att)


def finish_kernel(all_ref, tokens_ref, weight_ref, mixed_ref, grad_hbm, att_ref, grad_ref, sems):
    copies = []
    for h in range(SPLIT):
        for m in range(16):
            at = place(h, m // SPLIT, m % SPLIT)
            done = 0
            while done < SHARE:
                block, row = divmod(m * SHARE + done, GW)
                count = min(SHARE - done, (128 if row < 128 else GW) - row)
                dest = h * 128 + row if row < 128 else 512 + h * HD + row - 128
                grad_ref[dest : dest + count, block * 128 : (block + 1) * 128] = all_ref[
                    at, done : done + count, :
                ].astype(F32)
                done += count
        for n, (first, count) in enumerate(((h * 128, 128), (512 + h * HD, HD))):
            rows = slice(first, first + count)
            copy = pltpu.make_async_copy(grad_ref.at[rows], grad_hbm.at[rows], sems.at[2 * h + n])
            copy.start()
            copies.append(copy)
    lanes = lax.broadcasted_iota(jnp.int32, (8, 128), 1) < HD
    for a in range(SPLIT):
        for b in range(SPLIT):
            row = a * BLK + b * 8
            for h in range(SPLIT):
                att_ref[row : row + 8, h * 128 : (h + 1) * 128] = all_ref[place(h, a, b), SHARE : SHARE + 8, :]
            for h in range(0, SPLIT, 2):
                even = all_ref[place(h, a, b), SHARE + 8 :, :].astype(F32)
                odd = pltpu.roll(all_ref[place(h + 1, a, b), SHARE + 8 :, :].astype(F32), HD, 1)
                first = 512 + h * HD
                att_ref[row : row + 8, first : first + 128] = jnp.where(lanes, even, odd).astype(BF)
    mixed_ref[...] = (
        tokens_ref[...].astype(F32) + jnp.dot(att_ref[...], weight_ref[...], preferred_element_type=F32)
    ).astype(BF)
    for copy in copies:
        copy.wait()


def finish(received, tokens, weight):
    vmem = pl.BlockSpec(memory_space=pltpu.VMEM)
    return pl.pallas_call(
        finish_kernel,
        in_specs=[vmem] * 3,
        out_specs=(vmem, pl.BlockSpec(memory_space=pl.ANY)),
        out_shape=(
            jax.ShapeDtypeStruct((128, DM), BF),
            jax.ShapeDtypeStruct((DM, DM), F32),
        ),
        scratch_shapes=[
            pltpu.VMEM((128, DM), BF),
            pltpu.VMEM((DM, DM), F32),
            pltpu.SemaphoreType.DMA((8,)),
        ],
        compiler_params=pltpu.CompilerParams(vmem_limit_bytes=12 << 20),
        name="finish",
    )(received, tokens, weight)


ZW = 48
Z0 = 8


def stem_kernel(
    halo_ref,
    conv_ref,
    cot_ref,
    features_hbm,
    patch_hbm,
    wq_ref,
    wk_ref,
    wv_ref,
    tokens_ref,
    packed_ref,
    rest_ref,
    maps_ref,
    side_ref,
    left_ref,
    mid_ref,
    right_ref,
    hid_ref,
    patch_ref,
    sems,
):
    loads = [pltpu.make_async_copy(features_hbm.at[t], maps_ref.at[t, 1:33], sems.at[t]) for t in range(2)]
    parts = [slice(r * 1024, r * 1024 + 1024) for r in range(4)]
    loads += [pltpu.make_async_copy(patch_hbm.at[p], patch_ref.at[p], sems.at[2 + r]) for r, p in enumerate(parts)]
    for load in loads:
        load.start()
    zrefs = (left_ref, mid_ref, right_ref)

    def halo_rows(t, first, count):
        first = t * FACES + first
        total = halo_ref[0, first : first + count, :].astype(F32)
        for n in range(1, 8):
            total = total + halo_ref[n, first : first + count, :].astype(F32)
        return total

    corner = halo_rows(2, 0, 8)
    for t in range(2):
        maps_ref[t, 0] = halo_rows(t, 0, 32).astype(BF)
        maps_ref[t, 33] = halo_rows(t, 32, 32).astype(BF)
        for side in range(2):
            side_ref[side, t, Z0 : Z0 + 32, :] = halo_rows(t, 64 + 32 * side, 32)
            for end, row in enumerate((Z0 - 1, Z0 + 32)):
                cell = t * 4 + 2 * end + side
                side_ref[side, t, row : row + 1, :] = corner[cell : cell + 1]
    for t in range(2):
        for side in range(2):
            edge = jnp.zeros((32, 256), F32)
            for dy in range(3):
                part = side_ref[side, t, Z0 - 1 + dy : Z0 + 31 + dy, :].astype(BF)
                edge = edge + jnp.dot(part, conv_ref[dy * 3 + side * 2], preferred_element_type=F32)
            dest, first = ((left_ref, Z0 - 1), (right_ref, Z0 + 32))[side]
            for lt in range(2):
                dest[lt, pl.ds(t * 32 * ZW + first, 32, stride=ZW), :] = edge[:, lt * 128 : lt * 128 + 128]
    for t in range(2):
        loads[t].wait()
        for y in range(0, 32, 8):
            for dx in range(3):
                acc = jnp.zeros((256, 256), F32)
                for dy in range(3):
                    rows = maps_ref[t, y + dy : y + dy + 8].reshape(256, 256)
                    acc = acc + jnp.dot(rows, conv_ref[dy * 3 + dx], preferred_element_type=F32)
                for n in range(8):
                    first = (t * 32 + y + n) * ZW + Z0
                    for lt in range(2):
                        zrefs[dx][lt, first : first + 32, :] = acc[n * 32 : n * 32 + 32, lt * 128 : lt * 128 + 128]

    embedded = jnp.zeros((128, DM), F32)
    for r in range(4):
        for c in range(4):
            for t in range(2):
                for pr in range(8):
                    first = (t * 32 + pr * 4 + r) * ZW + Z0 + c
                    row = (t * 8 + pr) * 8
                    for lt in range(2):
                        total = (
                            mid_ref[lt, pl.ds(first, 8, stride=4), :]
                            + left_ref[lt, pl.ds(first - 1, 8, stride=4), :]
                            + right_ref[lt, pl.ds(first + 1, 8, stride=4), :]
                        )
                        col = (r * 4 + c) * 256 + lt * 128
                        hid_ref[row : row + 8, col : col + 128] = jax.nn.gelu(total).astype(BF)
        loads[2 + r].wait()
        embedded = embedded + jnp.dot(hid_ref[:, parts[r]], patch_ref[parts[r], :], preferred_element_type=F32)
    tokens = embedded.astype(BF)
    tokens_ref[...] = tokens
    query = jnp.dot(tokens, wq_ref[...], preferred_element_type=F32)
    keys = jnp.dot(tokens, wk_ref[...], preferred_element_type=F32)
    values = jnp.dot(tokens, wv_ref[...], preferred_element_type=F32)
    low = lax.broadcasted_iota(jnp.int32, (128, 128), 1) < HD

    def pair_of(x, h):
        return x[:, h * 128 : (h + 1) * 128]

    for h in range(SPLIT):
        one = 4 + h // 2
        q1, k1, v1 = pair_of(query, one), pair_of(keys, one), pair_of(values, one)
        if h % 2 == 0:
            k1 = pltpu.roll(k1, HD, 1)
            v2 = pltpu.roll(v1, HD, 1)
        else:
            q1 = pltpu.roll(q1, HD, 1)
            v2 = v1
            v1 = pltpu.roll(v1, HD, 1)
        pieces = (pair_of(query, h).astype(BF), pair_of(keys, h).astype(BF), pair_of(values, h).astype(BF))
        for a in range(SPLIT):
            for b in range(SPLIT):
                at = place(h, a, b)
                qa, kb = slice(a * BLK, (a + 1) * BLK), slice(b * BLK, (b + 1) * BLK)
                packed_ref[at, 0:32, :] = pieces[0][qa]
                packed_ref[at, 32:64, :] = pieces[1][kb]
                packed_ref[at, 64:96, :] = pieces[2][kb]
                rest_ref[at, 0:32, :] = jnp.where(low[:BLK], q1[qa], k1[kb]).astype(BF)
                half = b * BLK + BLK // 2
                rest_ref[at, 32:48, :] = jnp.where(
                    low[: BLK // 2], v1[b * BLK : half], v2[half : (b + 1) * BLK]
                ).astype(BF)
                row = a * BLK + b * 8
                for c in range(DM // 128):
                    rest_ref[at, 48 + 8 * c : 56 + 8 * c, :] = cot_ref[row : row + 8, c * 128 : (c + 1) * 128]


def stem(halo, conv_weight, cotangent, features, patch_weight, query_weight, key_weight, value_weight):
    hbm = pl.BlockSpec(memory_space=pl.ANY)
    vmem = pl.BlockSpec(memory_space=pltpu.VMEM)
    return pl.pallas_call(
        stem_kernel,
        in_specs=[vmem] * 3 + [hbm] * 2 + [vmem] * 3,
        out_specs=(vmem, vmem, vmem),
        out_shape=(
            jax.ShapeDtypeStruct((128, DM), BF),
            jax.ShapeDtypeStruct((64, CHUNK, 128), BF),
            jax.ShapeDtypeStruct((64, CHUNK, 128), BF),
        ),
        scratch_shapes=[
            pltpu.VMEM((2, 34, 32, 256), BF),
            pltpu.VMEM((2, 2, ZW, 256), F32),
            pltpu.VMEM((2, 65 * ZW, 128), F32),
            pltpu.VMEM((2, 65 * ZW, 128), F32),
            pltpu.VMEM((2, 65 * ZW, 128), F32),
            pltpu.VMEM((128, 4096), BF),
            pltpu.VMEM((4096, DM), BF),
            pltpu.SemaphoreType.DMA((6,)),
        ],
        compiler_params=pltpu.CompilerParams(vmem_limit_bytes=26 << 20),
        name="stem",
    )(halo, conv_weight, cotangent, features, patch_weight, query_weight, key_weight, value_weight)


def local(
    features,
    neighbours,
    conv_weight,
    patch_weight,
    query_weight,
    key_weight,
    value_weight,
    output_weight,
    cotangent,
):
    _, inner = split_device(lax.axis_index("tile"))
    faces = gather_faces(in_hbm(neighbours), in_hbm(features))
    faces, inner = lax.optimization_barrier((faces, inner))
    faces = swap(faces, INNER).reshape(16, FACES, 256)
    tiles = faces[:, 64, :8].astype(jnp.int32)
    outer, goal = split_device(tiles >> 1)
    targets = jnp.where((tiles < 128) & (goal == inner), (outer & 7) * 2 + (tiles & 1), -1)
    halo = swap(route(targets, faces), OUTER)
    tokens, packed, rest = stem(
        halo,
        conv_weight.reshape(9, 256, 256),
        cotangent,
        features,
        in_hbm(patch_weight),
        query_weight,
        key_weight,
        value_weight,
    )
    packed = swap(packed)
    packed, rest = lax.optimization_barrier((packed, rest))
    rest = swap(rest)
    parts = swap(attend_single(rest, *attend_pair(packed)), KEY_GROUPS)
    att, grad = merge(parts, rest)
    terms = swap(grad.reshape(16, SHARE, 128), HEAD_GROUPS)
    received = swap(share_out(terms, att))
    return finish(received, tokens, output_weight)


def solution(mesh):
    in_specs = (
        P(("slide", "tile"), None, None, None),
        P(("slide", "tile"), None),
        P(),
        P(),
        P(),
        P(),
        P(),
        P(),
        P(("slide", "tile"), None),
    )
    out_specs = (P(("slide", "tile"), None), P("slide", None))
    return jax.shard_map(local, mesh=mesh, in_specs=in_specs, out_specs=out_specs, check_vma=False)
```
